32 devices in a mesh: grp: 2 (over y), bin: 4 (over z), slab: 4 (over x, core).
Axes of the slice: x: 2, y: 2, z: 4, core: 2. Of those that a mesh axis runs over, the one named last changes fastest.
Arguments:
- density: bfloat16 [512, 256, 256], P('grp', 'slab'), parts along dimension 0, may hold values from -6 to 6
- images: bfloat16 [512, 128, 128], P(('grp', 'bin', 'slab')), parts along dimension 0, may hold values from -6 to 6
- image_bin: int32 [512, 1], P(('grp', 'bin', 'slab')), parts along dimension 0, may hold values from 0 to 3; in each aligned block of 16 rows (0 to 15, 16 to 31, ...) at most 4 rows name the same one
- image_pose: int32 [512], P(('grp', 'bin', 'slab')), parts along dimension 0, may hold values from 0 to 7
- image_class: int32 [512], P(('grp', 'bin', 'slab')), parts along dimension 0, may hold values from 0 to 15
- defocus: float32 [32], P('grp'), parts along dimension 0, may hold values from 1 to 3
- pose_offset: float32 [8, 8], P('grp'), parts along dimension 0, may hold values from 0 to 1
- step_sizes: float32 [2], replicated, may hold values from 0.2 to 0.8
Outputs:
- gradient: float32 [512, 256, 256], P(('grp', 'bin'), 'slab'), parts along dimension 0
- refined: float32 [512, 256, 256], P(('grp', 'bin'), 'slab'), parts along dimension 0
The draws below stay inside these ranges and needn't reach their ends.
There are 2 independent parts, one for each index of `grp`. The reference program is written for one: setup_inputs(seed, part) draws one part's arguments, and reference() takes and returns one part's arrays. A program takes and returns all parts, laid end to end along the dimension named above; an argument that names none is the same for every part. Nothing has to cross between parts.
Inputs may be any that keep to these rules, and one draw needn't show every extreme that they name: `image_bin`: the images of one device name each bin at most 4 times, a bound that some block reaches.
All inputs are finite; a program needn't handle non-finite values.
Results may differ from the reference program's by a relative error of at most 0.0032.
Values may be sent and summed in bfloat16 or wider, within the bound.
No kernel may reach another device: no remote copies, remote signals or barrier semaphores. Data moves between devices by JAX's collectives and lax.ppermute only.
A program may use at most 256 MiB of HBM per device.

```python
import math
import jax
import jax.numpy as jnp
import numpy as np
from jax import lax

MAP = 256
IMG = 128
POSES = 8
CLASSES = 16
IMG_DEV = 16
BINS = 4
CAP = 4
IMAGES = 256


def touch_ends(array, rng, smallest, largest):
    shape = array.shape
    index_at = [jax.random.randint(jax.random.fold_in(rng, axis), (), 0, shape[axis]) for axis in range(len(shape))]
    array = array.at[tuple(index_at)].set(smallest)
    longest = shape.index(max(shape))
    index_at[longest] = (index_at[longest] + 1) % shape[longest]
    return array.at[tuple(index_at)].set(largest)


def steps_of(own_key, dims, split, low, largest):
    def one(axis_at, parts):
        draws = jax.random.uniform(jax.random.fold_in(jax.random.fold_in(own_key, 6), axis_at), (parts,), jnp.float32, low / len(split), largest / len(split))
        return jnp.repeat(jnp.exp(draws), dims[axis_at] // parts).reshape((-1,) + (1,) * (len(dims) - axis_at - 1))

    factor_of = one(*split[0])
    for cut in split[1:]:
        factor_of = factor_of * one(*cut)
    return factor_of


def assign_block(own_key, own, number, rows, count, top, most, slope):
    ranking = jax.random.permutation(own_key, count)
    crowded, usual = portions_of(count, rows * top, most, slope, True), portions_of(count, rows * top, most, slope, False)
    places = jnp.arange(count)

    def named(tallies, turn):
        used = int((tallies > 0).sum())
        fixed = max(1, used // 4)
        passed = fixed + (places - fixed + turn * (used - fixed)) % max(1, count - fixed)
        return jnp.zeros((count,), jnp.int32).at[ranking[jnp.where(places < fixed, places, passed)]].set(jnp.asarray(tallies, jnp.int32))

    tallies = jnp.where(number % 4 == 0, named(crowded, number // 4), named(usual, number - number // 4 - 1))
    mixed = jax.random.permutation(jax.random.fold_in(own, 3), count)
    source_of, sink = mixed[0:count // 2 * 2:2], mixed[1:count // 2 * 2:2]
    margin = jnp.minimum(tallies[source_of] - 1, most - tallies[sink]) // 2
    margin = jnp.where((source_of == ranking[0]) | (sink == ranking[0]) | (tallies[sink] == 0), 0, jnp.maximum(margin, 0))
    passed = jax.random.randint(jax.random.fold_in(own, 4), (count // 2,), 0, 1 << 20) % (margin + 1)
    tallies = tallies.at[source_of].add(-passed).at[sink].add(passed)
    members = jnp.searchsorted(jnp.cumsum(tallies), jnp.arange(rows * top), side="right").astype(jnp.int32)
    listing = members.reshape(top, rows).T
    listing = listing[jax.random.permutation(jax.random.fold_in(own, 1), rows)]
    turn = jax.random.randint(jax.random.fold_in(own, 2), (rows, 1), 0, top)
    return jnp.take_along_axis(listing, (jnp.arange(top)[None, :] + turn) % top, axis=1)


def portions_of(count, total, limit, skew, full):
    weights = [(1 << 20) // math.isqrt(standing ** skew) + 1 for standing in range(1, count + 1)]
    largest = limit if full else min(limit, max(-(-total // count), total * weights[0] // sum(weights)))
    least = 1 if total - largest >= count - 1 else 0
    holding, surplus = [largest] + [least] * (count - 1), total - largest - least * (count - 1)
    while surplus > 0:
        movable = [i for i in range(1, count) if holding[i] < largest] or [i for i in range(1, count) if holding[i] < limit]
        mass, left = sum([weights[i] for i in movable]), surplus
        for i in movable:
            more = min(limit - holding[i], max(1, left * weights[i] // mass), surplus)
            holding[i] = holding[i] + more
            surplus = surplus - more
    return np.array(holding)


def gaussian(key, dims, spread, bound, pieces=(), held_as=jnp.bfloat16):
    result = spread * jax.random.normal(key, dims, jnp.float32)
    if pieces:
        result = result * steps_of(key, dims, pieces, -0.22, 0.18)
    return jnp.clip(result, -bound, bound).astype(held_as)


def setup_inputs(seed: int = 0, part: int = 0) -> dict:
    key_of = jax.random.split(jax.random.key(seed), 9)
    part_splits = jax.random.split(jax.random.fold_in(key_of[8], part), 9)
    density = gaussian(part_splits[0], (MAP, MAP, MAP), 1.0, 6.0, ((1, 4),))
    images = gaussian(part_splits[1], (IMAGES, IMG, IMG), 1.0, 6.0, ((0, 16),))
    image_bin_keys = jax.random.split(jax.random.fold_in(part_splits[2], 1), IMAGES // IMG_DEV)
    image_bin_turns = jax.random.permutation(jax.random.fold_in(part_splits[2], 3), IMAGES // IMG_DEV)
    image_bin = jax.vmap(lambda own, number: assign_block(jax.random.fold_in(part_splits[2], 2), own, number, IMG_DEV, BINS, 1, CAP, 2))(image_bin_keys, image_bin_turns).reshape((IMAGES, 1))
    image_pose = touch_ends(jax.random.randint(part_splits[3], (IMAGES,), 0, POSES), jax.random.fold_in(part_splits[3], 1), 0, POSES - 1).astype(jnp.int32)
    image_class = touch_ends(jax.random.randint(part_splits[4], (IMAGES,), 0, CLASSES), jax.random.fold_in(part_splits[4], 1), 0, CLASSES - 1).astype(jnp.int32)
    defocus = jnp.clip(jnp.exp(jax.random.uniform(part_splits[5], (CLASSES,), jnp.float32, math.log(1.0), math.log(3.0))), 1.0, 3.0)
    pose_offset = jnp.clip(jax.random.uniform(part_splits[6], (BINS, POSES), jnp.float32, 0.0, 1.0), 0.0, 1.0)
    step_sizes = jnp.clip(jnp.exp(jax.random.uniform(key_of[7], (2,), jnp.float32, math.log(0.2), math.log(0.8))), 0.2, 0.8)
    return {"density": density, "images": images, "image_bin": image_bin, "image_pose": image_pose, "image_class": image_class, "defocus": defocus, "pose_offset": pose_offset, "step_sizes": step_sizes}


AMP_CONTRAST = 0.1
PHASE_RATE = 60.0
PRECISE = lax.Precision.HIGHEST

def pool_table(image_side, map_side):
    row_index = jnp.arange(image_side, dtype=jnp.float32)[:, None]
    col_index = jnp.arange(map_side, dtype=jnp.float32)[None, :]
    return 0.5 * jnp.maximum(0.0, 1.0 - jnp.abs(col_index - 2.0 * row_index - 0.5) / 2.0)

def slice_weights(angle_value, image_side, map_side, first_plane, slab_depth):
    middle = map_side / 2.0
    y_coord = jnp.arange(map_side, dtype=jnp.float32)[:, None] + 0.5 - middle
    z_coord = (first_plane + jnp.arange(slab_depth, dtype=jnp.int32)).astype(jnp.float32)[None, :] + 0.5 - middle
    spot_line = (y_coord * jnp.cos(angle_value) + z_coord * jnp.sin(angle_value)).reshape(1, map_side * slab_depth)
    centre = 2.0 * jnp.arange(image_side, dtype=jnp.float32)[:, None] + 1.0 - middle
    factor = 0.5 / math.sqrt(map_side)
    return (factor * jnp.maximum(0.0, 1.0 - jnp.abs(spot_line - centre) / 2.0)).astype(jnp.bfloat16)

def ctf_of(defocus_value, image_side):
    index_row = jnp.arange(image_side, dtype=jnp.int32)
    frequency = jnp.where(index_row < image_side // 2, index_row, index_row - image_side).astype(jnp.float32) / image_side
    radius = frequency[:, None] * frequency[:, None] + frequency[None, :] * frequency[None, :]
    phase_shift = PHASE_RATE * defocus_value[:, None, None] * radius[None, :, :]
    return -(math.sqrt(1.0 - AMP_CONTRAST * AMP_CONTRAST) * jnp.sin(phase_shift) + AMP_CONTRAST * jnp.cos(phase_shift))

def reference(density, images, image_bin, image_pose, image_class, defocus, pose_offset, step_sizes):
    pooling = pool_table(IMG, MAP)
    angles = (math.pi * (jnp.arange(BINS, dtype=jnp.float32)[:, None] + pose_offset) / BINS).reshape(BINS * POSES)
    pose_ids = (image_bin[:, 0] * POSES + image_pose).astype(jnp.int32)
    weight = 16.0 * BINS * POSES / IMAGES
    pose_total = BINS * POSES

    def one_pass(volume):
        folded = jnp.einsum('yzx,ix->yzi', volume.astype(jnp.float32), pooling, precision=PRECISE)
        folded = folded.astype(jnp.bfloat16).reshape(MAP * MAP, IMG).astype(jnp.float32)

        def project(angle_value):
            weights = slice_weights(angle_value, IMG, MAP, 0, MAP).astype(jnp.float32)
            return jnp.dot(weights, folded, precision=PRECISE).T
        projection = lax.map(project, angles)
        model = jnp.fft.fft2(projection, norm='ortho')
        model_real = jnp.real(model)
        model_imag = jnp.imag(model)

        def add_block(carry, block):
            pixels, labels, classes = block
            spectrum = jnp.fft.fft2(pixels.astype(jnp.float32), norm='ortho')
            ctf = ctf_of(defocus[classes], IMG)
            term_real = ctf * (ctf * model_real[labels] - jnp.real(spectrum))
            term_imag = ctf * (ctf * model_imag[labels] - jnp.imag(spectrum))
            total_real = carry[0] + jax.ops.segment_sum(term_real, labels, num_segments=pose_total)
            total_imag = carry[1] + jax.ops.segment_sum(term_imag, labels, num_segments=pose_total)
            return ((total_real, total_imag), None)
        zeros_sum = jnp.zeros((pose_total, IMG, IMG), jnp.float32)
        blocks = (images.reshape(IMAGES // IMG_DEV, IMG_DEV, IMG, IMG), pose_ids.reshape(IMAGES // IMG_DEV, IMG_DEV), image_class.reshape(IMAGES // IMG_DEV, IMG_DEV))
        (sum_real, sum_imag), _ = lax.scan(add_block, (zeros_sum, zeros_sum), blocks)
        spectrum_sum = weight * sum_real + 1j * (weight * sum_imag)
        field_sheets = jnp.real(jnp.fft.ifft2(spectrum_sum, norm='ortho')).astype(jnp.bfloat16)

        def accumulate(carry, pair):
            angle_value, sheet = pair
            weights = slice_weights(angle_value, IMG, MAP, 0, MAP).astype(jnp.float32)
            return (carry + jnp.dot(weights.T, sheet.astype(jnp.float32).T, precision=PRECISE), None)
        back, _ = lax.scan(accumulate, jnp.zeros((MAP * MAP, IMG), jnp.float32), (angles, field_sheets))
        return jnp.dot(back, pooling, precision=PRECISE).reshape(MAP, MAP, MAP)
    gradient_first = one_pass(density)
    first = density.astype(jnp.float32) - step_sizes[0] * gradient_first
    gradient = one_pass(first.astype(jnp.bfloat16))
    refined = first - step_sizes[1] * gradient
    return (gradient, refined)
```

```python
import functools
import math

import jax
import jax.numpy as jnp
import numpy as np
from jax import lax
from jax.experimental import pallas as pl
from jax.experimental.pallas import tpu as pltpu
from jax.sharding import PartitionSpec as P

AMP_CONTRAST = 0.1
PHASE_RATE = 60.0
BLOCK = 16
WINDOW = 24
SMEM = pltpu.SMEM


def vmem():
    return pl.BlockSpec(memory_space=pltpu.VMEM)


def smem():
    return pl.BlockSpec(memory_space=SMEM)


def pool_table(image_side, map_side):
    row_index = np.arange(image_side)[:, None]
    col_index = np.arange(map_side)[None, :]
    return 0.5 * np.maximum(0.0, 1.0 - np.abs(col_index - 2.0 * row_index - 0.5) / 2.0)


def hartley_table(image_side):
    index_row = np.arange(image_side)
    phase_index = index_row[:, None] * index_row[None, :] % image_side
    angle_table = 2.0 * math.pi / image_side * phase_index
    table = (np.cos(angle_table) + np.sin(angle_table)) / math.sqrt(image_side)
    high = table.astype(jnp.bfloat16)
    low = (table - high.astype(np.float64)).astype(jnp.bfloat16)
    return jnp.asarray(np.concatenate([high, low], axis=1))


def ctf_table(defocus, image_side):
    index_row = jnp.arange(image_side, dtype=jnp.int32)
    frequency = (
        jnp.where(index_row < image_side // 2, index_row, index_row - image_side).astype(
            jnp.float32
        )
        / image_side
    )
    part = PHASE_RATE * defocus[:, None] * (frequency * frequency)[None, :]
    shifted = part + math.asin(AMP_CONTRAST)
    return -(
        jnp.sin(shifted)[:, :, None] * jnp.cos(part)[:, None, :]
        + jnp.cos(shifted)[:, :, None] * jnp.sin(part)[:, None, :]
    )


def geometry(angles, first_row, row_blocks, first_plane, plane_blocks, image_side, map_side):
    middle = map_side / 2.0
    scale = 0.25 / math.sqrt(map_side)
    cosine, sine = jnp.cos(angles), jnp.sin(angles)
    y_low = (first_row + BLOCK * jnp.arange(row_blocks)).astype(jnp.float32) + 0.5 - middle
    z_low = (first_plane + BLOCK * jnp.arange(plane_blocks)).astype(jnp.float32) + 0.5 - middle
    y_part = y_low[:, None] * cosine[None, :]
    z_part = z_low[:, None] * sine[None, :]
    y_edge = y_part + jnp.minimum(0.0, (BLOCK - 1) * cosine)[None, :]
    z_edge = z_part + jnp.minimum(0.0, (BLOCK - 1) * sine)[None, :]
    least = y_edge[:, None, :] + z_edge[None, :, :]
    column = jnp.floor((least - 3.0 + middle) / 16.0).astype(jnp.int32) * 8
    start = jnp.clip(column, 0, image_side - WINDOW)
    offset = scale * (
        y_part[:, None, :] + z_part[None, :, :] - (2.0 * start.astype(jnp.float32) + 1.0 - middle)
    )
    direction = jnp.stack([cosine, sine]) * scale
    return direction.reshape(-1), start.reshape(-1), offset.reshape(-1)


def local_tables(map_side):
    lane = lax.broadcasted_iota(jnp.int32, (8, BLOCK * BLOCK), 1)
    row = lax.broadcasted_iota(jnp.int32, (8, BLOCK * BLOCK), 0).astype(jnp.float32)
    y_local = (lane // BLOCK).astype(jnp.float32)
    z_local = (lane % BLOCK).astype(jnp.float32)
    scale = 0.25 / math.sqrt(map_side)
    rows = [(2.0 * scale) * (row + 8.0 * k) for k in range(WINDOW // 8)]
    return y_local, z_local, rows


def make_window(tables, direction, offset, pose, base, poses, map_side):
    y_local, z_local, rows = tables
    peak = 0.5 / math.sqrt(map_side)
    line = y_local * direction[pose] + z_local * direction[poses + pose] + offset[base + pose]
    return [jnp.maximum(0.0, peak - jnp.abs(line - r)) for r in rows]


def fill_windows(w_ref, tables, direction, offset, block, poses, map_side):
    base = block * poses

    def pair(k, _):
        parts = []
        for half in range(2):
            parts += make_window(
                tables, direction, offset, 2 * k + half, base, poses, map_side
            )
        at = pl.multiple_of(k * 2 * WINDOW, 2 * WINDOW)
        w_ref[pl.ds(at, 2 * WINDOW), :] = jnp.concatenate(parts, axis=0).astype(jnp.bfloat16)
        return 0

    lax.fori_loop(0, poses // 2, pair, 0, unroll=min(8, poses // 2))


def add_projection(outs, prod_ref, start, block, poses):
    base = block * poses
    share = poses // len(outs)

    for part, out in enumerate(outs):

        def one(k, _, part=part, out=out):
            pose = part * share + k
            at = pl.multiple_of(start[base + pose], 8)
            rows = pl.multiple_of(pose * WINDOW, 8)
            out[k, pl.ds(at, WINDOW), :] += prod_ref[pl.ds(rows, WINDOW), :]
            return 0

        lax.fori_loop(0, share, one, 0, unroll=min(8, share))


def first_projection_kernel(
    map_side, poses, plane_blocks, row_blocks, direction, start, offset, dens, pool_t, keep, send,
    w_ref, prod_ref
):
    step = pl.program_id(0)

    @pl.when(step == 0)
    def _():
        keep[...] = jnp.zeros_like(keep)
        send[...] = jnp.zeros_like(send)

    tables = local_tables(map_side)

    def block(k, _):
        row, plane = k // plane_blocks, k % plane_blocks
        rows = pl.ds(pl.multiple_of(row * BLOCK, BLOCK), BLOCK)
        planes = pl.ds(pl.multiple_of(plane * BLOCK, BLOCK), BLOCK)
        values = dens[rows, planes, :].reshape(BLOCK * BLOCK, map_side)
        folded = jnp.dot(values, pool_t[...], preferred_element_type=jnp.float32)
        index = step * row_blocks * plane_blocks + k
        fill_windows(w_ref, tables, direction, offset, index, poses, map_side)
        prod_ref[...] = jnp.dot(
            w_ref[...], folded.astype(jnp.bfloat16), preferred_element_type=jnp.float32
        )
        add_projection((keep, send), prod_ref, start, index, poses)
        return 0

    lax.fori_loop(0, row_blocks * plane_blocks, block, 0)


def first_projection(density, pool_t, geo, poses):
    map_side, depth, _ = density.shape
    side = pool_t.shape[1]
    row_blocks = 2
    half = jax.ShapeDtypeStruct((poses // 2, side, side), jnp.float32)
    return pl.pallas_call(
        functools.partial(first_projection_kernel, map_side, poses, depth // BLOCK, row_blocks),
        grid=(map_side // (BLOCK * row_blocks),),
        in_specs=[smem(), smem(), smem(),
                  pl.BlockSpec((BLOCK * row_blocks, depth, map_side), lambda i: (i, 0, 0)),
                  vmem()],
        out_specs=[vmem(), vmem()],
        out_shape=[half, half],
        scratch_shapes=[
            pltpu.VMEM((poses * WINDOW, BLOCK * BLOCK), jnp.bfloat16),
            pltpu.VMEM((poses * WINDOW, side), jnp.float32),
        ],
        name="first_projection",
    )(*geo, density, pool_t)


def pick_kernel(count, order, images, *rest):
    outs, sems = rest[:-1], rest[-1]
    each = count // len(outs)
    copies = [
        pltpu.make_async_copy(images.at[order[k]], outs[k // each].at[k % each], sems.at[k])
        for k in range(count)
    ]
    for copy in copies:
        copy.start()
    for copy in copies:
        copy.wait()


def pick_images(images, order, groups):
    count = order.shape[0]
    _, side, _ = images.shape
    out = jax.ShapeDtypeStruct((count // groups, side, side), images.dtype)
    return pl.pallas_call(
        functools.partial(pick_kernel, count),
        in_specs=[smem(), pl.BlockSpec(memory_space=pl.ANY)],
        out_specs=[pl.BlockSpec(memory_space=pl.ANY)] * groups,
        out_shape=[out] * groups,
        scratch_shapes=[pltpu.SemaphoreType.DMA((count,))],
        name="pick_images",
    )(order, images)


def times_hartley(value, table):
    count, side = value.shape
    high = value.astype(jnp.bfloat16)
    low = (value - high.astype(jnp.float32)).astype(jnp.bfloat16)
    both = jnp.dot(high, table, preferred_element_type=jnp.float32)
    rest = jnp.dot(low, table[:, :side], preferred_element_type=jnp.float32)
    return both[:, :side] + (both[:, side:] + rest)


def spectrum_kernel(groups, each, classes, label, ctf, table, *refs):
    images, (keep, send) = refs[:groups], refs[groups:]
    half = keep.shape[0]
    side = keep.shape[1]
    keep[...] = jnp.zeros_like(keep)
    send[...] = jnp.zeros_like(send)
    hart = table[...]
    for group in range(groups):
        pixels = images[group][...].reshape(each * side, side)
        both = jnp.dot(pixels, hart, preferred_element_type=jnp.float32)
        along = (both[:, :side] + both[:, side:]).reshape(each, side, side)
        turned = jnp.concatenate([along[k].T for k in range(each)], axis=0)
        full = times_hartley(turned, hart).reshape(each, side, side)
        for k in range(each):
            mark = label[group * each + k]
            pose = mark // classes
            value = ctf[mark % classes] * full[k]

            @pl.when(jnp.logical_and(mark >= 0, pose < half))
            def _(pose=pose, value=value):
                keep[pose] += value

            @pl.when(pose >= half)
            def _(pose=pose, value=value):
                send[pose - half] += value

    for out in (keep, send):
        for pose in range(half):
            out[pose] = out[pose].T


def image_sums(images, label, ctf, table, poses):
    each, side, _ = images[0].shape
    half = jax.ShapeDtypeStruct((poses // 2, side, side), jnp.float32)
    return pl.pallas_call(
        functools.partial(spectrum_kernel, len(images), each, ctf.shape[0]),
        in_specs=[smem(), vmem(), vmem()] + [vmem()] * len(images),
        out_specs=[vmem(), vmem()],
        out_shape=[half, half],
        name="image_sums",
    )(label, ctf, table, *images)


def filter_kernel(weight, tally, ctf, table, power, *refs):
    proj, total, out = refs[:-2], refs[-2], refs[-1]
    owned, side, _ = out.shape
    classes = ctf.shape[0]
    hart = table[...]
    value = proj[0][...]
    for part in proj[1:]:
        value = value + part[...]
    along = times_hartley(value.reshape(owned * side, side), hart)
    turned = jnp.concatenate([along[k * side : (k + 1) * side].T for k in range(owned)], axis=0)
    full = times_hartley(turned, hart)
    parts = []
    for k in range(owned):
        gain = jnp.zeros((side, side), jnp.float32)
        for c in range(classes):
            gain = gain + tally[k * classes + c] * (ctf[c] * ctf[c])
        parts.append(weight * (gain * full[k * side : (k + 1) * side] - total[k]))
    along = times_hartley(jnp.concatenate(parts, axis=0), hart)
    turned = jnp.concatenate([along[k * side : (k + 1) * side].T for k in range(owned)], axis=0)
    field = times_hartley(turned, hart)
    out[...] = field.reshape(owned, side, side).astype(out.dtype)


def residual_field(parts, total, tally, ctf, table, weight):
    owned, side, _ = total.shape

    def kernel(tally, ctf, table, *refs):
        filter_kernel(weight, tally, ctf, table, None, *refs)

    return pl.pallas_call(
        kernel,
        in_specs=[smem(), vmem(), vmem()] + [vmem()] * (len(parts) + 1),
        out_specs=vmem(),
        out_shape=jax.ShapeDtypeStruct((owned, side, side), jnp.bfloat16),
        name="residual_field",
    )(tally, ctf, table, *parts, total)


def load_fields(field, fields):
    at = 0
    for part in fields:
        count = part.shape[0]
        field[at : at + count] = part[...].astype(jnp.float32)
        at += count


def gather_windows(f_ref, field, start, block, poses):
    base = block * poses

    def pair(k, _):
        parts = []
        for half in range(2):
            at = pl.multiple_of(start[base + 2 * k + half], 8)
            parts.append(field[2 * k + half, pl.ds(at, WINDOW), :])
        rows = pl.multiple_of(k * 2 * WINDOW, 2 * WINDOW)
        f_ref[pl.ds(rows, 2 * WINDOW), :] = jnp.concatenate(parts, axis=0).astype(jnp.bfloat16)
        return 0

    lax.fori_loop(0, poses // 2, pair, 0, unroll=min(8, poses // 2))


def block_gradient(w_ref, f_ref, pool2):
    back = lax.dot_general(
        w_ref[...], f_ref[...], (((0,), (0,)), ((), ())), preferred_element_type=jnp.float32
    )
    high = back.astype(jnp.bfloat16)
    low = (back - high.astype(jnp.float32)).astype(jnp.bfloat16)
    return jnp.dot(
        jnp.concatenate([high, low], axis=1), pool2[...], preferred_element_type=jnp.float32
    )


def step_kernel(
    map_side, poses, plane_blocks, parts, bin_ref, direction, start, offset, sizes, dens, pool2,
    pool_t, *refs
):
    fields = refs[:parts]
    first, keep, send, field, w_ref, f_ref, prod_ref = refs[parts:]
    step = pl.program_id(0)

    @pl.when(step == 0)
    def _():
        keep[...] = jnp.zeros_like(keep)
        send[...] = jnp.zeros_like(send)
        load_fields(field, fields)

    tables = local_tables(map_side)

    def block(k, _):
        planes = pl.ds(pl.multiple_of(k * BLOCK, BLOCK), BLOCK)
        index = step * plane_blocks + k
        fill_windows(w_ref, tables, direction, offset, index, poses, map_side)
        gather_windows(f_ref, field, start, index, poses)
        grad = block_gradient(w_ref, f_ref, pool2)
        values = dens[:, planes, :].reshape(BLOCK * BLOCK, map_side).astype(jnp.float32)
        moved = values - sizes[0] * grad
        first[:, planes, :] = moved.reshape(BLOCK, BLOCK, map_side)
        folded = jnp.dot(
            moved.astype(jnp.bfloat16), pool_t[...], preferred_element_type=jnp.float32
        )
        prod_ref[...] = jnp.dot(
            w_ref[...], folded.astype(jnp.bfloat16), preferred_element_type=jnp.float32
        )
        add_projection((keep, send), prod_ref, start, index, poses)
        return 0

    lax.fori_loop(0, plane_blocks, block, 0)


def take_step(density, fields, geo, sizes, bin_index, pool2, pool_t, poses, row_share):
    map_side, depth, _ = density.shape
    side = pool_t.shape[1]
    half = jax.ShapeDtypeStruct((poses // 2, side, side), jnp.float32)
    row_blocks = row_share // BLOCK
    rows = (BLOCK, depth, map_side)
    scalars = (geo[0], geo[1], geo[2], sizes)
    return pl.pallas_call(
        functools.partial(step_kernel, map_side, poses, depth // BLOCK, len(fields)),
        grid_spec=pltpu.PrefetchScalarGridSpec(
            num_scalar_prefetch=1,
            grid=(row_blocks,),
            in_specs=[smem()] * len(scalars)
            + [pl.BlockSpec(rows, lambda i, at: (at[0] * row_blocks + i, 0, 0))]
            + [vmem()] * (2 + len(fields)),
            out_specs=[pl.BlockSpec(rows, lambda i, at: (i, 0, 0)), vmem(), vmem()],
            scratch_shapes=[
                pltpu.VMEM((poses, side, side), jnp.float32),
                pltpu.VMEM((poses * WINDOW, BLOCK * BLOCK), jnp.bfloat16),
                pltpu.VMEM((poses * WINDOW, side), jnp.bfloat16),
                pltpu.VMEM((poses * WINDOW, side), jnp.float32),
            ],
        ),
        out_shape=[jax.ShapeDtypeStruct((row_share, depth, map_side), jnp.float32), half, half],
        name="take_step",
    )(bin_index.reshape(1), *scalars, density, pool2, pool_t, *fields)


def finish_kernel(
    map_side, poses, plane_blocks, parts, direction, start, offset, sizes, first, pool2, *refs
):
    fields = refs[:parts]
    gradient, refined, field, w_ref, f_ref = refs[parts:]
    step = pl.program_id(0)

    @pl.when(step == 0)
    def _():
        load_fields(field, fields)

    tables = local_tables(map_side)

    def block(k, _):
        planes = pl.ds(pl.multiple_of(k * BLOCK, BLOCK), BLOCK)
        index = step * plane_blocks + k
        fill_windows(w_ref, tables, direction, offset, index, poses, map_side)
        gather_windows(f_ref, field, start, index, poses)
        grad = block_gradient(w_ref, f_ref, pool2).reshape(BLOCK, BLOCK, map_side)
        gradient[:, planes, :] = grad
        refined[:, planes, :] = first[:, planes, :] - sizes[1] * grad
        return 0

    lax.fori_loop(0, plane_blocks, block, 0)


def finish(first, fields, geo, sizes, pool2, poses):
    row_share, depth, map_side = first.shape
    side = pool2.shape[0] // 2
    rows = pl.BlockSpec((BLOCK, depth, map_side), lambda i: (i, 0, 0))
    out = jax.ShapeDtypeStruct(first.shape, jnp.float32)
    return pl.pallas_call(
        functools.partial(finish_kernel, map_side, poses, depth // BLOCK, len(fields)),
        grid=(row_share // BLOCK,),
        in_specs=[smem()] * 4 + [rows] + [vmem()] * (1 + len(fields)),
        out_specs=[rows, rows],
        out_shape=[out, out],
        scratch_shapes=[
            pltpu.VMEM((poses, side, side), jnp.float32),
            pltpu.VMEM((poses * WINDOW, BLOCK * BLOCK), jnp.bfloat16),
            pltpu.VMEM((poses * WINDOW, side), jnp.bfloat16),
        ],
        name="finish",
    )(*geo, sizes, first, pool2, *fields)


def on_device(
    density, images, image_bin, image_pose, image_class, defocus, pose_offset, step_sizes
):
    bins = lax.axis_size("bin")
    slabs = lax.axis_size("slab")
    chips = slabs // 2
    bin_index = lax.axis_index("bin")
    slab_index = lax.axis_index("slab")
    chip, core = slab_index // 2, slab_index % 2
    map_side, depth, _ = density.shape
    image_count, side, _ = images.shape
    pose_count = pose_offset.shape[1]
    classes = defocus.shape[0]
    capacity = image_count // 4
    row_share = map_side // bins
    owned = pose_count // slabs
    weight = 16.0 * pose_count / (image_count * slabs)

    def to_core(value):
        return lax.ppermute(value, "slab", [(s, s ^ 1) for s in range(slabs)])

    def to_chip(value, shift):
        return lax.ppermute(
            value, "slab", [(s, (s + 2 * shift) % slabs) for s in range(slabs)]
        )

    def to_bin(value, shift):
        return lax.ppermute(value, "bin", [(b, (b + shift) % bins) for b in range(bins)])

    cores_on, chips_on, place = jnp.meshgrid(
        jnp.arange(2), jnp.arange(chips), jnp.arange(owned), indexing="ij"
    )
    owner = (chip + chips_on) % chips * 2 + (core + cores_on) % 2
    own_order = (owner * owned + place).reshape(-1)
    own_offset = jnp.take(
        lax.dynamic_index_in_dim(pose_offset, bin_index, 0, keepdims=False), own_order
    )
    own_angles = math.pi * (bin_index.astype(jnp.float32) + own_offset) / bins
    bin_order = (bin_index + jnp.arange(bins)) % bins
    rel = jnp.take(jnp.take(pose_offset, bin_order, axis=0), own_order, axis=1)
    rel = math.pi * (bin_order.astype(jnp.float32)[:, None] + rel) / bins
    rel = rel.reshape(bins, 2, chips, owned).transpose(1, 2, 0, 3).reshape(-1)
    poses = bins * pose_count
    first_plane = slab_index * depth
    own_geo = geometry(
        own_angles, 0, map_side // BLOCK, first_plane, depth // BLOCK, side, map_side
    )
    geo = geometry(
        rel, bin_index * row_share, row_share // BLOCK, first_plane, depth // BLOCK, side, map_side
    )
    pooling = pool_table(side, map_side).astype(jnp.bfloat16)
    pool_t = jnp.asarray(pooling.T)
    pool2 = jnp.asarray(np.concatenate([pooling, pooling], axis=0))
    table = hartley_table(side)
    ctf = ctf_table(defocus, side)

    target = image_bin[:, 0]
    chosen = (target[:, None] == jnp.arange(bins, dtype=jnp.int32)[None, :]).astype(jnp.int32)
    rank = jnp.sum((jnp.cumsum(chosen, axis=0) - chosen) * chosen, axis=1)
    slot = (target - bin_index) % bins * capacity + rank
    placement = jnp.arange(bins * capacity, dtype=jnp.int32)[:, None] == slot[None, :]
    order = jnp.sum(
        jnp.where(placement, jnp.arange(image_count, dtype=jnp.int32)[None, :], 0), axis=1
    )
    mark = image_pose * classes + image_class + 1
    marks = jnp.sum(jnp.where(placement, mark[None, :], 0), axis=1) - 1
    picked = pick_images(images, order, bins)
    marks = marks.reshape(bins, capacity)
    got_images = [picked[0]] + [to_bin(picked[d], d) for d in range(1, bins)]
    got_marks = [marks[0]] + [to_bin(marks[d], d) for d in range(1, bins)]
    got_marks = jnp.concatenate(got_marks)
    got_pose, got_class = got_marks // classes, got_marks % classes
    at = jnp.argmax(
        (got_pose[:, None] == own_order[None, :]).astype(jnp.int32), axis=1
    ).astype(jnp.int32)
    label = jnp.where(got_marks >= 0, at * classes + got_class, -1)
    tally = jnp.sum(
        (
            label[:, None]
            == jnp.arange(pose_count * classes, dtype=jnp.int32)[None, :]
        ).astype(jnp.float32),
        axis=0,
    ).reshape(2, chips, owned * classes)

    def reduce_slab(keep, send):
        got = to_core(send)
        sums = [keep[d] + got[d] for d in range(chips)]
        moved = [to_chip(sums[d], d) for d in range(1, chips)]
        return [sums[0]] + moved

    tally = functools.reduce(jnp.add, reduce_slab(tally[0], tally[1]))

    def split(value):
        return value.reshape(chips, -1, *value.shape[1:])

    keep, send = first_projection(density, pool_t, own_geo, pose_count)
    proj_parts = reduce_slab(split(keep), split(send))
    keep, send = image_sums(got_images, label, ctf, table, pose_count)
    total = functools.reduce(jnp.add, reduce_slab(split(keep), split(send)))

    def share_field(field):
        near = [field] + [to_bin(field, bins - d) for d in range(1, bins)]
        near = jnp.concatenate(near, axis=0)
        row = [near] + [to_chip(near, chips - d) for d in range(1, chips)]
        return row + [to_core(part) for part in row]

    field = residual_field(proj_parts, total, tally, ctf, table, weight)
    first, keep, send = take_step(
        density, share_field(field), geo, step_sizes, bin_index, pool2, pool_t, poses, row_share
    )
    parts = functools.reduce(jnp.add, reduce_slab(split(keep), split(send)))
    parts = parts.reshape(bins, owned, side, side)
    parts = [parts[0]] + [to_bin(parts[d], d) for d in range(1, bins)]
    field = residual_field(parts, total, tally, ctf, table, weight)
    gradient, refined = finish(first, share_field(field), geo, step_sizes, pool2, poses)
    return (gradient, refined)


def solution(mesh):
    return jax.shard_map(
        on_device,
        mesh=mesh,
        in_specs=(
            P("grp", "slab", None),
            P(("grp", "bin", "slab"), None, None),
            P(("grp", "bin", "slab"), None),
            P(("grp", "bin", "slab")),
            P(("grp", "bin", "slab")),
            P("grp"),
            P("grp", None),
            P(),
        ),
        out_specs=(P(("grp", "bin"), "slab", None), P(("grp", "bin"), "slab", None)),
        check_vma=False,
    )
```

```python
import functools
import math

import jax
import jax.numpy as jnp
import numpy as np
from jax import lax
from jax.experimental import pallas as pl
from jax.experimental.pallas import tpu as pltpu
from jax.sharding import PartitionSpec as P

AMP_CONTRAST = 0.1
PHASE_RATE = 60.0
BLOCK = 16
WINDOW = 16
LANES = 128
SMEM = pltpu.SMEM


def vmem():
    return pl.BlockSpec(memory_space=pltpu.VMEM)


def smem():
    return pl.BlockSpec(memory_space=SMEM)


def pool_table(image_side, map_side):
    row_index = np.arange(image_side)[:, None]
    col_index = np.arange(map_side)[None, :]
    return 0.5 * np.maximum(0.0, 1.0 - np.abs(col_index - 2.0 * row_index - 0.5) / 2.0)


def hartley_table(image_side):
    index_row = np.arange(image_side)
    phase_index = index_row[:, None] * index_row[None, :] % image_side
    angle_table = 2.0 * math.pi / image_side * phase_index
    table = (np.cos(angle_table) + np.sin(angle_table)) / math.sqrt(image_side)
    high = table.astype(jnp.bfloat16)
    low = (table - high.astype(np.float64)).astype(jnp.bfloat16)
    return jnp.asarray(np.concatenate([high, low], axis=1))


def ctf_table(defocus, image_side):
    index_row = jnp.arange(image_side, dtype=jnp.int32)
    frequency = (
        jnp.where(index_row < image_side // 2, index_row, index_row - image_side).astype(
            jnp.float32
        )
        / image_side
    )
    part = PHASE_RATE * defocus[:, None] * (frequency * frequency)[None, :]
    shifted = part + math.asin(AMP_CONTRAST)
    return -(
        jnp.sin(shifted)[:, :, None] * jnp.cos(part)[:, None, :]
        + jnp.cos(shifted)[:, :, None] * jnp.sin(part)[:, None, :]
    )


def geometry(angles, first_row, row_blocks, first_plane, plane_blocks, image_side, map_side):
    middle = map_side / 2.0
    scale = 0.25 / math.sqrt(map_side)
    cosine, sine = jnp.cos(angles), jnp.sin(angles)
    y_low = (first_row + BLOCK * jnp.arange(row_blocks)).astype(jnp.float32) + 0.5 - middle
    z_low = (first_plane + BLOCK * jnp.arange(plane_blocks)).astype(jnp.float32) + 0.5 - middle
    y_part = y_low[:, None] * cosine[None, :]
    z_part = z_low[:, None] * sine[None, :]
    y_edge = y_part + jnp.minimum(0.0, (BLOCK - 1) * cosine)[None, :]
    z_edge = z_part + jnp.minimum(0.0, (BLOCK - 1) * sine)[None, :]
    least = y_edge[:, None, :] + z_edge[None, :, :]
    column = jnp.floor((least - 3.0 + middle) / 2.0).astype(jnp.int32)
    start = jnp.clip(column, 0, image_side - WINDOW)
    offset = scale * (
        y_part[:, None, :] + z_part[None, :, :] - (2.0 * start.astype(jnp.float32) + 1.0 - middle)
    )
    direction = jnp.stack([cosine, sine]) * scale
    blocks = row_blocks * plane_blocks
    lanes = offset.reshape(blocks, 1, -1, 1) - 2.0 * scale * jnp.arange(
        WINDOW, dtype=jnp.float32
    )
    wide = jnp.repeat(direction, WINDOW, axis=1)
    return (
        (direction.reshape(-1), start.reshape(-1), offset.reshape(-1)),
        (wide, lanes.reshape(blocks, 1, -1)),
    )


def fill_windows(w_ref, direction, offset, block, poses, map_side):
    lane = lax.broadcasted_iota(jnp.int32, (8, BLOCK * BLOCK), 1)
    row = lax.broadcasted_iota(jnp.int32, (8, BLOCK * BLOCK), 0).astype(jnp.float32)
    y_local = (lane // BLOCK).astype(jnp.float32)
    z_local = (lane % BLOCK).astype(jnp.float32)
    peak = 0.5 / math.sqrt(map_side)
    rows = [peak * (row + 8.0 * k) for k in range(WINDOW // 8)]
    base = block * poses
    for pose in range(poses):
        line = (
            y_local * direction[pose] + z_local * direction[poses + pose] + offset[base + pose]
        )
        parts = [jnp.maximum(0.0, peak - jnp.abs(line - r)) for r in rows]
        w_ref[pose * WINDOW : (pose + 1) * WINDOW, :] = jnp.concatenate(parts, axis=0).astype(
            jnp.bfloat16
        )


def fill_turned(t_ref, wide, lanes, block, map_side):
    peak = 0.5 / math.sqrt(map_side)
    local = lax.broadcasted_iota(jnp.int32, (BLOCK, LANES), 0).astype(jnp.float32)
    offset = lanes[block]
    for at in range(0, wide.shape[1], LANES):
        span = slice(at, at + LANES)
        along_z = local * wide[1:2, span] + offset[:, span]
        along_y = wide[0:1, span]
        for y in range(BLOCK):
            line = along_z + float(y) * along_y
            t_ref[y * BLOCK : (y + 1) * BLOCK, span] = jnp.maximum(
                0.0, peak - jnp.abs(line)
            ).astype(jnp.bfloat16)


def add_projection(outs, prod, start, block, poses):
    base = block * poses
    share = poses // len(outs)
    for pose in range(poses):
        rows = pl.ds(start[base + pose], WINDOW)
        outs[pose // share][pose % share, rows, :] += prod[pose * WINDOW : (pose + 1) * WINDOW]


def first_projection_kernel(
    map_side, poses, direction, start, offset, dens, pool_t, keep, send, fold_ref, w_ref
):
    step = pl.program_id(0)

    @pl.when(step == 0)
    def _():
        keep[...] = jnp.zeros_like(keep)
        send[...] = jnp.zeros_like(send)

    height, depth, _ = dens.shape
    side = pool_t.shape[1]
    folded = jnp.dot(
        dens[...].reshape(height * depth, map_side), pool_t[...], preferred_element_type=jnp.float32
    )
    fold_ref[...] = folded.astype(jnp.bfloat16).reshape(height, depth, side)
    count = height * depth // (BLOCK * BLOCK)
    for k in range(count):
        row, plane = k // (depth // BLOCK) * BLOCK, k % (depth // BLOCK) * BLOCK
        weights = w_ref.at[k % 2]
        fill_windows(weights, direction, offset, step * count + k, poses, map_side)
        pixels = fold_ref[row : row + BLOCK, plane : plane + BLOCK, :].reshape(-1, side)
        prod = jnp.dot(weights[...], pixels, preferred_element_type=jnp.float32)
        add_projection((keep, send), prod, start, step * count + k, poses)


def first_projection(density, pool_t, geo, poses):
    map_side, depth, _ = density.shape
    side = pool_t.shape[1]
    height = 2 * BLOCK
    half = jax.ShapeDtypeStruct((poses // 2, side, side), jnp.float32)
    return pl.pallas_call(
        functools.partial(first_projection_kernel, map_side, poses),
        grid=(map_side // height,),
        in_specs=[smem(), smem(), smem(),
                  pl.BlockSpec((height, depth, map_side), lambda i: (i, 0, 0)),
                  vmem()],
        out_specs=[vmem(), vmem()],
        out_shape=[half, half],
        scratch_shapes=[
            pltpu.VMEM((height, depth, side), jnp.bfloat16),
            pltpu.VMEM((2, poses * WINDOW, BLOCK * BLOCK), jnp.bfloat16),
        ],
        name="first_projection",
    )(*geo, density, pool_t)


def pick_kernel(order, images, *outs):
    each = outs[0].shape[0]
    for group, out in enumerate(outs):
        for k in range(each):
            out[k] = images[order[group * each + k]]


def pick_images(images, order, groups):
    count = order.shape[0]
    _, side, _ = images.shape
    out = jax.ShapeDtypeStruct((count // groups, side, side), images.dtype)
    return pl.pallas_call(
        pick_kernel,
        in_specs=[smem(), vmem()],
        out_specs=[vmem()] * groups,
        out_shape=[out] * groups,
        name="pick_images",
    )(order, images)


def times_hartley(value, table):
    count, side = value.shape
    high = value.astype(jnp.bfloat16)
    low = (value - high.astype(jnp.float32)).astype(jnp.bfloat16)
    both = jnp.dot(high, table, preferred_element_type=jnp.float32)
    rest = jnp.dot(low, table[:, :side], preferred_element_type=jnp.float32)
    return both[:, :side] + (both[:, side:] + rest)


def spectrum_kernel(groups, each, classes, label, ctf, table, *refs):
    images, (keep, send) = refs[:groups], refs[groups:]
    half = keep.shape[0]
    side = keep.shape[1]
    keep[...] = jnp.zeros_like(keep)
    send[...] = jnp.zeros_like(send)
    hart = table[...]
    for group in range(groups):
        pixels = images[group][...].reshape(each * side, side)
        both = jnp.dot(pixels, hart, preferred_element_type=jnp.float32)
        along = (both[:, :side] + both[:, side:]).reshape(each, side, side)
        turned = jnp.concatenate([along[k].T for k in range(each)], axis=0)
        full = times_hartley(turned, hart).reshape(each, side, side)
        for k in range(each):
            mark = label[group * each + k]
            pose = mark // classes
            value = ctf[mark % classes] * full[k]

            @pl.when(jnp.logical_and(mark >= 0, pose < half))
            def _(pose=pose, value=value):
                keep[pose] += value

            @pl.when(pose >= half)
            def _(pose=pose, value=value):
                send[pose - half] += value

    for out in (keep, send):
        for pose in range(half):
            out[pose] = out[pose].T


def image_sums(images, label, ctf, table, poses):
    each, side, _ = images[0].shape
    half = jax.ShapeDtypeStruct((poses // 2, side, side), jnp.float32)
    return pl.pallas_call(
        functools.partial(spectrum_kernel, len(images), each, ctf.shape[0]),
        in_specs=[smem(), vmem(), vmem()] + [vmem()] * len(images),
        out_specs=[vmem(), vmem()],
        out_shape=[half, half],
        name="image_sums",
    )(label, ctf, table, *images)


def filter_kernel(weight, tally, ctf, table, power, *refs):
    proj, total, out = refs[:-2], refs[-2], refs[-1]
    owned, side, _ = out.shape
    classes = ctf.shape[0]
    hart = table[...]
    value = proj[0][...]
    for part in proj[1:]:
        value = value + part[...]
    along = times_hartley(value.reshape(owned * side, side), hart)
    turned = jnp.concatenate([along[k * side : (k + 1) * side].T for k in range(owned)], axis=0)
    full = times_hartley(turned, hart)
    parts = []
    for k in range(owned):
        gain = jnp.zeros((side, side), jnp.float32)
        for c in range(classes):
            gain = gain + tally[k * classes + c] * (ctf[c] * ctf[c])
        parts.append(weight * (gain * full[k * side : (k + 1) * side] - total[k]))
    along = times_hartley(jnp.concatenate(parts, axis=0), hart)
    turned = jnp.concatenate([along[k * side : (k + 1) * side].T for k in range(owned)], axis=0)
    field = times_hartley(turned, hart)
    out[...] = field.reshape(owned, side, side).astype(out.dtype)


def residual_field(parts, total, tally, ctf, table, weight):
    owned, side, _ = total.shape

    def kernel(tally, ctf, table, *refs):
        filter_kernel(weight, tally, ctf, table, None, *refs)

    return pl.pallas_call(
        kernel,
        in_specs=[smem(), vmem(), vmem()] + [vmem()] * (len(parts) + 1),
        out_specs=vmem(),
        out_shape=jax.ShapeDtypeStruct((owned, side, side), jnp.bfloat16),
        name="residual_field",
    )(tally, ctf, table, *parts, total)


def load_fields(field, fields):
    at = 0
    for part in fields:
        count = part.shape[0]
        field[at : at + count] = part[...].astype(jnp.float32)
        at += count


def gather_windows(f_ref, field, start, block, poses):
    base = block * poses
    for pose in range(poses):
        f_ref[pose * WINDOW : (pose + 1) * WINDOW, :] = field[
            pose, pl.ds(start[base + pose], WINDOW), :
        ].astype(jnp.bfloat16)


def block_gradient(t_ref, f_ref, pool2):
    back = jnp.dot(t_ref[...], f_ref[...], preferred_element_type=jnp.float32)
    high = back.astype(jnp.bfloat16)
    low = (back - high.astype(jnp.float32)).astype(jnp.bfloat16)
    return jnp.dot(
        jnp.concatenate([high, low], axis=1), pool2[...], preferred_element_type=jnp.float32
    )


def step_kernel(
    map_side, poses, parts, bin_ref, direction, start, offset, sizes, dens, wide, lanes, pool2,
    pool_t, *refs
):
    fields = refs[:parts]
    first, keep, send, field, t_ref, w_ref, f_ref = refs[parts:]
    step = pl.program_id(0)

    @pl.when(step == 0)
    def _():
        keep[...] = jnp.zeros_like(keep)
        send[...] = jnp.zeros_like(send)
        load_fields(field, fields)

    count = dens.shape[1] // BLOCK
    for k in range(count):
        planes = slice(k * BLOCK, (k + 1) * BLOCK)
        index = step * count + k
        turned, weights, windows = t_ref.at[k % 2], w_ref.at[k % 2], f_ref.at[k % 2]
        fill_turned(turned, wide, lanes, index, map_side)
        gather_windows(windows, field, start, index, poses)
        grad = block_gradient(turned, windows, pool2)
        values = dens[:, planes, :].reshape(BLOCK * BLOCK, map_side).astype(jnp.float32)
        moved = values - sizes[0] * grad
        first[:, planes, :] = moved.reshape(BLOCK, BLOCK, map_side)
        folded = jnp.dot(
            moved.astype(jnp.bfloat16), pool_t[...], preferred_element_type=jnp.float32
        )
        fill_windows(weights, direction, offset, index, poses, map_side)
        prod = jnp.dot(
            weights[...], folded.astype(jnp.bfloat16), preferred_element_type=jnp.float32
        )
        add_projection((keep, send), prod, start, index, poses)


def take_step(density, fields, geo, wide_geo, sizes, bin_index, pool2, pool_t, poses, row_share):
    map_side, depth, _ = density.shape
    side = pool_t.shape[1]
    half = jax.ShapeDtypeStruct((poses // 2, side, side), jnp.float32)
    row_blocks = row_share // BLOCK
    rows = (BLOCK, depth, map_side)
    return pl.pallas_call(
        functools.partial(step_kernel, map_side, poses, len(fields)),
        grid_spec=pltpu.PrefetchScalarGridSpec(
            num_scalar_prefetch=1,
            grid=(row_blocks,),
            in_specs=[smem()] * 4
            + [pl.BlockSpec(rows, lambda i, at: (at[0] * row_blocks + i, 0, 0))]
            + [vmem()] * (4 + len(fields)),
            out_specs=[pl.BlockSpec(rows, lambda i, at: (i, 0, 0)), vmem(), vmem()],
            scratch_shapes=[
                pltpu.VMEM((poses, side, side), jnp.float32),
                pltpu.VMEM((2, BLOCK * BLOCK, poses * WINDOW), jnp.bfloat16),
                pltpu.VMEM((2, poses * WINDOW, BLOCK * BLOCK), jnp.bfloat16),
                pltpu.VMEM((2, poses * WINDOW, side), jnp.bfloat16),
            ],
        ),
        out_shape=[jax.ShapeDtypeStruct((row_share, depth, map_side), jnp.float32), half, half],
        name="take_step",
    )(bin_index.reshape(1), *geo, sizes, density, *wide_geo, pool2, pool_t, *fields)


def finish_kernel(map_side, poses, parts, start, sizes, first, wide, lanes, pool2, *refs):
    fields = refs[:parts]
    gradient, refined, field, t_ref, f_ref = refs[parts:]
    step = pl.program_id(0)

    @pl.when(step == 0)
    def _():
        load_fields(field, fields)

    count = first.shape[1] // BLOCK
    for k in range(count):
        planes = slice(k * BLOCK, (k + 1) * BLOCK)
        index = step * count + k
        turned, windows = t_ref.at[k % 2], f_ref.at[k % 2]
        fill_turned(turned, wide, lanes, index, map_side)
        gather_windows(windows, field, start, index, poses)
        grad = block_gradient(turned, windows, pool2).reshape(BLOCK, BLOCK, map_side)
        gradient[:, planes, :] = grad
        refined[:, planes, :] = first[:, planes, :] - sizes[1] * grad


def finish(first, fields, geo, wide_geo, sizes, pool2, poses):
    row_share, depth, map_side = first.shape
    side = pool2.shape[0] // 2
    rows = pl.BlockSpec((BLOCK, depth, map_side), lambda i: (i, 0, 0))
    out = jax.ShapeDtypeStruct(first.shape, jnp.float32)
    return pl.pallas_call(
        functools.partial(finish_kernel, map_side, poses, len(fields)),
        grid=(row_share // BLOCK,),
        in_specs=[smem()] * 2 + [rows] + [vmem()] * (3 + len(fields)),
        out_specs=[rows, rows],
        out_shape=[out, out],
        scratch_shapes=[
            pltpu.VMEM((poses, side, side), jnp.float32),
            pltpu.VMEM((2, BLOCK * BLOCK, poses * WINDOW), jnp.bfloat16),
            pltpu.VMEM((2, poses * WINDOW, side), jnp.bfloat16),
        ],
        name="finish",
    )(geo[1], sizes, first, *wide_geo, pool2, *fields)


def on_device(
    density, images, image_bin, image_pose, image_class, defocus, pose_offset, step_sizes
):
    bins = lax.axis_size("bin")
    slabs = lax.axis_size("slab")
    chips = slabs // 2
    bin_index = lax.axis_index("bin")
    slab_index = lax.axis_index("slab")
    chip, core = slab_index // 2, slab_index % 2
    map_side, depth, _ = density.shape
    image_count, side, _ = images.shape
    pose_count = pose_offset.shape[1]
    classes = defocus.shape[0]
    capacity = image_count // 4
    row_share = map_side // bins
    owned = pose_count // slabs
    weight = 16.0 * pose_count / (image_count * slabs)

    def to_core(value):
        return lax.ppermute(value, "slab", [(s, s ^ 1) for s in range(slabs)])

    def to_chip(value, shift):
        return lax.ppermute(
            value, "slab", [(s, (s + 2 * shift) % slabs) for s in range(slabs)]
        )

    def to_bin(value, shift):
        return lax.ppermute(value, "bin", [(b, (b + shift) % bins) for b in range(bins)])

    cores_on, chips_on, place = jnp.meshgrid(
        jnp.arange(2), jnp.arange(chips), jnp.arange(owned), indexing="ij"
    )
    owner = (chip + chips_on) % chips * 2 + (core + cores_on) % 2
    own_order = (owner * owned + place).reshape(-1)
    own_offset = jnp.take(
        lax.dynamic_index_in_dim(pose_offset, bin_index, 0, keepdims=False), own_order
    )
    own_angles = math.pi * (bin_index.astype(jnp.float32) + own_offset) / bins
    bin_order = (bin_index + jnp.arange(bins)) % bins
    rel = jnp.take(jnp.take(pose_offset, bin_order, axis=0), own_order, axis=1)
    rel = math.pi * (bin_order.astype(jnp.float32)[:, None] + rel) / bins
    rel = rel.reshape(bins, 2, chips, owned).transpose(1, 2, 0, 3).reshape(-1)
    poses = bins * pose_count
    first_plane = slab_index * depth
    own_geo, _ = geometry(
        own_angles, 0, map_side // BLOCK, first_plane, depth // BLOCK, side, map_side
    )
    geo, wide_geo = geometry(
        rel, bin_index * row_share, row_share // BLOCK, first_plane, depth // BLOCK, side, map_side
    )
    pooling = pool_table(side, map_side).astype(jnp.bfloat16)
    pool_t = jnp.asarray(pooling.T)
    pool2 = jnp.asarray(np.concatenate([pooling, pooling], axis=0))
    table = hartley_table(side)
    ctf = ctf_table(defocus, side)

    target = image_bin[:, 0]
    chosen = (target[:, None] == jnp.arange(bins, dtype=jnp.int32)[None, :]).astype(jnp.int32)
    rank = jnp.sum((jnp.cumsum(chosen, axis=0) - chosen) * chosen, axis=1)
    slot = (target - bin_index) % bins * capacity + rank
    placement = jnp.arange(bins * capacity, dtype=jnp.int32)[:, None] == slot[None, :]
    order = jnp.sum(
        jnp.where(placement, jnp.arange(image_count, dtype=jnp.int32)[None, :], 0), axis=1
    )
    mark = image_pose * classes + image_class + 1
    marks = jnp.sum(jnp.where(placement, mark[None, :], 0), axis=1) - 1
    picked = pick_images(images, order, bins)
    picked, own_geo = lax.optimization_barrier((picked, own_geo))
    marks = marks.reshape(bins, capacity)
    got_images = [picked[0]] + [to_bin(picked[d], d) for d in range(1, bins)]
    got_marks = [marks[0]] + [to_bin(marks[d], d) for d in range(1, bins)]
    got_marks = jnp.concatenate(got_marks)
    got_pose, got_class = got_marks // classes, got_marks % classes
    at = jnp.argmax(
        (got_pose[:, None] == own_order[None, :]).astype(jnp.int32), axis=1
    ).astype(jnp.int32)
    label = jnp.where(got_marks >= 0, at * classes + got_class, -1)
    tally = jnp.sum(
        (
            label[:, None]
            == jnp.arange(pose_count * classes, dtype=jnp.int32)[None, :]
        ).astype(jnp.float32),
        axis=0,
    ).reshape(2, chips, owned * classes)

    def reduce_slab(keep, send):
        got = to_core(send)
        sums = [keep[d] + got[d] for d in range(chips)]
        moved = [to_chip(sums[d], d) for d in range(1, chips)]
        return [sums[0]] + moved

    tally = functools.reduce(jnp.add, reduce_slab(tally[0], tally[1]))

    def split(value):
        return value.reshape(chips, -1, *value.shape[1:])

    keep, send = first_projection(density, pool_t, own_geo, pose_count)
    proj_parts = reduce_slab(split(keep), split(send))
    keep, send = image_sums(got_images, label, ctf, table, pose_count)
    total = functools.reduce(jnp.add, reduce_slab(split(keep), split(send)))

    def share_field(field):
        near = [field] + [to_bin(field, bins - d) for d in range(1, bins)]
        near = jnp.concatenate(near, axis=0)
        row = [near] + [to_chip(near, chips - d) for d in range(1, chips)]
        return row + [to_core(part) for part in row]

    field = residual_field(proj_parts, total, tally, ctf, table, weight)
    first, keep, send = take_step(
        density, share_field(field), geo, wide_geo, step_sizes, bin_index, pool2, pool_t, poses,
        row_share,
    )
    parts = functools.reduce(jnp.add, reduce_slab(split(keep), split(send)))
    parts = parts.reshape(bins, owned, side, side)
    parts = [parts[0]] + [to_bin(parts[d], d) for d in range(1, bins)]
    field = residual_field(parts, total, tally, ctf, table, weight)
    gradient, refined = finish(first, share_field(field), geo, wide_geo, step_sizes, pool2, poses)
    return (gradient, refined)


def solution(mesh):
    return jax.shard_map(
        on_device,
        mesh=mesh,
        in_specs=(
            P("grp", "slab", None),
            P(("grp", "bin", "slab"), None, None),
            P(("grp", "bin", "slab"), None),
            P(("grp", "bin", "slab")),
            P(("grp", "bin", "slab")),
            P("grp"),
            P("grp", None),
            P(),
        ),
        out_specs=(P(("grp", "bin"), "slab", None), P(("grp", "bin"), "slab", None)),
        check_vma=False,
    )
```

```python
import functools
import math

import jax
import jax.numpy as jnp
import numpy as np
from jax import lax
from jax.experimental import pallas as pl
from jax.experimental.pallas import tpu as pltpu
from jax.sharding import PartitionSpec as P

AMP_CONTRAST = 0.1
PHASE_RATE = 60.0
BLOCK = 16
WINDOW = 16
LANES = 128
SMEM = pltpu.SMEM


def vmem():
    return pl.BlockSpec(memory_space=pltpu.VMEM)


def smem():
    return pl.BlockSpec(memory_space=SMEM)


def pool_table(image_side, map_side):
    row_index = np.arange(image_side)[:, None]
    col_index = np.arange(map_side)[None, :]
    return 0.5 * np.maximum(0.0, 1.0 - np.abs(col_index - 2.0 * row_index - 0.5) / 2.0)


def hartley_table(image_side):
    index_row = np.arange(image_side)
    phase_index = index_row[:, None] * index_row[None, :] % image_side
    angle_table = 2.0 * math.pi / image_side * phase_index
    table = (np.cos(angle_table) + np.sin(angle_table)) / math.sqrt(image_side)
    high = table.astype(jnp.bfloat16)
    low = (table - high.astype(np.float64)).astype(jnp.bfloat16)
    return jnp.asarray(np.concatenate([high, low], axis=1))


def ctf_table(defocus, image_side):
    index_row = jnp.arange(image_side, dtype=jnp.int32)
    frequency = (
        jnp.where(index_row < image_side // 2, index_row, index_row - image_side).astype(
            jnp.float32
        )
        / image_side
    )
    part = PHASE_RATE * defocus[:, None] * (frequency * frequency)[None, :]
    shifted = part + math.asin(AMP_CONTRAST)
    return -(
        jnp.sin(shifted)[:, :, None] * jnp.cos(part)[:, None, :]
        + jnp.cos(shifted)[:, :, None] * jnp.sin(part)[:, None, :]
    )


def geometry(angles, first_row, row_blocks, first_plane, plane_blocks, image_side, map_side):
    middle = map_side / 2.0
    scale = 0.25 / math.sqrt(map_side)
    cosine, sine = jnp.cos(angles), jnp.sin(angles)
    y_low = (first_row + BLOCK * jnp.arange(row_blocks)).astype(jnp.float32) + 0.5 - middle
    z_low = (first_plane + BLOCK * jnp.arange(plane_blocks)).astype(jnp.float32) + 0.5 - middle
    y_part = y_low[:, None] * cosine[None, :]
    z_part = z_low[:, None] * sine[None, :]
    y_edge = y_part + jnp.minimum(0.0, (BLOCK - 1) * cosine)[None, :]
    z_edge = z_part + jnp.minimum(0.0, (BLOCK - 1) * sine)[None, :]
    least = y_edge[:, None, :] + z_edge[None, :, :]
    column = jnp.floor((least - 3.0 + middle) / 2.0).astype(jnp.int32)
    start = jnp.clip(column, 0, image_side - WINDOW)
    offset = scale * (
        y_part[:, None, :] + z_part[None, :, :] - (2.0 * start.astype(jnp.float32) + 1.0 - middle)
    )
    direction = jnp.stack([cosine, sine]) * scale
    blocks = row_blocks * plane_blocks
    lanes = offset.reshape(blocks, 1, -1, 1) - 2.0 * scale * jnp.arange(
        WINDOW, dtype=jnp.float32
    )
    wide = jnp.repeat(direction, WINDOW, axis=1)
    return (
        (direction.reshape(-1), start.reshape(-1), offset.reshape(-1)),
        (wide, lanes.reshape(blocks, 1, -1)),
    )


def fill_windows(w_ref, direction, offset, block, poses, map_side):
    lane = lax.broadcasted_iota(jnp.int32, (8, BLOCK * BLOCK), 1)
    row = lax.broadcasted_iota(jnp.int32, (8, BLOCK * BLOCK), 0).astype(jnp.float32)
    y_local = (lane // BLOCK).astype(jnp.float32)
    z_local = (lane % BLOCK).astype(jnp.float32)
    peak = 0.5 / math.sqrt(map_side)
    rows = [peak * (row + 8.0 * k) for k in range(WINDOW // 8)]
    base = block * poses
    for pose in range(poses):
        line = (
            y_local * direction[pose] + z_local * direction[poses + pose] + offset[base + pose]
        )
        parts = [jnp.maximum(0.0, peak - jnp.abs(line - r)) for r in rows]
        w_ref[pose * WINDOW : (pose + 1) * WINDOW, :] = jnp.concatenate(parts, axis=0).astype(
            jnp.bfloat16
        )


def fill_turned(t_ref, wide, lanes, block, map_side):
    peak = 0.5 / math.sqrt(map_side)
    local = lax.broadcasted_iota(jnp.int32, (BLOCK, LANES), 0).astype(jnp.float32)
    offset = lanes[block]
    for at in range(0, wide.shape[1], LANES):
        span = slice(at, at + LANES)
        along_z = local * wide[1:2, span] + offset[:, span]
        along_y = wide[0:1, span]
        for y in range(BLOCK):
            line = along_z + float(y) * along_y
            t_ref[y * BLOCK : (y + 1) * BLOCK, span] = jnp.maximum(
                0.0, peak - jnp.abs(line)
            ).astype(jnp.bfloat16)


def add_projection(outs, prod, start, block, poses):
    base = block * poses
    share = poses // len(outs)
    for pose in range(poses):
        rows = pl.ds(start[base + pose], WINDOW)
        outs[pose // share][pose % share, rows, :] += prod[pose * WINDOW : (pose + 1) * WINDOW]


def first_projection_kernel(
    map_side, poses, direction, start, offset, dens, pool_t, keep, send, fold_ref, w_ref
):
    step = pl.program_id(0)

    @pl.when(step == 0)
    def _():
        keep[...] = jnp.zeros_like(keep)
        send[...] = jnp.zeros_like(send)

    height, depth, _ = dens.shape
    side = pool_t.shape[1]
    folded = jnp.dot(
        dens[...].reshape(height * depth, map_side), pool_t[...], preferred_element_type=jnp.float32
    )
    fold_ref[...] = folded.astype(jnp.bfloat16).reshape(height, depth, side)
    count = height * depth // (BLOCK * BLOCK)
    for k in range(count):
        row, plane = k // (depth // BLOCK) * BLOCK, k % (depth // BLOCK) * BLOCK
        weights = w_ref.at[k % 2]
        fill_windows(weights, direction, offset, step * count + k, poses, map_side)
        pixels = fold_ref[row : row + BLOCK, plane : plane + BLOCK, :].reshape(-1, side)
        prod = jnp.dot(weights[...], pixels, preferred_element_type=jnp.float32)
        add_projection((keep, send), prod, start, step * count + k, poses)


def first_projection(density, pool_t, geo, poses):
    map_side, depth, _ = density.shape
    side = pool_t.shape[1]
    height = 2 * BLOCK
    half = jax.ShapeDtypeStruct((poses // 2, side, side), jnp.float32)
    return pl.pallas_call(
        functools.partial(first_projection_kernel, map_side, poses),
        grid=(map_side // height,),
        in_specs=[smem(), smem(), smem(),
                  pl.BlockSpec((height, depth, map_side), lambda i: (i, 0, 0)),
                  vmem()],
        out_specs=[vmem(), vmem()],
        out_shape=[half, half],
        scratch_shapes=[
            pltpu.VMEM((height, depth, side), jnp.bfloat16),
            pltpu.VMEM((2, poses * WINDOW, BLOCK * BLOCK), jnp.bfloat16),
        ],
        name="first_projection",
    )(*geo, density, pool_t)


def pick_kernel(classes, owned, chips, where, bins_of, poses_of, classes_of, images, *refs):
    groups = (len(refs) - 1) // 2
    outs, labels, order = refs[:groups], refs[groups:-1], refs[-1]
    each = outs[0].shape[0]
    here, chip, core = where[0], where[1], where[2]
    for slot in range(groups * each):
        order[slot] = -1

    def place(n, _):
        away = lax.rem(bins_of[n] - here + groups, groups) * each

        def taken(k, rank):
            same = lax.rem(bins_of[k] - here + groups, groups) * each == away
            return rank + jnp.where(same, 1, 0)

        order[away + lax.fori_loop(0, n, taken, 0)] = n
        return 0

    lax.fori_loop(0, images.shape[0], place, 0)
    for group in range(groups):
        for k in range(each):
            source = order[group * each + k]
            image = jnp.maximum(source, 0)
            outs[group][k] = images[image]
            pose = poses_of[image]
            owner = pose // owned
            ahead = lax.rem(owner // 2 - chip + chips, chips)
            across = lax.rem(lax.rem(owner, 2) + core, 2)
            at = (across * chips + ahead) * owned + lax.rem(pose, owned)
            labels[group][k] = jnp.where(source >= 0, at * classes + classes_of[image], -1)


def pick_images(images, where, image_bin, image_pose, image_class, classes, owned, chips, groups):
    count, side, _ = images.shape
    each = count // 4
    return pl.pallas_call(
        functools.partial(pick_kernel, classes, owned, chips),
        in_specs=[smem()] * 4 + [vmem()],
        out_specs=[vmem()] * groups + [smem()] * groups,
        out_shape=[jax.ShapeDtypeStruct((each, side, side), images.dtype)] * groups
        + [jax.ShapeDtypeStruct((each,), jnp.int32)] * groups,
        scratch_shapes=[pltpu.SMEM((groups * each,), jnp.int32)],
        name="pick_images",
    )(where, image_bin, image_pose, image_class, images)


def times_hartley(value, table):
    count, side = value.shape
    high = value.astype(jnp.bfloat16)
    low = (value - high.astype(jnp.float32)).astype(jnp.bfloat16)
    both = jnp.dot(high, table, preferred_element_type=jnp.float32)
    rest = jnp.dot(low, table[:, :side], preferred_element_type=jnp.float32)
    return both[:, :side] + (both[:, side:] + rest)


def spectrum_kernel(groups, each, classes, label, ctf, table, *refs):
    images, (keep, send) = refs[:groups], refs[groups:]
    half = keep.shape[0]
    side = keep.shape[1]
    keep[...] = jnp.zeros_like(keep)
    send[...] = jnp.zeros_like(send)
    hart = table[...]
    for group in range(groups):
        pixels = images[group][...].reshape(each * side, side)
        both = jnp.dot(pixels, hart, preferred_element_type=jnp.float32)
        along = (both[:, :side] + both[:, side:]).reshape(each, side, side)
        turned = jnp.concatenate([along[k].T for k in range(each)], axis=0)
        full = times_hartley(turned, hart).reshape(each, side, side)
        for k in range(each):
            mark = label[group * each + k]
            pose = mark // classes
            value = ctf[mark % classes] * full[k]

            @pl.when(jnp.logical_and(mark >= 0, pose < half))
            def _(pose=pose, value=value):
                keep[pose] += value

            @pl.when(pose >= half)
            def _(pose=pose, value=value):
                send[pose - half] += value

    for out in (keep, send):
        for pose in range(half):
            out[pose] = out[pose].T


def image_sums(images, label, ctf, table, poses):
    each, side, _ = images[0].shape
    half = jax.ShapeDtypeStruct((poses // 2, side, side), jnp.float32)
    return pl.pallas_call(
        functools.partial(spectrum_kernel, len(images), each, ctf.shape[0]),
        in_specs=[smem(), vmem(), vmem()] + [vmem()] * len(images),
        out_specs=[vmem(), vmem()],
        out_shape=[half, half],
        name="image_sums",
    )(label, ctf, table, *images)


def filter_kernel(weight, tally, ctf, table, power, *refs):
    proj, total, out = refs[:-2], refs[-2], refs[-1]
    owned, side, _ = out.shape
    classes = ctf.shape[0]
    hart = table[...]
    value = proj[0][...]
    for part in proj[1:]:
        value = value + part[...]
    along = times_hartley(value.reshape(owned * side, side), hart)
    turned = jnp.concatenate([along[k * side : (k + 1) * side].T for k in range(owned)], axis=0)
    full = times_hartley(turned, hart)
    parts = []
    for k in range(owned):
        gain = jnp.zeros((side, side), jnp.float32)
        for c in range(classes):
            gain = gain + tally[k * classes + c] * (ctf[c] * ctf[c])
        parts.append(weight * (gain * full[k * side : (k + 1) * side] - total[k]))
    along = times_hartley(jnp.concatenate(parts, axis=0), hart)
    turned = jnp.concatenate([along[k * side : (k + 1) * side].T for k in range(owned)], axis=0)
    field = times_hartley(turned, hart)
    out[...] = field.reshape(owned, side, side).astype(out.dtype)


def residual_field(parts, total, tally, ctf, table, weight):
    owned, side, _ = total.shape

    def kernel(tally, ctf, table, *refs):
        filter_kernel(weight, tally, ctf, table, None, *refs)

    return pl.pallas_call(
        kernel,
        in_specs=[smem(), vmem(), vmem()] + [vmem()] * (len(parts) + 1),
        out_specs=vmem(),
        out_shape=jax.ShapeDtypeStruct((owned, side, side), jnp.bfloat16),
        name="residual_field",
    )(tally, ctf, table, *parts, total)


def load_fields(field, fields):
    at = 0
    for part in fields:
        count = part.shape[0]
        field[at : at + count] = part[...].astype(jnp.float32)
        at += count


def gather_windows(f_ref, field, start, block, poses):
    base = block * poses
    for pose in range(poses):
        f_ref[pose * WINDOW : (pose + 1) * WINDOW, :] = field[
            pose, pl.ds(start[base + pose], WINDOW), :
        ].astype(jnp.bfloat16)


def block_gradient(t_ref, f_ref, pool2):
    back = jnp.dot(t_ref[...], f_ref[...], preferred_element_type=jnp.float32)
    high = back.astype(jnp.bfloat16)
    low = (back - high.astype(jnp.float32)).astype(jnp.bfloat16)
    return jnp.dot(
        jnp.concatenate([high, low], axis=1), pool2[...], preferred_element_type=jnp.float32
    )


def step_kernel(
    map_side, poses, parts, bin_ref, direction, start, offset, sizes, dens, wide, lanes, pool2,
    pool_t, *refs
):
    fields = refs[:parts]
    first, keep, send, field, t_ref, w_ref, f_ref = refs[parts:]
    step = pl.program_id(0)

    @pl.when(step == 0)
    def _():
        keep[...] = jnp.zeros_like(keep)
        send[...] = jnp.zeros_like(send)
        load_fields(field, fields)

    count = dens.shape[1] // BLOCK
    for k in range(count):
        planes = slice(k * BLOCK, (k + 1) * BLOCK)
        index = step * count + k
        turned, weights, windows = t_ref.at[k % 2], w_ref.at[k % 2], f_ref.at[k % 2]
        fill_turned(turned, wide, lanes, index, map_side)
        gather_windows(windows, field, start, index, poses)
        grad = block_gradient(turned, windows, pool2)
        values = dens[:, planes, :].reshape(BLOCK * BLOCK, map_side).astype(jnp.float32)
        moved = values - sizes[0] * grad
        first[:, planes, :] = moved.reshape(BLOCK, BLOCK, map_side)
        folded = jnp.dot(
            moved.astype(jnp.bfloat16), pool_t[...], preferred_element_type=jnp.float32
        )
        fill_windows(weights, direction, offset, index, poses, map_side)
        prod = jnp.dot(
            weights[...], folded.astype(jnp.bfloat16), preferred_element_type=jnp.float32
        )
        add_projection((keep, send), prod, start, index, poses)


def take_step(density, fields, geo, wide_geo, sizes, bin_index, pool2, pool_t, poses, row_share):
    map_side, depth, _ = density.shape
    side = pool_t.shape[1]
    half = jax.ShapeDtypeStruct((poses // 2, side, side), jnp.float32)
    row_blocks = row_share // BLOCK
    rows = (BLOCK, depth, map_side)
    return pl.pallas_call(
        functools.partial(step_kernel, map_side, poses, len(fields)),
        grid_spec=pltpu.PrefetchScalarGridSpec(
            num_scalar_prefetch=1,
            grid=(row_blocks,),
            in_specs=[smem()] * 4
            + [pl.BlockSpec(rows, lambda i, at: (at[0] * row_blocks + i, 0, 0))]
            + [vmem()] * (4 + len(fields)),
            out_specs=[pl.BlockSpec(rows, lambda i, at: (i, 0, 0)), vmem(), vmem()],
            scratch_shapes=[
                pltpu.VMEM((poses, side, side), jnp.float32),
                pltpu.VMEM((2, BLOCK * BLOCK, poses * WINDOW), jnp.bfloat16),
                pltpu.VMEM((2, poses * WINDOW, BLOCK * BLOCK), jnp.bfloat16),
                pltpu.VMEM((2, poses * WINDOW, side), jnp.bfloat16),
            ],
        ),
        out_shape=[jax.ShapeDtypeStruct((row_share, depth, map_side), jnp.float32), half, half],
        name="take_step",
    )(bin_index.reshape(1), *geo, sizes, density, *wide_geo, pool2, pool_t, *fields)


def finish_kernel(map_side, poses, parts, start, sizes, first, wide, lanes, pool2, *refs):
    fields = refs[:parts]
    gradient, refined, field, t_ref, f_ref = refs[parts:]
    step = pl.program_id(0)

    @pl.when(step == 0)
    def _():
        load_fields(field, fields)

    count = first.shape[1] // BLOCK
    for k in range(count):
        planes = slice(k * BLOCK, (k + 1) * BLOCK)
        index = step * count + k
        turned, windows = t_ref.at[k % 2], f_ref.at[k % 2]
        fill_turned(turned, wide, lanes, index, map_side)
        gather_windows(windows, field, start, index, poses)
        grad = block_gradient(turned, windows, pool2).reshape(BLOCK, BLOCK, map_side)
        gradient[:, planes, :] = grad
        refined[:, planes, :] = first[:, planes, :] - sizes[1] * grad


def finish(first, fields, geo, wide_geo, sizes, pool2, poses):
    row_share, depth, map_side = first.shape
    side = pool2.shape[0] // 2
    rows = pl.BlockSpec((BLOCK, depth, map_side), lambda i: (i, 0, 0))
    out = jax.ShapeDtypeStruct(first.shape, jnp.float32)
    return pl.pallas_call(
        functools.partial(finish_kernel, map_side, poses, len(fields)),
        grid=(row_share // BLOCK,),
        in_specs=[smem()] * 2 + [rows] + [vmem()] * (3 + len(fields)),
        out_specs=[rows, rows],
        out_shape=[out, out],
        scratch_shapes=[
            pltpu.VMEM((poses, side, side), jnp.float32),
            pltpu.VMEM((2, BLOCK * BLOCK, poses * WINDOW), jnp.bfloat16),
            pltpu.VMEM((2, poses * WINDOW, side), jnp.bfloat16),
        ],
        name="finish",
    )(geo[1], sizes, first, *wide_geo, pool2, *fields)


def on_device(
    density, images, image_bin, image_pose, image_class, defocus, pose_offset, step_sizes
):
    bins = lax.axis_size("bin")
    slabs = lax.axis_size("slab")
    chips = slabs // 2
    bin_index = lax.axis_index("bin")
    slab_index = lax.axis_index("slab")
    chip, core = slab_index // 2, slab_index % 2
    map_side, depth, _ = density.shape
    image_count, side, _ = images.shape
    pose_count = pose_offset.shape[1]
    classes = defocus.shape[0]
    row_share = map_side // bins
    owned = pose_count // slabs
    weight = 16.0 * pose_count / (image_count * slabs)

    def to_core(value):
        return lax.ppermute(value, "slab", [(s, s ^ 1) for s in range(slabs)])

    def to_chip(value, shift):
        return lax.ppermute(
            value, "slab", [(s, (s + 2 * shift) % slabs) for s in range(slabs)]
        )

    def to_bin(value, shift):
        return lax.ppermute(value, "bin", [(b, (b + shift) % bins) for b in range(bins)])

    where = jnp.stack([bin_index, chip, core]).astype(jnp.int32)
    picked = pick_images(
        images, where, image_bin[:, 0], image_pose, image_class, classes, owned, chips, bins
    )
    picked, pose_offset, defocus = lax.optimization_barrier((picked, pose_offset, defocus))
    marks, picked = picked[bins:], picked[:bins]
    got_marks = [marks[0]] + [to_bin(marks[d], d) for d in range(1, bins)]
    got_images = [picked[0]] + [to_bin(picked[d], d) for d in range(1, bins)]
    label = jnp.concatenate(got_marks)
    cores_on, chips_on, place = jnp.meshgrid(
        jnp.arange(2), jnp.arange(chips), jnp.arange(owned), indexing="ij"
    )
    owner = (chip + chips_on) % chips * 2 + (core + cores_on) % 2
    own_order = (owner * owned + place).reshape(-1)
    own_offset = jnp.take(
        lax.dynamic_index_in_dim(pose_offset, bin_index, 0, keepdims=False), own_order
    )
    own_angles = math.pi * (bin_index.astype(jnp.float32) + own_offset) / bins
    bin_order = (bin_index + jnp.arange(bins)) % bins
    rel = jnp.take(jnp.take(pose_offset, bin_order, axis=0), own_order, axis=1)
    rel = math.pi * (bin_order.astype(jnp.float32)[:, None] + rel) / bins
    rel = rel.reshape(bins, 2, chips, owned).transpose(1, 2, 0, 3).reshape(-1)
    poses = bins * pose_count
    first_plane = slab_index * depth
    own_geo, _ = geometry(
        own_angles, 0, map_side // BLOCK, first_plane, depth // BLOCK, side, map_side
    )
    geo, wide_geo = geometry(
        rel, bin_index * row_share, row_share // BLOCK, first_plane, depth // BLOCK, side, map_side
    )
    pooling = pool_table(side, map_side).astype(jnp.bfloat16)
    pool_t = jnp.asarray(pooling.T)
    pool2 = jnp.asarray(np.concatenate([pooling, pooling], axis=0))
    table = hartley_table(side)
    ctf = ctf_table(defocus, side)

    tally = jnp.sum(
        (
            label[:, None]
            == jnp.arange(pose_count * classes, dtype=jnp.int32)[None, :]
        ).astype(jnp.float32),
        axis=0,
    ).reshape(2, chips, owned * classes)

    def reduce_slab(keep, send):
        got = to_core(send)
        sums = [keep[d] + got[d] for d in range(chips)]
        moved = [to_chip(sums[d], d) for d in range(1, chips)]
        return [sums[0]] + moved

    tally = functools.reduce(jnp.add, reduce_slab(tally[0], tally[1]))

    def split(value):
        return value.reshape(chips, -1, *value.shape[1:])

    keep, send = first_projection(density, pool_t, own_geo, pose_count)
    keep, send, geo, wide_geo = lax.optimization_barrier((keep, send, geo, wide_geo))
    proj_parts = reduce_slab(split(keep), split(send))
    keep, send = image_sums(got_images, label, ctf, table, pose_count)
    total = functools.reduce(jnp.add, reduce_slab(split(keep), split(send)))

    def share_field(field):
        near = [field] + [to_bin(field, bins - d) for d in range(1, bins)]
        near = jnp.concatenate(near, axis=0)
        row = [near] + [to_chip(near, chips - d) for d in range(1, chips)]
        return row + [to_core(part) for part in row]

    field = residual_field(proj_parts, total, tally, ctf, table, weight)
    first, keep, send = take_step(
        density, share_field(field), geo, wide_geo, step_sizes, bin_index, pool2, pool_t, poses,
        row_share,
    )
    parts = functools.reduce(jnp.add, reduce_slab(split(keep), split(send)))
    parts = parts.reshape(bins, owned, side, side)
    parts = [parts[0]] + [to_bin(parts[d], d) for d in range(1, bins)]
    field = residual_field(parts, total, tally, ctf, table, weight)
    gradient, refined = finish(first, share_field(field), geo, wide_geo, step_sizes, pool2, poses)
    return (gradient, refined)


def solution(mesh):
    return jax.shard_map(
        on_device,
        mesh=mesh,
        in_specs=(
            P("grp", "slab", None),
            P(("grp", "bin", "slab"), None, None),
            P(("grp", "bin", "slab"), None),
            P(("grp", "bin", "slab")),
            P(("grp", "bin", "slab")),
            P("grp"),
            P("grp", None),
            P(),
        ),
        out_specs=(P(("grp", "bin"), "slab", None), P(("grp", "bin"), "slab", None)),
        check_vma=False,
    )
```

```python
import functools
import math

import jax
import jax.numpy as jnp
import numpy as np
from jax import lax
from jax.experimental import pallas as pl
from jax.experimental.pallas import tpu as pltpu
from jax.sharding import PartitionSpec as P

AMP_CONTRAST = 0.1
PHASE_RATE = 60.0
BLOCK = 16
WINDOW = 16
LANES = 128
SMEM = pltpu.SMEM


def vmem():
    return pl.BlockSpec(memory_space=pltpu.VMEM)


def smem():
    return pl.BlockSpec(memory_space=SMEM)


def pool_table(image_side, map_side):
    row_index = np.arange(image_side)[:, None]
    col_index = np.arange(map_side)[None, :]
    return 0.5 * np.maximum(0.0, 1.0 - np.abs(col_index - 2.0 * row_index - 0.5) / 2.0)


def hartley_table(image_side):
    index_row = np.arange(image_side)
    phase_index = index_row[:, None] * index_row[None, :] % image_side
    angle_table = 2.0 * math.pi / image_side * phase_index
    table = (np.cos(angle_table) + np.sin(angle_table)) / math.sqrt(image_side)
    high = table.astype(jnp.bfloat16)
    low = (table - high.astype(np.float64)).astype(jnp.bfloat16)
    return jnp.asarray(np.concatenate([high, low], axis=1))


def ctf_table(defocus, image_side):
    index_row = jnp.arange(image_side, dtype=jnp.int32)
    frequency = (
        jnp.where(index_row < image_side // 2, index_row, index_row - image_side).astype(
            jnp.float32
        )
        / image_side
    )
    part = PHASE_RATE * defocus[:, None] * (frequency * frequency)[None, :]
    shifted = part + math.asin(AMP_CONTRAST)
    return -(
        jnp.sin(shifted)[:, :, None] * jnp.cos(part)[:, None, :]
        + jnp.cos(shifted)[:, :, None] * jnp.sin(part)[:, None, :]
    )


def block_lines(theta, y_low, z_low, side, map_side):
    middle = map_side / 2.0
    scale = 0.25 / math.sqrt(map_side)
    cosine, sine = jnp.cos(theta), jnp.sin(theta)
    y_part = (y_low.astype(jnp.float32) + (0.5 - middle)) * cosine
    z_part = (z_low.astype(jnp.float32) + (0.5 - middle)) * sine
    least = (
        y_part
        + jnp.minimum(0.0, (BLOCK - 1.0) * cosine)
        + z_part
        + jnp.minimum(0.0, (BLOCK - 1.0) * sine)
    )
    column = jnp.floor((least + (middle - 3.0)) * 0.5).astype(jnp.int32)
    start = jnp.clip(column, 0, side - WINDOW)
    offset = scale * (y_part + z_part - (2.0 * start.astype(jnp.float32) + (1.0 - middle)))
    return cosine * scale, sine * scale, start, offset


def geometry_kernel(
    sizes, where, offsets, own_cos, own_sin, own_start, own_offset, cosine, sine, start, offset,
    wide, lanes
):
    map_side, side, depth, row_share, bins, chips, owned = sizes
    here, chip, core = where[0], where[1], where[2]
    first_plane = (chip * 2 + core) * depth
    plane_blocks = depth // BLOCK

    def turn(away, place):
        across, ahead, beyond = away
        bin_at = lax.rem(here + beyond, bins)
        owner = lax.rem(chip + ahead, chips) * 2 + lax.rem(core + across, 2)
        return bin_at.astype(jnp.float32) + offsets[bin_at, owner * owned + place]

    def listed(beyonds):
        return [
            turn((across, ahead, beyond), place)
            for across in range(2)
            for ahead in range(chips)
            for beyond in range(beyonds)
            for place in range(owned)
        ]

    def spread(values, index, shape):
        theta = jnp.zeros(shape, jnp.float32)
        for k, value in enumerate(values):
            theta = jnp.where(index == k, value, theta)
        return math.pi * theta / bins

    def fill(outs, values, first_row):
        shape = outs[0].shape
        row = lax.broadcasted_iota(jnp.int32, shape, 0)
        block = lax.broadcasted_iota(jnp.int32, shape, 1)
        theta = spread(values, row, shape)
        found = block_lines(
            theta,
            first_row + block // plane_blocks * BLOCK,
            first_plane + block % plane_blocks * BLOCK,
            side,
            map_side,
        )
        for out, value in zip(outs, found):
            out[...] = value

    first_row = here * row_share
    values = listed(bins)
    fill((own_cos, own_sin, own_start, own_offset), listed(1), 0)
    fill((cosine, sine, start, offset), values, first_row)
    shape = lanes.shape
    block = lax.broadcasted_iota(jnp.int32, shape, 0)
    lane = lax.broadcasted_iota(jnp.int32, shape, 1)
    along_y, along_z, _, offset_wide = block_lines(
        spread(values, lane // WINDOW, shape),
        first_row + block // plane_blocks * BLOCK,
        first_plane + block % plane_blocks * BLOCK,
        side,
        map_side,
    )
    peak = 0.5 / math.sqrt(map_side)
    lanes[...] = offset_wide - peak * (lane % WINDOW).astype(jnp.float32)
    wide[0:1, :] = along_y[0:1]
    wide[1:2, :] = along_z[0:1]


def make_geometry(where, pose_offset, map_side, side, depth, row_share, chips, owned):
    bins, pose_count = pose_offset.shape
    poses = bins * pose_count

    def tables(count, blocks):
        shape = (count, -(-blocks // LANES) * LANES)
        return [jax.ShapeDtypeStruct(shape, t) for t in (jnp.float32,) * 2] + [
            jax.ShapeDtypeStruct(shape, jnp.int32),
            jax.ShapeDtypeStruct(shape, jnp.float32),
        ]

    plane_blocks = depth // BLOCK
    blocks = row_share // BLOCK * plane_blocks
    shapes = (
        tables(pose_count, map_side // BLOCK * plane_blocks)
        + tables(poses, blocks)
        + [
            jax.ShapeDtypeStruct((2, poses * WINDOW), jnp.float32),
            jax.ShapeDtypeStruct((blocks, poses * WINDOW), jnp.float32),
        ]
    )
    sizes = (map_side, side, depth, row_share, bins, chips, owned)
    out = pl.pallas_call(
        functools.partial(geometry_kernel, sizes),
        in_specs=[smem(), smem()],
        out_specs=[vmem()] * len(shapes),
        out_shape=shapes,
        name="geometry",
    )(where, pose_offset)
    return out[:4], out[4:8], out[8:]


def fill_windows(w_ref, geo, block, poses, map_side):
    lane = lax.broadcasted_iota(jnp.int32, (8, BLOCK * BLOCK), 1)
    row = lax.broadcasted_iota(jnp.int32, (8, BLOCK * BLOCK), 0).astype(jnp.float32)
    y_local = (lane // BLOCK).astype(jnp.float32)
    z_local = (lane % BLOCK).astype(jnp.float32)
    peak = 0.5 / math.sqrt(map_side)
    rows = [peak * (row + 8.0 * k) for k in range(WINDOW // 8)]
    cosine, sine, _, offset = geo
    for pose in range(poses):
        line = y_local * cosine[pose, 0] + z_local * sine[pose, 0] + offset[pose, block]
        parts = [jnp.maximum(0.0, peak - jnp.abs(line - r)) for r in rows]
        w_ref[pose * WINDOW : (pose + 1) * WINDOW, :] = jnp.concatenate(parts, axis=0).astype(
            jnp.bfloat16
        )


def fill_turned(t_ref, wide, lanes, block, map_side):
    peak = 0.5 / math.sqrt(map_side)
    local = lax.broadcasted_iota(jnp.int32, (BLOCK, LANES), 0).astype(jnp.float32)
    offset = lanes[pl.ds(block, 1), :]
    for at in range(0, wide.shape[1], LANES):
        span = slice(at, at + LANES)
        along_z = local * wide[1:2, span] + offset[:, span]
        along_y = wide[0:1, span]
        for y in range(BLOCK):
            line = along_z + float(y) * along_y
            t_ref[y * BLOCK : (y + 1) * BLOCK, span] = jnp.maximum(
                0.0, peak - jnp.abs(line)
            ).astype(jnp.bfloat16)


def add_projection(outs, prod, start, block, poses):
    share = poses // len(outs)
    for pose in range(poses):
        rows = pl.ds(start[pose, block], WINDOW)
        outs[pose // share][pose % share, rows, :] += prod[pose * WINDOW : (pose + 1) * WINDOW]


def first_projection_kernel(
    map_side, poses, cosine, sine, start, offset, dens, pool_t, keep, send, fold_ref, w_ref
):
    step = pl.program_id(0)
    geo = (cosine, sine, start, offset)

    @pl.when(step == 0)
    def _():
        keep[...] = jnp.zeros_like(keep)
        send[...] = jnp.zeros_like(send)

    height, depth, _ = dens.shape
    side = pool_t.shape[1]
    folded = jnp.dot(
        dens[...].reshape(height * depth, map_side), pool_t[...], preferred_element_type=jnp.float32
    )
    fold_ref[...] = folded.astype(jnp.bfloat16).reshape(height, depth, side)
    count = height * depth // (BLOCK * BLOCK)
    for k in range(count):
        row, plane = k // (depth // BLOCK) * BLOCK, k % (depth // BLOCK) * BLOCK
        weights = w_ref.at[k % 2]
        fill_windows(weights, geo, step * count + k, poses, map_side)
        pixels = fold_ref[row : row + BLOCK, plane : plane + BLOCK, :].reshape(-1, side)
        prod = jnp.dot(weights[...], pixels, preferred_element_type=jnp.float32)
        add_projection((keep, send), prod, start, step * count + k, poses)


def first_projection(density, pool_t, geo, poses):
    map_side, depth, _ = density.shape
    side = pool_t.shape[1]
    height = 2 * BLOCK
    half = jax.ShapeDtypeStruct((poses // 2, side, side), jnp.float32)
    return pl.pallas_call(
        functools.partial(first_projection_kernel, map_side, poses),
        grid=(map_side // height,),
        in_specs=[smem(), smem(), smem(), smem(),
                  pl.BlockSpec((height, depth, map_side), lambda i: (i, 0, 0)),
                  vmem()],
        out_specs=[vmem(), vmem()],
        out_shape=[half, half],
        scratch_shapes=[
            pltpu.VMEM((height, depth, side), jnp.bfloat16),
            pltpu.VMEM((2, poses * WINDOW, BLOCK * BLOCK), jnp.bfloat16),
        ],
        name="first_projection",
    )(*geo, density, pool_t)


def pick_kernel(owned, chips, where, bins_of, poses_of, classes_of, images, *refs):
    outs, order = refs[:-1], refs[-1]
    groups = len(outs)
    each = outs[0].shape[0]
    side = images.shape[1]
    lane = lax.broadcasted_iota(jnp.int32, (BLOCK, side), 1)
    here, chip, core = where[0], where[1], where[2]
    for slot in range(groups * each):
        order[slot] = -1

    def place(n, _):
        away = lax.rem(bins_of[n] - here + groups, groups) * each

        def taken(k, rank):
            same = lax.rem(bins_of[k] - here + groups, groups) * each == away
            return rank + jnp.where(same, 1, 0)

        order[away + lax.fori_loop(0, n, taken, 0)] = n
        return 0

    lax.fori_loop(0, images.shape[0], place, 0)
    for group in range(groups):
        for k in range(each):
            source = order[group * each + k]
            image = jnp.maximum(source, 0)
            outs[group][k, 0:side, :] = images[image]
            pose = poses_of[image]
            owner = pose // owned
            ahead = lax.rem(owner // 2 - chip + chips, chips)
            across = lax.rem(lax.rem(owner, 2) + core, 2)
            at = (across * chips + ahead) * owned + lax.rem(pose, owned)
            at = jnp.where(source >= 0, at, -1).astype(jnp.float32)
            named = classes_of[image].astype(jnp.float32)
            outs[group][k, side : side + BLOCK, :] = jnp.where(
                lane == 0, at, jnp.where(lane == 1, named, 0.0)
            ).astype(images.dtype)


def pick_images(images, where, image_bin, image_pose, image_class, owned, chips, groups):
    count, side, _ = images.shape
    each = count // 4
    out = jax.ShapeDtypeStruct((each, side + BLOCK, side), images.dtype)
    return pl.pallas_call(
        functools.partial(pick_kernel, owned, chips),
        in_specs=[smem()] * 4 + [vmem()],
        out_specs=[vmem()] * groups,
        out_shape=[out] * groups,
        scratch_shapes=[pltpu.SMEM((groups * each,), jnp.int32)],
        name="pick_images",
    )(where, image_bin, image_pose, image_class, images)


def times_hartley(value, table):
    count, side = value.shape
    high = value.astype(jnp.bfloat16)
    low = (value - high.astype(jnp.float32)).astype(jnp.bfloat16)
    both = jnp.dot(high, table, preferred_element_type=jnp.float32)
    rest = jnp.dot(low, table[:, :side], preferred_element_type=jnp.float32)
    return both[:, :side] + (both[:, side:] + rest)


def spectrum_kernel(groups, each, ctf, table, *refs):
    images, (keep, send, tally, marks, label, sem) = refs[:groups], refs[groups:]
    half = keep.shape[0]
    side = keep.shape[1]
    classes = ctf.shape[0]
    for group in range(groups):
        for k in range(each):
            at = group * each + k
            row = images[group][k, side : side + BLOCK, :].astype(jnp.float32)
            marks[at : at + 1, :] = row[0:1].astype(jnp.int32)
    copy = pltpu.make_async_copy(marks, label, sem)
    copy.start()
    keep[...] = jnp.zeros_like(keep)
    send[...] = jnp.zeros_like(send)
    for k in range(tally.shape[0]):
        tally[k] = 0.0
    hart = table[...]
    copy.wait()
    for group in range(groups):
        pixels = images[group][:, 0:side, :].reshape(each * side, side)
        both = jnp.dot(pixels, hart, preferred_element_type=jnp.float32)
        along = (both[:, :side] + both[:, side:]).reshape(each, side, side)
        turned = jnp.concatenate([along[k].T for k in range(each)], axis=0)
        full = times_hartley(turned, hart).reshape(each, side, side)
        for k in range(each):
            pose, kind = label[group * each + k, 0], label[group * each + k, 1]
            value = ctf[kind] * full[k]

            @pl.when(pose >= 0)
            def _(pose=pose, kind=kind):
                tally[pose * classes + kind] += 1.0

            @pl.when(jnp.logical_and(pose >= 0, pose < half))
            def _(pose=pose, value=value):
                keep[pose] += value

            @pl.when(pose >= half)
            def _(pose=pose, value=value):
                send[pose - half] += value

    for out in (keep, send):
        for pose in range(half):
            out[pose] = out[pose].T


def image_sums(images, ctf, table, poses):
    each, _, side = images[0].shape
    slots = each * len(images)
    half = jax.ShapeDtypeStruct((poses // 2, side, side), jnp.float32)
    return pl.pallas_call(
        functools.partial(spectrum_kernel, len(images), each),
        in_specs=[vmem(), vmem()] + [vmem()] * len(images),
        out_specs=[vmem(), vmem(), smem()],
        out_shape=[half, half, jax.ShapeDtypeStruct((poses * ctf.shape[0],), jnp.float32)],
        scratch_shapes=[
            pltpu.VMEM((slots, side), jnp.int32),
            pltpu.SMEM((slots, side), jnp.int32),
            pltpu.SemaphoreType.DMA(()),
        ],
        name="image_sums",
    )(ctf, table, *images)


def filter_kernel(weight, tally, ctf, table, power, *refs):
    proj, total, out = refs[:-2], refs[-2], refs[-1]
    owned, side, _ = out.shape
    classes = ctf.shape[0]
    hart = table[...]
    value = proj[0][...]
    for part in proj[1:]:
        value = value + part[...]
    along = times_hartley(value.reshape(owned * side, side), hart)
    turned = jnp.concatenate([along[k * side : (k + 1) * side].T for k in range(owned)], axis=0)
    full = times_hartley(turned, hart)
    parts = []
    for k in range(owned):
        gain = jnp.zeros((side, side), jnp.float32)
        for c in range(classes):
            gain = gain + tally[k * classes + c] * (ctf[c] * ctf[c])
        parts.append(weight * (gain * full[k * side : (k + 1) * side] - total[k]))
    along = times_hartley(jnp.concatenate(parts, axis=0), hart)
    turned = jnp.concatenate([along[k * side : (k + 1) * side].T for k in range(owned)], axis=0)
    field = times_hartley(turned, hart)
    out[...] = field.reshape(owned, side, side).astype(out.dtype)


def residual_field(parts, total, tally, ctf, table, weight):
    owned, side, _ = total.shape

    def kernel(tally, ctf, table, *refs):
        filter_kernel(weight, tally, ctf, table, None, *refs)

    return pl.pallas_call(
        kernel,
        in_specs=[smem(), vmem(), vmem()] + [vmem()] * (len(parts) + 1),
        out_specs=vmem(),
        out_shape=jax.ShapeDtypeStruct((owned, side, side), jnp.bfloat16),
        name="residual_field",
    )(tally, ctf, table, *parts, total)


def load_fields(field, fields):
    at = 0
    for part in fields:
        count = part.shape[0]
        field[at : at + count] = part[...].astype(jnp.float32)
        at += count


def gather_windows(f_ref, field, start, block, poses):
    for pose in range(poses):
        f_ref[pose * WINDOW : (pose + 1) * WINDOW, :] = field[
            pose, pl.ds(start[pose, block], WINDOW), :
        ].astype(jnp.bfloat16)


def block_gradient(t_ref, f_ref, pool2):
    back = jnp.dot(t_ref[...], f_ref[...], preferred_element_type=jnp.float32)
    high = back.astype(jnp.bfloat16)
    low = (back - high.astype(jnp.float32)).astype(jnp.bfloat16)
    return jnp.dot(
        jnp.concatenate([high, low], axis=1), pool2[...], preferred_element_type=jnp.float32
    )


def step_kernel(
    map_side, poses, parts, bin_ref, cosine, sine, start, offset, sizes, dens, wide, lanes, pool2,
    pool_t, *refs
):
    geo = (cosine, sine, start, offset)
    fields = refs[:parts]
    first, keep, send, field, t_ref, w_ref, f_ref = refs[parts:]
    step = pl.program_id(0)

    @pl.when(step == 0)
    def _():
        keep[...] = jnp.zeros_like(keep)
        send[...] = jnp.zeros_like(send)
        load_fields(field, fields)

    count = dens.shape[1] // BLOCK
    for k in range(count):
        planes = slice(k * BLOCK, (k + 1) * BLOCK)
        index = step * count + k
        turned, weights, windows = t_ref.at[k % 2], w_ref.at[k % 2], f_ref.at[k % 2]
        fill_turned(turned, wide, lanes, index, map_side)
        gather_windows(windows, field, start, index, poses)
        grad = block_gradient(turned, windows, pool2)
        values = dens[:, planes, :].reshape(BLOCK * BLOCK, map_side).astype(jnp.float32)
        moved = values - sizes[0] * grad
        first[:, planes, :] = moved.reshape(BLOCK, BLOCK, map_side)
        folded = jnp.dot(
            moved.astype(jnp.bfloat16), pool_t[...], preferred_element_type=jnp.float32
        )
        fill_windows(weights, geo, index, poses, map_side)
        prod = jnp.dot(
            weights[...], folded.astype(jnp.bfloat16), preferred_element_type=jnp.float32
        )
        add_projection((keep, send), prod, start, index, poses)


def take_step(density, fields, geo, wide_geo, sizes, bin_index, pool2, pool_t, poses, row_share):
    map_side, depth, _ = density.shape
    side = pool_t.shape[1]
    half = jax.ShapeDtypeStruct((poses // 2, side, side), jnp.float32)
    row_blocks = row_share // BLOCK
    rows = (BLOCK, depth, map_side)
    return pl.pallas_call(
        functools.partial(step_kernel, map_side, poses, len(fields)),
        grid_spec=pltpu.PrefetchScalarGridSpec(
            num_scalar_prefetch=1,
            grid=(row_blocks,),
            in_specs=[smem()] * 5
            + [pl.BlockSpec(rows, lambda i, at: (at[0] * row_blocks + i, 0, 0))]
            + [vmem()] * (4 + len(fields)),
            out_specs=[pl.BlockSpec(rows, lambda i, at: (i, 0, 0)), vmem(), vmem()],
            scratch_shapes=[
                pltpu.VMEM((poses, side, side), jnp.float32),
                pltpu.VMEM((2, BLOCK * BLOCK, poses * WINDOW), jnp.bfloat16),
                pltpu.VMEM((2, poses * WINDOW, BLOCK * BLOCK), jnp.bfloat16),
                pltpu.VMEM((2, poses * WINDOW, side), jnp.bfloat16),
            ],
        ),
        out_shape=[jax.ShapeDtypeStruct((row_share, depth, map_side), jnp.float32), half, half],
        name="take_step",
    )(bin_index.reshape(1), *geo, sizes, density, *wide_geo, pool2, pool_t, *fields)


def finish_kernel(map_side, poses, parts, start, sizes, first, wide, lanes, pool2, *refs):
    fields = refs[:parts]
    gradient, refined, field, t_ref, f_ref = refs[parts:]
    step = pl.program_id(0)

    @pl.when(step == 0)
    def _():
        load_fields(field, fields)

    count = first.shape[1] // BLOCK
    for k in range(count):
        planes = slice(k * BLOCK, (k + 1) * BLOCK)
        index = step * count + k
        turned, windows = t_ref.at[k % 2], f_ref.at[k % 2]
        fill_turned(turned, wide, lanes, index, map_side)
        gather_windows(windows, field, start, index, poses)
        grad = block_gradient(turned, windows, pool2).reshape(BLOCK, BLOCK, map_side)
        gradient[:, planes, :] = grad
        refined[:, planes, :] = first[:, planes, :] - sizes[1] * grad


def finish(first, fields, geo, wide_geo, sizes, pool2, poses):
    row_share, depth, map_side = first.shape
    side = pool2.shape[0] // 2
    rows = pl.BlockSpec((BLOCK, depth, map_side), lambda i: (i, 0, 0))
    out = jax.ShapeDtypeStruct(first.shape, jnp.float32)
    return pl.pallas_call(
        functools.partial(finish_kernel, map_side, poses, len(fields)),
        grid=(row_share // BLOCK,),
        in_specs=[smem()] * 2 + [rows] + [vmem()] * (3 + len(fields)),
        out_specs=[rows, rows],
        out_shape=[out, out],
        scratch_shapes=[
            pltpu.VMEM((poses, side, side), jnp.float32),
            pltpu.VMEM((2, BLOCK * BLOCK, poses * WINDOW), jnp.bfloat16),
            pltpu.VMEM((2, poses * WINDOW, side), jnp.bfloat16),
        ],
        name="finish",
    )(geo[2], sizes, first, *wide_geo, pool2, *fields)


def on_device(
    density, images, image_bin, image_pose, image_class, defocus, pose_offset, step_sizes
):
    bins = lax.axis_size("bin")
    slabs = lax.axis_size("slab")
    chips = slabs // 2
    bin_index = lax.axis_index("bin")
    slab_index = lax.axis_index("slab")
    chip, core = slab_index // 2, slab_index % 2
    map_side, depth, _ = density.shape
    image_count, side, _ = images.shape
    pose_count = pose_offset.shape[1]
    classes = defocus.shape[0]
    row_share = map_side // bins
    owned = pose_count // slabs
    weight = 16.0 * pose_count / (image_count * slabs)

    def to_core(value):
        return lax.ppermute(value, "slab", [(s, s ^ 1) for s in range(slabs)])

    def to_chip(value, shift):
        return lax.ppermute(
            value, "slab", [(s, (s + 2 * shift) % slabs) for s in range(slabs)]
        )

    def to_bin(value, shift):
        return lax.ppermute(value, "bin", [(b, (b + shift) % bins) for b in range(bins)])

    where = jnp.stack([bin_index, chip, core]).astype(jnp.int32)
    picked = pick_images(
        images, where, image_bin[:, 0], image_pose, image_class, owned, chips, bins
    )
    picked, pose_offset, defocus = lax.optimization_barrier((picked, pose_offset, defocus))
    got_images = [picked[0]] + [to_bin(picked[d], d) for d in range(1, bins)]

    poses = bins * pose_count
    own_geo, geo, wide_geo = make_geometry(
        where, pose_offset, map_side, side, depth, row_share, chips, owned
    )
    pooling = pool_table(side, map_side).astype(jnp.bfloat16)
    pool_t = jnp.asarray(pooling.T)
    pool2 = jnp.asarray(np.concatenate([pooling, pooling], axis=0))
    table = hartley_table(side)
    ctf = ctf_table(defocus, side)

    def reduce_slab(keep, send):
        got = to_core(send)
        sums = [keep[d] + got[d] for d in range(chips)]
        moved = [to_chip(sums[d], d) for d in range(1, chips)]
        return [sums[0]] + moved

    def split(value):
        return value.reshape(chips, -1, *value.shape[1:])

    keep, send = first_projection(density, pool_t, own_geo, pose_count)
    proj_parts = reduce_slab(split(keep), split(send))
    keep, send, tally = image_sums(got_images, ctf, table, pose_count)
    tally = tally.reshape(2, chips, owned * classes)
    tally = functools.reduce(jnp.add, reduce_slab(tally[0], tally[1]))
    total = functools.reduce(jnp.add, reduce_slab(split(keep), split(send)))

    def share_field(field):
        near = [field] + [to_bin(field, bins - d) for d in range(1, bins)]
        near = jnp.concatenate(near, axis=0)
        row = [near] + [to_chip(near, chips - d) for d in range(1, chips)]
        return row + [to_core(part) for part in row]

    field = residual_field(proj_parts, total, tally, ctf, table, weight)
    first, keep, send = take_step(
        density, share_field(field), geo, wide_geo, step_sizes, bin_index, pool2, pool_t, poses,
        row_share,
    )
    parts = functools.reduce(jnp.add, reduce_slab(split(keep), split(send)))
    parts = parts.reshape(bins, owned, side, side)
    parts = [parts[0]] + [to_bin(parts[d], d) for d in range(1, bins)]
    field = residual_field(parts, total, tally, ctf, table, weight)
    gradient, refined = finish(first, share_field(field), geo, wide_geo, step_sizes, pool2, poses)
    return (gradient, refined)


def solution(mesh):
    return jax.shard_map(
        on_device,
        mesh=mesh,
        in_specs=(
            P("grp", "slab", None),
            P(("grp", "bin", "slab"), None, None),
            P(("grp", "bin", "slab"), None),
            P(("grp", "bin", "slab")),
            P(("grp", "bin", "slab")),
            P("grp"),
            P("grp", None),
            P(),
        ),
        out_specs=(P(("grp", "bin"), "slab", None), P(("grp", "bin"), "slab", None)),
        check_vma=False,
    )
```

```python
import functools
import math

import jax
import jax.numpy as jnp
import numpy as np
from jax import lax
from jax.experimental import pallas as pl
from jax.experimental.pallas import tpu as pltpu
from jax.sharding import PartitionSpec as P

AMP_CONTRAST = 0.1
PHASE_RATE = 60.0
BLOCK = 16
WINDOW = 16
LANES = 128
SMEM = pltpu.SMEM


def vmem():
    return pl.BlockSpec(memory_space=pltpu.VMEM)


def smem():
    return pl.BlockSpec(memory_space=SMEM)


def pool_table(image_side, map_side):
    row_index = np.arange(image_side)[:, None]
    col_index = np.arange(map_side)[None, :]
    return 0.5 * np.maximum(0.0, 1.0 - np.abs(col_index - 2.0 * row_index - 0.5) / 2.0)


def hartley_table(image_side):
    index_row = np.arange(image_side)
    phase_index = index_row[:, None] * index_row[None, :] % image_side
    angle_table = 2.0 * math.pi / image_side * phase_index
    table = (np.cos(angle_table) + np.sin(angle_table)) / math.sqrt(image_side)
    high = table.astype(jnp.bfloat16)
    low = (table - high.astype(np.float64)).astype(jnp.bfloat16)
    return jnp.asarray(np.concatenate([high, low], axis=1))


def ctf_table(defocus, image_side):
    index_row = jnp.arange(image_side, dtype=jnp.int32)
    frequency = (
        jnp.where(index_row < image_side // 2, index_row, index_row - image_side).astype(
            jnp.float32
        )
        / image_side
    )
    part = PHASE_RATE * defocus[:, None] * (frequency * frequency)[None, :]
    shifted = part + math.asin(AMP_CONTRAST)
    return -(
        jnp.sin(shifted)[:, :, None] * jnp.cos(part)[:, None, :]
        + jnp.cos(shifted)[:, :, None] * jnp.sin(part)[:, None, :]
    )


def block_lines(theta, y_low, z_low, side, map_side):
    middle = map_side / 2.0
    scale = 0.25 / math.sqrt(map_side)
    cosine, sine = jnp.cos(theta), jnp.sin(theta)
    y_part = (y_low.astype(jnp.float32) + (0.5 - middle)) * cosine
    z_part = (z_low.astype(jnp.float32) + (0.5 - middle)) * sine
    least = (
        y_part
        + jnp.minimum(0.0, (BLOCK - 1.0) * cosine)
        + z_part
        + jnp.minimum(0.0, (BLOCK - 1.0) * sine)
    )
    column = jnp.floor((least + (middle - 3.0)) * 0.5).astype(jnp.int32)
    start = jnp.clip(column, 0, side - WINDOW)
    offset = scale * (y_part + z_part - (2.0 * start.astype(jnp.float32) + (1.0 - middle)))
    return cosine * scale, sine * scale, start, offset


def geometry_kernel(
    sizes, where, offsets, own_cos, own_sin, own_start, own_offset, cosine, sine, start, offset,
    wide, lanes
):
    map_side, side, depth, row_share, bins, chips, owned = sizes
    here, chip, core = where[0], where[1], where[2]
    first_plane = (chip * 2 + core) * depth
    plane_blocks = depth // BLOCK

    def turn(away, place):
        across, ahead, beyond = away
        bin_at = lax.rem(here + beyond, bins)
        owner = lax.rem(chip + ahead, chips) * 2 + lax.rem(core + across, 2)
        return bin_at.astype(jnp.float32) + offsets[bin_at, owner * owned + place]

    def listed(beyonds):
        return [
            turn((across, ahead, beyond), place)
            for across in range(2)
            for ahead in range(chips)
            for beyond in range(beyonds)
            for place in range(owned)
        ]

    def spread(values, index, shape):
        theta = jnp.zeros(shape, jnp.float32)
        for k, value in enumerate(values):
            theta = jnp.where(index == k, value, theta)
        return math.pi * theta / bins

    def fill(outs, values, first_row):
        shape = outs[0].shape
        row = lax.broadcasted_iota(jnp.int32, shape, 0)
        block = lax.broadcasted_iota(jnp.int32, shape, 1)
        theta = spread(values, row, shape)
        found = block_lines(
            theta,
            first_row + block // plane_blocks * BLOCK,
            first_plane + block % plane_blocks * BLOCK,
            side,
            map_side,
        )
        for out, value in zip(outs, found):
            out[...] = value

    first_row = here * row_share
    values = listed(bins)
    fill((own_cos, own_sin, own_start, own_offset), listed(1), 0)
    fill((cosine, sine, start, offset), values, first_row)
    shape = lanes.shape
    block = lax.broadcasted_iota(jnp.int32, shape, 0)
    lane = lax.broadcasted_iota(jnp.int32, shape, 1)
    along_y, along_z, _, offset_wide = block_lines(
        spread(values, lane // WINDOW, shape),
        first_row + block // plane_blocks * BLOCK,
        first_plane + block % plane_blocks * BLOCK,
        side,
        map_side,
    )
    peak = 0.5 / math.sqrt(map_side)
    lanes[...] = offset_wide - peak * (lane % WINDOW).astype(jnp.float32)
    wide[0:1, :] = along_y[0:1]
    wide[1:2, :] = along_z[0:1]


def make_geometry(where, pose_offset, map_side, side, depth, row_share, chips, owned):
    bins, pose_count = pose_offset.shape
    poses = bins * pose_count

    def tables(count, blocks):
        shape = (count, -(-blocks // LANES) * LANES)
        return [jax.ShapeDtypeStruct(shape, t) for t in (jnp.float32,) * 2] + [
            jax.ShapeDtypeStruct(shape, jnp.int32),
            jax.ShapeDtypeStruct(shape, jnp.float32),
        ]

    plane_blocks = depth // BLOCK
    blocks = row_share // BLOCK * plane_blocks
    shapes = (
        tables(pose_count, map_side // BLOCK * plane_blocks)
        + tables(poses, blocks)
        + [
            jax.ShapeDtypeStruct((2, poses * WINDOW), jnp.float32),
            jax.ShapeDtypeStruct((blocks, poses * WINDOW), jnp.float32),
        ]
    )
    sizes = (map_side, side, depth, row_share, bins, chips, owned)
    out = pl.pallas_call(
        functools.partial(geometry_kernel, sizes),
        in_specs=[smem(), smem()],
        out_specs=[vmem()] * len(shapes),
        out_shape=shapes,
        name="geometry",
    )(where, pose_offset)
    return out[:4], out[4:8], out[8:]


def fill_windows(w_ref, geo, block, poses, map_side):
    lane = lax.broadcasted_iota(jnp.int32, (8, BLOCK * BLOCK), 1)
    row = lax.broadcasted_iota(jnp.int32, (8, BLOCK * BLOCK), 0).astype(jnp.float32)
    y_local = (lane // BLOCK).astype(jnp.float32)
    z_local = (lane % BLOCK).astype(jnp.float32)
    peak = 0.5 / math.sqrt(map_side)
    rows = [peak * (row + 8.0 * k) for k in range(WINDOW // 8)]
    cosine, sine, _, offset = geo
    for pose in range(poses):
        line = y_local * cosine[pose, 0] + z_local * sine[pose, 0] + offset[pose, block]
        parts = [jnp.maximum(0.0, peak - jnp.abs(line - r)) for r in rows]
        w_ref[pose * WINDOW : (pose + 1) * WINDOW, :] = jnp.concatenate(parts, axis=0).astype(
            jnp.bfloat16
        )


def fill_turned(t_ref, wide, lanes, block, map_side):
    peak = 0.5 / math.sqrt(map_side)
    local = lax.broadcasted_iota(jnp.int32, (BLOCK, LANES), 0).astype(jnp.float32)
    offset = lanes[pl.ds(block, 1), :]
    for at in range(0, wide.shape[1], LANES):
        span = slice(at, at + LANES)
        along_z = local * wide[1:2, span] + offset[:, span]
        along_y = wide[0:1, span]
        for y in range(BLOCK):
            line = along_z + float(y) * along_y
            t_ref[y * BLOCK : (y + 1) * BLOCK, span] = jnp.maximum(
                0.0, peak - jnp.abs(line)
            ).astype(jnp.bfloat16)


def add_projection(outs, prod, start, block, poses):
    share = poses // len(outs)
    for pose in range(poses):
        rows = pl.ds(start[pose, block], WINDOW)
        outs[pose // share][pose % share, rows, :] += prod[pose * WINDOW : (pose + 1) * WINDOW]


def first_projection_kernel(
    map_side, poses, cosine, sine, start, offset, dens, pool_t, keep, send, fold_ref, w_ref
):
    step = pl.program_id(0)
    geo = (cosine, sine, start, offset)

    @pl.when(step == 0)
    def _():
        keep[...] = jnp.zeros_like(keep)
        send[...] = jnp.zeros_like(send)

    height, depth, _ = dens.shape
    side = pool_t.shape[1]
    folded = jnp.dot(
        dens[...].reshape(height * depth, map_side), pool_t[...], preferred_element_type=jnp.float32
    )
    fold_ref[...] = folded.astype(jnp.bfloat16).reshape(height, depth, side)
    count = height * depth // (BLOCK * BLOCK)
    for k in range(count):
        row, plane = k // (depth // BLOCK) * BLOCK, k % (depth // BLOCK) * BLOCK
        weights = w_ref.at[k % 2]
        fill_windows(weights, geo, step * count + k, poses, map_side)
        pixels = fold_ref[row : row + BLOCK, plane : plane + BLOCK, :].reshape(-1, side)
        prod = jnp.dot(weights[...], pixels, preferred_element_type=jnp.float32)
        add_projection((keep, send), prod, start, step * count + k, poses)


def first_projection(density, pool_t, geo, poses):
    map_side, depth, _ = density.shape
    side = pool_t.shape[1]
    height = 2 * BLOCK
    half = jax.ShapeDtypeStruct((poses // 2, side, side), jnp.float32)
    return pl.pallas_call(
        functools.partial(first_projection_kernel, map_side, poses),
        grid=(map_side // height,),
        in_specs=[smem(), smem(), smem(), smem(),
                  pl.BlockSpec((height, depth, map_side), lambda i: (i, 0, 0)),
                  vmem()],
        out_specs=[vmem(), vmem()],
        out_shape=[half, half],
        scratch_shapes=[
            pltpu.VMEM((height, depth, side), jnp.bfloat16),
            pltpu.VMEM((2, poses * WINDOW, BLOCK * BLOCK), jnp.bfloat16),
        ],
        name="first_projection",
    )(*geo, density, pool_t)


def pick_kernel(owned, chips, where, bins_of, poses_of, classes_of, images, *refs):
    outs, order = refs[:-1], refs[-1]
    groups = len(outs)
    each = outs[0].shape[0]
    side = images.shape[1]
    lane = lax.broadcasted_iota(jnp.int32, (BLOCK, side), 1)
    here, chip, core = where[0], where[1], where[2]
    for slot in range(groups * each):
        order[slot] = -1

    def place(n, _):
        away = lax.rem(bins_of[n] - here + groups, groups) * each

        def taken(k, rank):
            same = lax.rem(bins_of[k] - here + groups, groups) * each == away
            return rank + jnp.where(same, 1, 0)

        order[away + lax.fori_loop(0, n, taken, 0)] = n
        return 0

    lax.fori_loop(0, images.shape[0], place, 0)
    for group in range(groups):
        for k in range(each):
            source = order[group * each + k]
            image = jnp.maximum(source, 0)
            outs[group][k, 0:side, :] = images[image]
            pose = poses_of[image]
            owner = pose // owned
            ahead = lax.rem(owner // 2 - chip + chips, chips)
            across = lax.rem(lax.rem(owner, 2) + core, 2)
            at = (across * chips + ahead) * owned + lax.rem(pose, owned)
            at = jnp.where(source >= 0, at, -1).astype(jnp.float32)
            named = classes_of[image].astype(jnp.float32)
            outs[group][k, side : side + BLOCK, :] = jnp.where(
                lane == 0, at, jnp.where(lane == 1, named, 0.0)
            ).astype(images.dtype)


def pick_images(images, where, image_bin, image_pose, image_class, owned, chips, groups):
    count, side, _ = images.shape
    each = count // 4
    out = jax.ShapeDtypeStruct((each, side + BLOCK, side), images.dtype)
    return pl.pallas_call(
        functools.partial(pick_kernel, owned, chips),
        in_specs=[smem()] * 4 + [vmem()],
        out_specs=[vmem()] * groups,
        out_shape=[out] * groups,
        scratch_shapes=[pltpu.SMEM((groups * each,), jnp.int32)],
        name="pick_images",
    )(where, image_bin, image_pose, image_class, images)


def times_hartley(value, table):
    count, side = value.shape
    high = value.astype(jnp.bfloat16)
    low = (value - high.astype(jnp.float32)).astype(jnp.bfloat16)
    both = jnp.dot(high, table, preferred_element_type=jnp.float32)
    rest = jnp.dot(low, table[:, :side], preferred_element_type=jnp.float32)
    return both[:, :side] + (both[:, side:] + rest)


def spectrum_kernel(groups, each, ctf, table, *refs):
    images, (keep, send, tally, marks, label, sem) = refs[:groups], refs[groups:]
    half = keep.shape[0]
    side = keep.shape[1]
    classes = ctf.shape[0]
    for group in range(groups):
        for k in range(each):
            at = group * each + k
            row = images[group][k, side : side + BLOCK, :].astype(jnp.float32)
            marks[at : at + 1, :] = row[0:1].astype(jnp.int32)
    copy = pltpu.make_async_copy(marks, label, sem)
    copy.start()
    keep[...] = jnp.zeros_like(keep)
    send[...] = jnp.zeros_like(send)
    for k in range(tally.shape[0]):
        tally[k] = 0.0
    hart = table[...]
    copy.wait()
    for group in range(groups):
        pixels = images[group][:, 0:side, :].reshape(each * side, side)
        both = jnp.dot(pixels, hart, preferred_element_type=jnp.float32)
        along = (both[:, :side] + both[:, side:]).reshape(each, side, side)
        turned = jnp.concatenate([along[k].T for k in range(each)], axis=0)
        full = times_hartley(turned, hart).reshape(each, side, side)
        for k in range(each):
            pose, kind = label[group * each + k, 0], label[group * each + k, 1]
            value = ctf[kind] * full[k]

            @pl.when(pose >= 0)
            def _(pose=pose, kind=kind):
                tally[pose * classes + kind] += 1.0

            @pl.when(jnp.logical_and(pose >= 0, pose < half))
            def _(pose=pose, value=value):
                keep[pose] += value

            @pl.when(pose >= half)
            def _(pose=pose, value=value):
                send[pose - half] += value

    for out in (keep, send):
        for pose in range(half):
            out[pose] = out[pose].T


def image_sums(images, ctf, table, poses):
    each, _, side = images[0].shape
    slots = each * len(images)
    half = jax.ShapeDtypeStruct((poses // 2, side, side), jnp.float32)
    return pl.pallas_call(
        functools.partial(spectrum_kernel, len(images), each),
        in_specs=[vmem(), vmem()] + [vmem()] * len(images),
        out_specs=[vmem(), vmem(), smem()],
        out_shape=[half, half, jax.ShapeDtypeStruct((poses * ctf.shape[0],), jnp.float32)],
        scratch_shapes=[
            pltpu.VMEM((slots, side), jnp.int32),
            pltpu.SMEM((slots, side), jnp.int32),
            pltpu.SemaphoreType.DMA(()),
        ],
        name="image_sums",
    )(ctf, table, *images)


def filter_kernel(weight, count, tally, ctf, table, *refs):
    proj, totals, out = refs[:count], refs[count:-1], refs[-1]
    owned, side, _ = out.shape
    classes = ctf.shape[0]
    hart = table[...]
    value, total = (
        functools.reduce(jnp.add, [part[...].astype(jnp.float32) for part in parts])
        for parts in (proj, totals)
    )
    along = times_hartley(value.reshape(owned * side, side), hart)
    turned = jnp.concatenate([along[k * side : (k + 1) * side].T for k in range(owned)], axis=0)
    full = times_hartley(turned, hart)
    parts = []
    for k in range(owned):
        gain = jnp.zeros((side, side), jnp.float32)
        for c in range(classes):
            gain = gain + tally[k * classes + c] * (ctf[c] * ctf[c])
        parts.append(weight * (gain * full[k * side : (k + 1) * side] - total[k]))
    along = times_hartley(jnp.concatenate(parts, axis=0), hart)
    turned = jnp.concatenate([along[k * side : (k + 1) * side].T for k in range(owned)], axis=0)
    field = times_hartley(turned, hart)
    out[...] = field.reshape(owned, side, side).astype(out.dtype)


def residual_field(parts, totals, tally, ctf, table, weight):
    owned, side, _ = totals[0].shape
    return pl.pallas_call(
        functools.partial(filter_kernel, weight, len(parts)),
        in_specs=[smem(), vmem(), vmem()] + [vmem()] * (len(parts) + len(totals)),
        out_specs=vmem(),
        out_shape=jax.ShapeDtypeStruct((owned, side, side), jnp.bfloat16),
        name="residual_field",
    )(tally, ctf, table, *parts, *totals)


def load_fields(field, fields):
    at = 0
    for part in fields:
        count = part.shape[0]
        field[at : at + count] = part[...].astype(jnp.float32)
        at += count


def gather_windows(f_ref, field, start, block, poses):
    for pose in range(poses):
        f_ref[pose * WINDOW : (pose + 1) * WINDOW, :] = field[
            pose, pl.ds(start[pose, block], WINDOW), :
        ].astype(jnp.bfloat16)


def block_gradient(t_ref, f_ref, pool2):
    back = jnp.dot(t_ref[...], f_ref[...], preferred_element_type=jnp.float32)
    high = back.astype(jnp.bfloat16)
    low = (back - high.astype(jnp.float32)).astype(jnp.bfloat16)
    return jnp.dot(
        jnp.concatenate([high, low], axis=1), pool2[...], preferred_element_type=jnp.float32
    )


def step_kernel(
    map_side, poses, parts, bin_ref, cosine, sine, start, offset, sizes, dens, wide, lanes, pool2,
    pool_t, *refs
):
    geo = (cosine, sine, start, offset)
    fields = refs[:parts]
    first, keep, send, field, t_ref, w_ref, f_ref = refs[parts:]
    step = pl.program_id(0)

    @pl.when(step == 0)
    def _():
        keep[...] = jnp.zeros_like(keep)
        send[...] = jnp.zeros_like(send)
        load_fields(field, fields)

    def fold(values):
        folded = jnp.dot(values, pool_t[...], preferred_element_type=jnp.float32)
        return folded.astype(jnp.bfloat16).astype(jnp.float32)

    count = dens.shape[1] // BLOCK
    for k in range(count):
        planes = slice(k * BLOCK, (k + 1) * BLOCK)
        index = step * count + k
        turned, weights, windows = t_ref.at[k % 2], w_ref.at[k % 2], f_ref.at[k % 2]
        fill_turned(turned, wide, lanes, index, map_side)
        gather_windows(windows, field, start, index, poses)
        grad = block_gradient(turned, windows, pool2)
        kept = dens[:, planes, :].reshape(BLOCK * BLOCK, map_side)
        moved = kept.astype(jnp.float32) - sizes[0] * grad
        first[:, planes, :] = moved.reshape(BLOCK, BLOCK, map_side)
        change = fold(moved.astype(jnp.bfloat16)) - fold(kept)
        high = change.astype(jnp.bfloat16)
        low = (change - high.astype(jnp.float32)).astype(jnp.bfloat16)
        fill_windows(weights, geo, index, poses, map_side)
        prod = jnp.dot(
            weights[...],
            jnp.concatenate([high, low], axis=1),
            preferred_element_type=jnp.float32,
        )
        side = high.shape[1]
        add_projection((keep, send), prod[:, :side] + prod[:, side:], start, index, poses)


def take_step(density, fields, geo, wide_geo, sizes, bin_index, pool2, pool_t, poses, row_share):
    map_side, depth, _ = density.shape
    side = pool_t.shape[1]
    half = jax.ShapeDtypeStruct((poses // 2, side, side), jnp.float32)
    row_blocks = row_share // BLOCK
    rows = (BLOCK, depth, map_side)
    return pl.pallas_call(
        functools.partial(step_kernel, map_side, poses, len(fields)),
        grid_spec=pltpu.PrefetchScalarGridSpec(
            num_scalar_prefetch=1,
            grid=(row_blocks,),
            in_specs=[smem()] * 5
            + [pl.BlockSpec(rows, lambda i, at: (at[0] * row_blocks + i, 0, 0))]
            + [vmem()] * (4 + len(fields)),
            out_specs=[pl.BlockSpec(rows, lambda i, at: (i, 0, 0)), vmem(), vmem()],
            scratch_shapes=[
                pltpu.VMEM((poses, side, side), jnp.float32),
                pltpu.VMEM((2, BLOCK * BLOCK, poses * WINDOW), jnp.bfloat16),
                pltpu.VMEM((2, poses * WINDOW, BLOCK * BLOCK), jnp.bfloat16),
                pltpu.VMEM((2, poses * WINDOW, side), jnp.bfloat16),
            ],
        ),
        out_shape=[jax.ShapeDtypeStruct((row_share, depth, map_side), jnp.float32), half, half],
        name="take_step",
    )(bin_index.reshape(1), *geo, sizes, density, *wide_geo, pool2, pool_t, *fields)


def finish_kernel(map_side, poses, parts, start, sizes, first, wide, lanes, pool2, *refs):
    fields = refs[:parts]
    gradient, refined, field, t_ref, f_ref = refs[parts:]
    step = pl.program_id(0)

    @pl.when(step == 0)
    def _():
        load_fields(field, fields)

    count = first.shape[1] // BLOCK
    for k in range(count):
        planes = slice(k * BLOCK, (k + 1) * BLOCK)
        index = step * count + k
        turned, windows = t_ref.at[k % 2], f_ref.at[k % 2]
        fill_turned(turned, wide, lanes, index, map_side)
        gather_windows(windows, field, start, index, poses)
        grad = block_gradient(turned, windows, pool2).reshape(BLOCK, BLOCK, map_side)
        gradient[:, planes, :] = grad
        refined[:, planes, :] = first[:, planes, :] - sizes[1] * grad


def finish(first, fields, geo, wide_geo, sizes, pool2, poses):
    row_share, depth, map_side = first.shape
    side = pool2.shape[0] // 2
    rows = pl.BlockSpec((BLOCK, depth, map_side), lambda i: (i, 0, 0))
    out = jax.ShapeDtypeStruct(first.shape, jnp.float32)
    return pl.pallas_call(
        functools.partial(finish_kernel, map_side, poses, len(fields)),
        grid=(row_share // BLOCK,),
        in_specs=[smem()] * 2 + [rows] + [vmem()] * (3 + len(fields)),
        out_specs=[rows, rows],
        out_shape=[out, out],
        scratch_shapes=[
            pltpu.VMEM((poses, side, side), jnp.float32),
            pltpu.VMEM((2, BLOCK * BLOCK, poses * WINDOW), jnp.bfloat16),
            pltpu.VMEM((2, poses * WINDOW, side), jnp.bfloat16),
        ],
        name="finish",
    )(geo[2], sizes, first, *wide_geo, pool2, *fields)


def on_device(
    density, images, image_bin, image_pose, image_class, defocus, pose_offset, step_sizes
):
    bins = lax.axis_size("bin")
    slabs = lax.axis_size("slab")
    chips = slabs // 2
    bin_index = lax.axis_index("bin")
    slab_index = lax.axis_index("slab")
    chip, core = slab_index // 2, slab_index % 2
    map_side, depth, _ = density.shape
    image_count, side, _ = images.shape
    pose_count = pose_offset.shape[1]
    classes = defocus.shape[0]
    row_share = map_side // bins
    owned = pose_count // slabs
    weight = 16.0 * pose_count / (image_count * slabs)

    def to_core(value):
        return lax.ppermute(value, "slab", [(s, s ^ 1) for s in range(slabs)])

    def to_chip(value, shift):
        return lax.ppermute(
            value, "slab", [(s, (s + 2 * shift) % slabs) for s in range(slabs)]
        )

    def to_bin(value, shift):
        return lax.ppermute(value, "bin", [(b, (b + shift) % bins) for b in range(bins)])

    where = jnp.stack([bin_index, chip, core]).astype(jnp.int32)
    picked = pick_images(
        images, where, image_bin[:, 0], image_pose, image_class, owned, chips, bins
    )
    picked, pose_offset, defocus = lax.optimization_barrier((picked, pose_offset, defocus))
    got_images = [picked[0]] + [to_bin(picked[d], d) for d in range(1, bins)]

    poses = bins * pose_count
    own_geo, geo, wide_geo = make_geometry(
        where, pose_offset, map_side, side, depth, row_share, chips, owned
    )
    pooling = pool_table(side, map_side).astype(jnp.bfloat16)
    pool_t = jnp.asarray(pooling.T)
    pool2 = jnp.asarray(np.concatenate([pooling, pooling], axis=0))
    table = hartley_table(side)
    ctf = ctf_table(defocus, side)

    def reduce_slab(keep, send, sent_as=jnp.float32):
        got = to_core(send)
        moved = [to_chip((keep[d] + got[d]).astype(sent_as), d) for d in range(1, chips)]
        return [keep[0] + got[0]] + moved

    def added(parts):
        return functools.reduce(jnp.add, [part.astype(jnp.float32) for part in parts])

    def split(value):
        return value.reshape(chips, -1, *value.shape[1:])

    keep, send = first_projection(density, pool_t, own_geo, pose_count)
    keep, send, ctf = lax.optimization_barrier((keep, send, ctf))
    proj_parts = reduce_slab(split(keep), split(send))
    keep, send, tally = image_sums(got_images, ctf, table, pose_count)
    tally = tally.reshape(2, chips, owned * classes)
    tally = added(reduce_slab(tally[0], tally[1]))
    totals = reduce_slab(split(keep), split(send))

    def share_field(field):
        near = [field] + [to_bin(field, bins - d) for d in range(1, bins)]
        near = jnp.concatenate(near, axis=0)
        row = [near] + [to_chip(near, chips - d) for d in range(1, chips)]
        return row + [to_core(part) for part in row]

    field = residual_field(proj_parts, totals, tally, ctf, table, weight)
    first, keep, send = take_step(
        density, share_field(field), geo, wide_geo, step_sizes, bin_index, pool2, pool_t, poses,
        row_share,
    )
    change = added(reduce_slab(split(keep), split(send), jnp.bfloat16))
    change = change.reshape(bins, owned, side, side)
    moved = [to_bin(change[d].astype(jnp.bfloat16), d) for d in range(1, bins)]
    parts = proj_parts + [change[0]] + moved
    field = residual_field(parts, totals, tally, ctf, table, weight)
    gradient, refined = finish(first, share_field(field), geo, wide_geo, step_sizes, pool2, poses)
    return (gradient, refined)


def solution(mesh):
    return jax.shard_map(
        on_device,
        mesh=mesh,
        in_specs=(
            P("grp", "slab", None),
            P(("grp", "bin", "slab"), None, None),
            P(("grp", "bin", "slab"), None),
            P(("grp", "bin", "slab")),
            P(("grp", "bin", "slab")),
            P("grp"),
            P("grp", None),
            P(),
        ),
        out_specs=(P(("grp", "bin"), "slab", None), P(("grp", "bin"), "slab", None)),
        check_vma=False,
    )
```

```python
import functools
import math

import jax
import jax.numpy as jnp
import numpy as np
from jax import lax
from jax.experimental import pallas as pl
from jax.experimental.pallas import tpu as pltpu
from jax.sharding import PartitionSpec as P

AMP_CONTRAST = 0.1
PHASE_RATE = 60.0
BLOCK = 16
WINDOW = 16
LANES = 128
SMEM = pltpu.SMEM


def vmem():
    return pl.BlockSpec(memory_space=pltpu.VMEM)


def smem():
    return pl.BlockSpec(memory_space=SMEM)


def pool_table(image_side, map_side):
    row_index = np.arange(image_side)[:, None]
    col_index = np.arange(map_side)[None, :]
    return 0.5 * np.maximum(0.0, 1.0 - np.abs(col_index - 2.0 * row_index - 0.5) / 2.0)


def hartley_table(image_side):
    index_row = np.arange(image_side)
    phase_index = index_row[:, None] * index_row[None, :] % image_side
    angle_table = 2.0 * math.pi / image_side * phase_index
    table = (np.cos(angle_table) + np.sin(angle_table)) / math.sqrt(image_side)
    high = table.astype(jnp.bfloat16)
    low = (table - high.astype(np.float64)).astype(jnp.bfloat16)
    return jnp.asarray(np.concatenate([high, low], axis=1))


def ctf_table(defocus, image_side):
    index_row = jnp.arange(image_side, dtype=jnp.int32)
    frequency = (
        jnp.where(index_row < image_side // 2, index_row, index_row - image_side).astype(
            jnp.float32
        )
        / image_side
    )
    part = PHASE_RATE * defocus[:, None] * (frequency * frequency)[None, :]
    shifted = part + math.asin(AMP_CONTRAST)
    return -(
        jnp.sin(shifted)[:, :, None] * jnp.cos(part)[:, None, :]
        + jnp.cos(shifted)[:, :, None] * jnp.sin(part)[:, None, :]
    )


def block_lines(theta, y_low, z_low, side, map_side):
    middle = map_side / 2.0
    scale = 0.25 / math.sqrt(map_side)
    cosine, sine = jnp.cos(theta), jnp.sin(theta)
    y_part = (y_low.astype(jnp.float32) + (0.5 - middle)) * cosine
    z_part = (z_low.astype(jnp.float32) + (0.5 - middle)) * sine
    least = (
        y_part
        + jnp.minimum(0.0, (BLOCK - 1.0) * cosine)
        + z_part
        + jnp.minimum(0.0, (BLOCK - 1.0) * sine)
    )
    column = jnp.floor((least + (middle - 3.0)) * 0.5).astype(jnp.int32)
    start = jnp.clip(column, 0, side - WINDOW)
    offset = scale * (y_part + z_part - (2.0 * start.astype(jnp.float32) + (1.0 - middle)))
    return cosine * scale, sine * scale, start, offset


def geometry_kernel(
    sizes, where, offsets, own_cos, own_sin, own_start, own_offset, cosine, sine, start, offset,
    wide, lanes
):
    map_side, side, depth, row_share, bins, chips, owned = sizes
    here, chip, core = where[0], where[1], where[2]
    first_plane = (chip * 2 + core) * depth
    plane_blocks = depth // BLOCK

    def turn(away, place):
        across, ahead, beyond = away
        bin_at = lax.rem(here + beyond, bins)
        owner = lax.rem(chip + ahead, chips) * 2 + lax.rem(core + across, 2)
        return bin_at.astype(jnp.float32) + offsets[bin_at, owner * owned + place]

    def listed(beyonds):
        return [
            turn((across, ahead, beyond), place)
            for across in range(2)
            for ahead in range(chips)
            for beyond in range(beyonds)
            for place in range(owned)
        ]

    def spread(values, index, shape):
        theta = jnp.zeros(shape, jnp.float32)
        for k, value in enumerate(values):
            theta = jnp.where(index == k, value, theta)
        return math.pi * theta / bins

    def fill(outs, values, first_row):
        shape = outs[0].shape
        row = lax.broadcasted_iota(jnp.int32, shape, 0)
        block = lax.broadcasted_iota(jnp.int32, shape, 1)
        theta = spread(values, row, shape)
        found = block_lines(
            theta,
            first_row + block // plane_blocks * BLOCK,
            first_plane + block % plane_blocks * BLOCK,
            side,
            map_side,
        )
        for out, value in zip(outs, found):
            out[...] = value

    first_row = here * row_share
    values = listed(bins)
    fill((own_cos, own_sin, own_start, own_offset), listed(1), 0)
    fill((cosine, sine, start, offset), values, first_row)
    shape = lanes.shape
    block = lax.broadcasted_iota(jnp.int32, shape, 0)
    lane = lax.broadcasted_iota(jnp.int32, shape, 1)
    along_y, along_z, _, offset_wide = block_lines(
        spread(values, lane // WINDOW, shape),
        first_row + block // plane_blocks * BLOCK,
        first_plane + block % plane_blocks * BLOCK,
        side,
        map_side,
    )
    peak = 0.5 / math.sqrt(map_side)
    lanes[...] = offset_wide - peak * (lane % WINDOW).astype(jnp.float32)
    wide[0:1, :] = along_y[0:1]
    wide[1:2, :] = along_z[0:1]


def make_geometry(where, pose_offset, map_side, side, depth, row_share, chips, owned):
    bins, pose_count = pose_offset.shape
    poses = bins * pose_count

    def tables(count, blocks):
        shape = (count, -(-blocks // LANES) * LANES)
        return [jax.ShapeDtypeStruct(shape, t) for t in (jnp.float32,) * 2] + [
            jax.ShapeDtypeStruct(shape, jnp.int32),
            jax.ShapeDtypeStruct(shape, jnp.float32),
        ]

    plane_blocks = depth // BLOCK
    blocks = row_share // BLOCK * plane_blocks
    shapes = (
        tables(pose_count, map_side // BLOCK * plane_blocks)
        + tables(poses, blocks)
        + [
            jax.ShapeDtypeStruct((2, poses * WINDOW), jnp.float32),
            jax.ShapeDtypeStruct((blocks, poses * WINDOW), jnp.float32),
        ]
    )
    sizes = (map_side, side, depth, row_share, bins, chips, owned)
    out = pl.pallas_call(
        functools.partial(geometry_kernel, sizes),
        in_specs=[smem(), smem()],
        out_specs=[vmem()] * len(shapes),
        out_shape=shapes,
        name="geometry",
    )(where, pose_offset)
    return out[:4], out[4:8], out[8:]


def fill_windows(w_ref, geo, block, poses, map_side):
    lane = lax.broadcasted_iota(jnp.int32, (8, BLOCK * BLOCK), 1)
    row = lax.broadcasted_iota(jnp.int32, (8, BLOCK * BLOCK), 0).astype(jnp.float32)
    y_local = (lane // BLOCK).astype(jnp.float32)
    z_local = (lane % BLOCK).astype(jnp.float32)
    peak = 0.5 / math.sqrt(map_side)
    rows = [peak * (row + 8.0 * k) for k in range(WINDOW // 8)]
    cosine, sine, _, offset = geo
    for pose in range(poses):
        line = y_local * cosine[pose, 0] + z_local * sine[pose, 0] + offset[pose, block]
        parts = [jnp.maximum(0.0, peak - jnp.abs(line - r)) for r in rows]
        w_ref[pose * WINDOW : (pose + 1) * WINDOW, :] = jnp.concatenate(parts, axis=0).astype(
            jnp.bfloat16
        )


def fill_turned(t_ref, wide, lanes, block, map_side):
    peak = 0.5 / math.sqrt(map_side)
    local = lax.broadcasted_iota(jnp.int32, (BLOCK, LANES), 0).astype(jnp.float32)
    offset = lanes[pl.ds(block, 1), :]
    for at in range(0, wide.shape[1], LANES):
        span = slice(at, at + LANES)
        along_z = local * wide[1:2, span] + offset[:, span]
        along_y = wide[0:1, span]
        for y in range(BLOCK):
            line = along_z + float(y) * along_y
            t_ref[y * BLOCK : (y + 1) * BLOCK, span] = jnp.maximum(
                0.0, peak - jnp.abs(line)
            ).astype(jnp.bfloat16)


def windows_kernel(poses, map_side, cosine, sine, start, offset, windows):
    count = windows.shape[0]
    for k in range(count):
        index = pl.program_id(0) * count + k
        fill_windows(windows.at[k], (cosine, sine, start, offset), index, poses, map_side)


def turned_kernel(map_side, wide, lanes, turned):
    count = turned.shape[0]
    for k in range(count):
        index = pl.program_id(0) * count + k
        fill_turned(turned.at[k], wide, lanes, index, map_side)


def table_call(kernel, name, blocks, shape, operands, specs):
    count = math.gcd(blocks, 4)
    return pl.pallas_call(
        kernel,
        grid=(blocks // count,),
        in_specs=specs,
        out_specs=pl.BlockSpec((count, *shape), lambda i: (i, 0, 0)),
        out_shape=jax.ShapeDtypeStruct((blocks, *shape), jnp.bfloat16),
        name=name,
    )(*operands)


def window_table(geo, blocks, poses, map_side):
    return table_call(
        functools.partial(windows_kernel, poses, map_side), "window_table", blocks,
        (poses * WINDOW, BLOCK * BLOCK), geo, [smem()] * 4,
    )


def turned_table(wide_geo, blocks, poses, map_side):
    return table_call(
        functools.partial(turned_kernel, map_side), "turned_table", blocks,
        (BLOCK * BLOCK, poses * WINDOW), wide_geo, [vmem()] * 2,
    )


def add_projection(outs, prod, start, block, poses):
    share = poses // len(outs)
    for pose in range(poses):
        rows = pl.ds(start[pose, block], WINDOW)
        outs[pose // share][pose % share, rows, :] += prod[pose * WINDOW : (pose + 1) * WINDOW]


def first_projection_kernel(
    map_side, poses, cosine, sine, start, offset, dens, pool_t, keep, send, fold_ref, w_ref
):
    step = pl.program_id(0)
    geo = (cosine, sine, start, offset)

    @pl.when(step == 0)
    def _():
        keep[...] = jnp.zeros_like(keep)
        send[...] = jnp.zeros_like(send)

    height, depth, _ = dens.shape
    side = pool_t.shape[1]
    folded = jnp.dot(
        dens[...].reshape(height * depth, map_side), pool_t[...], preferred_element_type=jnp.float32
    )
    fold_ref[...] = folded.astype(jnp.bfloat16).reshape(height, depth, side)
    count = height * depth // (BLOCK * BLOCK)
    for k in range(count):
        row, plane = k // (depth // BLOCK) * BLOCK, k % (depth // BLOCK) * BLOCK
        weights = w_ref.at[k]
        fill_windows(weights, geo, step * count + k, poses, map_side)
        pixels = fold_ref[row : row + BLOCK, plane : plane + BLOCK, :].reshape(-1, side)
        prod = jnp.dot(weights[...], pixels, preferred_element_type=jnp.float32)
        add_projection((keep, send), prod, start, step * count + k, poses)


def first_projection(density, pool_t, geo, poses):
    map_side, depth, _ = density.shape
    side = pool_t.shape[1]
    height = 2 * BLOCK
    half = jax.ShapeDtypeStruct((poses // 2, side, side), jnp.float32)
    return pl.pallas_call(
        functools.partial(first_projection_kernel, map_side, poses),
        grid=(map_side // height,),
        in_specs=[smem(), smem(), smem(), smem(),
                  pl.BlockSpec((height, depth, map_side), lambda i: (i, 0, 0)),
                  vmem()],
        out_specs=[vmem(), vmem(), pl.BlockSpec((height, depth, side), lambda i: (i, 0, 0))],
        out_shape=[half, half, jax.ShapeDtypeStruct((map_side, depth, side), jnp.bfloat16)],
        scratch_shapes=[
            pltpu.VMEM(
                (height * depth // BLOCK**2, poses * WINDOW, BLOCK * BLOCK), jnp.bfloat16
            ),
        ],
        name="first_projection",
    )(*geo, density, pool_t)


def pick_kernel(owned, chips, where, bins_of, poses_of, classes_of, images, *refs):
    outs, order = refs[:-1], refs[-1]
    groups = len(outs)
    each = outs[0].shape[0]
    side = images.shape[1]
    lane = lax.broadcasted_iota(jnp.int32, (BLOCK, side), 1)
    here, chip, core = where[0], where[1], where[2]
    for slot in range(groups * each):
        order[slot] = -1

    def place(n, _):
        away = lax.rem(bins_of[n] - here + groups, groups) * each

        def taken(k, rank):
            same = lax.rem(bins_of[k] - here + groups, groups) * each == away
            return rank + jnp.where(same, 1, 0)

        order[away + lax.fori_loop(0, n, taken, 0)] = n
        return 0

    lax.fori_loop(0, images.shape[0], place, 0)
    for group in range(groups):
        for k in range(each):
            source = order[group * each + k]
            image = jnp.maximum(source, 0)
            outs[group][k, 0:side, :] = images[image]
            pose = poses_of[image]
            owner = pose // owned
            ahead = lax.rem(owner // 2 - chip + chips, chips)
            across = lax.rem(lax.rem(owner, 2) + core, 2)
            at = (across * chips + ahead) * owned + lax.rem(pose, owned)
            at = jnp.where(source >= 0, at, -1).astype(jnp.float32)
            named = classes_of[image].astype(jnp.float32)
            outs[group][k, side : side + BLOCK, :] = jnp.where(
                lane == 0, at, jnp.where(lane == 1, named, 0.0)
            ).astype(images.dtype)


def pick_images(images, where, image_bin, image_pose, image_class, owned, chips, groups):
    count, side, _ = images.shape
    each = count // 4
    out = jax.ShapeDtypeStruct((each, side + BLOCK, side), images.dtype)
    return pl.pallas_call(
        functools.partial(pick_kernel, owned, chips),
        in_specs=[smem()] * 4 + [vmem()],
        out_specs=[vmem()] * groups,
        out_shape=[out] * groups,
        scratch_shapes=[pltpu.SMEM((groups * each,), jnp.int32)],
        name="pick_images",
    )(where, image_bin, image_pose, image_class, images)


def times_hartley(value, table):
    count, side = value.shape
    high = value.astype(jnp.bfloat16)
    low = (value - high.astype(jnp.float32)).astype(jnp.bfloat16)
    both = jnp.dot(high, table, preferred_element_type=jnp.float32)
    rest = jnp.dot(low, table[:, :side], preferred_element_type=jnp.float32)
    return both[:, :side] + (both[:, side:] + rest)


def spectrum_kernel(groups, each, ctf, table, *refs):
    images, (keep, send, tally, marks, label, sem) = refs[:groups], refs[groups:]
    half = keep.shape[0]
    side = keep.shape[1]
    classes = ctf.shape[0]
    for group in range(groups):
        for k in range(each):
            at = group * each + k
            row = images[group][k, side : side + BLOCK, :].astype(jnp.float32)
            marks[at : at + 1, :] = row[0:1].astype(jnp.int32)
    copy = pltpu.make_async_copy(marks, label, sem)
    copy.start()
    keep[...] = jnp.zeros_like(keep)
    send[...] = jnp.zeros_like(send)
    for k in range(tally.shape[0]):
        tally[k] = 0.0
    hart = table[...]
    copy.wait()
    for group in range(groups):
        pixels = images[group][:, 0:side, :].reshape(each * side, side)
        both = jnp.dot(pixels, hart, preferred_element_type=jnp.float32)
        along = (both[:, :side] + both[:, side:]).reshape(each, side, side)
        turned = jnp.concatenate([along[k].T for k in range(each)], axis=0)
        full = times_hartley(turned, hart).reshape(each, side, side)
        for k in range(each):
            pose, kind = label[group * each + k, 0], label[group * each + k, 1]
            value = ctf[kind] * full[k]

            @pl.when(pose >= 0)
            def _(pose=pose, kind=kind):
                tally[pose * classes + kind] += 1.0

            @pl.when(jnp.logical_and(pose >= 0, pose < half))
            def _(pose=pose, value=value):
                keep[pose] += value

            @pl.when(pose >= half)
            def _(pose=pose, value=value):
                send[pose - half] += value

    for out in (keep, send):
        for pose in range(half):
            out[pose] = out[pose].T


def image_sums(images, ctf, table, poses):
    each, _, side = images[0].shape
    slots = each * len(images)
    half = jax.ShapeDtypeStruct((poses // 2, side, side), jnp.float32)
    return pl.pallas_call(
        functools.partial(spectrum_kernel, len(images), each),
        in_specs=[vmem(), vmem()] + [vmem()] * len(images),
        out_specs=[vmem(), vmem(), smem()],
        out_shape=[half, half, jax.ShapeDtypeStruct((poses * ctf.shape[0],), jnp.float32)],
        scratch_shapes=[
            pltpu.VMEM((slots, side), jnp.int32),
            pltpu.SMEM((slots, side), jnp.int32),
            pltpu.SemaphoreType.DMA(()),
        ],
        name="image_sums",
    )(ctf, table, *images)


def filter_kernel(weight, count, tally, ctf, table, *refs):
    proj, rest = refs[:count], refs[count:]
    out = rest[-2] if len(rest) > 2 else rest[-1]
    owned, side, _ = out.shape
    classes = ctf.shape[0]
    hart = table[...]

    def added(parts):
        return functools.reduce(jnp.add, [part[...].astype(jnp.float32) for part in parts])

    along = times_hartley(added(proj).reshape(owned * side, side), hart)
    turned = jnp.concatenate([along[k * side : (k + 1) * side].T for k in range(owned)], axis=0)
    full = times_hartley(turned, hart)
    total = added(rest[:-2]) if len(rest) > 2 else None
    parts = []
    for k in range(owned):
        gain = jnp.zeros((side, side), jnp.float32)
        for c in range(classes):
            gain = gain + tally[k * classes + c] * (ctf[c] * ctf[c])
        value = gain * full[k * side : (k + 1) * side]
        if total is None:
            value = weight * value + rest[0][k]
        else:
            value = weight * (value - total[k])
            rest[-1][k] = value
        parts.append(value)
    along = times_hartley(jnp.concatenate(parts, axis=0), hart)
    turned = jnp.concatenate([along[k * side : (k + 1) * side].T for k in range(owned)], axis=0)
    field = times_hartley(turned, hart)
    out[...] = field.reshape(owned, side, side).astype(out.dtype)


def residual_field(parts, rest, tally, ctf, table, weight, owned):
    side = table.shape[0]
    block = pl.BlockSpec((owned, side, side), lambda i: (0, 0, 0))
    field = jax.ShapeDtypeStruct((owned, side, side), jnp.bfloat16)
    first = len(rest) > 1
    return pl.pallas_call(
        functools.partial(filter_kernel, weight, len(parts)),
        grid=(1,),
        in_specs=[smem(), vmem(), vmem()] + [block] * (len(parts) + len(rest)),
        out_specs=[block, block] if first else block,
        out_shape=[field, jax.ShapeDtypeStruct(field.shape, jnp.float32)] if first else field,
        name="residual_field",
    )(tally, ctf, table, *parts, *rest)


def load_fields(field, fields):
    at = 0
    for part in fields:
        count = part.shape[0]
        field[at : at + count] = part[...].astype(jnp.float32)
        at += count


def gather_windows(f_ref, field, start, block, poses):
    for pose in range(poses):
        f_ref[pose * WINDOW : (pose + 1) * WINDOW, :] = field[
            pose, pl.ds(start[pose, block], WINDOW), :
        ].astype(jnp.bfloat16)


def block_gradient(t_ref, f_ref, pool2):
    back = jnp.dot(t_ref[...], f_ref[...], preferred_element_type=jnp.float32)
    high = back.astype(jnp.bfloat16)
    low = (back - high.astype(jnp.float32)).astype(jnp.bfloat16)
    return jnp.dot(
        jnp.concatenate([high, low], axis=1), pool2[...], preferred_element_type=jnp.float32
    )


def step_kernel(
    map_side, poses, parts, bin_ref, start, sizes, dens, fold, windows, turned, pool2, pool_t, *refs
):
    fields = refs[:parts]
    first, keep, send, field, f_ref = refs[parts:]
    step = pl.program_id(0)

    @pl.when(step == 0)
    def _():
        keep[...] = jnp.zeros_like(keep)
        send[...] = jnp.zeros_like(send)
        load_fields(field, fields)

    side = fold.shape[2]
    count = dens.shape[1] // BLOCK
    for k in range(count):
        planes = slice(k * BLOCK, (k + 1) * BLOCK)
        index = step * count + k
        gather_windows(f_ref.at[k], field, start, index, poses)
        grad = block_gradient(turned.at[k], f_ref.at[k], pool2)
        kept = dens[:, planes, :].reshape(BLOCK * BLOCK, map_side).astype(jnp.float32)
        moved = kept - sizes[0] * grad
        first[:, planes, :] = moved.reshape(BLOCK, BLOCK, map_side)
        folded = jnp.dot(
            moved.astype(jnp.bfloat16), pool_t[...], preferred_element_type=jnp.float32
        )
        before = fold[:, planes, :].reshape(BLOCK * BLOCK, side).astype(jnp.float32)
        change = folded.astype(jnp.bfloat16).astype(jnp.float32) - before
        high = change.astype(jnp.bfloat16)
        low = (change - high.astype(jnp.float32)).astype(jnp.bfloat16)
        prod = jnp.dot(
            windows[k], jnp.concatenate([high, low], axis=1), preferred_element_type=jnp.float32
        )
        add_projection((keep, send), prod[:, :side] + prod[:, side:], start, index, poses)


def take_step(density, fold, fields, start, tables, sizes, bin_index, pool2, pool_t, row_share):
    map_side, depth, _ = density.shape
    side = pool_t.shape[1]
    poses = start.shape[0]
    half = jax.ShapeDtypeStruct((poses // 2, side, side), jnp.float32)
    row_blocks, count = row_share // BLOCK, depth // BLOCK

    def own(width):
        return pl.BlockSpec((BLOCK, depth, width), lambda i, at: (at[0] * row_blocks + i, 0, 0))

    return pl.pallas_call(
        functools.partial(step_kernel, map_side, poses, len(fields)),
        grid_spec=pltpu.PrefetchScalarGridSpec(
            num_scalar_prefetch=1,
            grid=(row_blocks,),
            in_specs=[smem()] * 2
            + [own(map_side), own(side)]
            + [pl.BlockSpec((count, *table.shape[1:]), lambda i, at: (i, 0, 0)) for table in tables]
            + [vmem()] * (2 + len(fields)),
            out_specs=[
                pl.BlockSpec((BLOCK, depth, map_side), lambda i, at: (i, 0, 0)), vmem(), vmem()
            ],
            scratch_shapes=[
                pltpu.VMEM((poses, side, side), jnp.float32),
                pltpu.VMEM((count, poses * WINDOW, side), jnp.bfloat16),
            ],
        ),
        out_shape=[jax.ShapeDtypeStruct((row_share, depth, map_side), jnp.float32), half, half],
        name="take_step",
    )(bin_index.reshape(1), start, sizes, density, fold, *tables, pool2, pool_t, *fields)


def finish_kernel(map_side, poses, parts, start, sizes, first, turned, pool2, *refs):
    fields = refs[:parts]
    gradient, refined, field, f_ref = refs[parts:]
    step = pl.program_id(0)

    @pl.when(step == 0)
    def _():
        load_fields(field, fields)

    count = first.shape[1] // BLOCK
    for k in range(count):
        planes = slice(k * BLOCK, (k + 1) * BLOCK)
        gather_windows(f_ref.at[k], field, start, step * count + k, poses)
        grad = block_gradient(turned.at[k], f_ref.at[k], pool2).reshape(BLOCK, BLOCK, map_side)
        gradient[:, planes, :] = grad
        refined[:, planes, :] = first[:, planes, :] - sizes[1] * grad


def finish(first, fields, start, turned, sizes, pool2):
    row_share, depth, map_side = first.shape
    side = pool2.shape[0] // 2
    poses = start.shape[0]
    count = depth // BLOCK
    rows = pl.BlockSpec((BLOCK, depth, map_side), lambda i: (i, 0, 0))
    out = jax.ShapeDtypeStruct(first.shape, jnp.float32)
    return pl.pallas_call(
        functools.partial(finish_kernel, map_side, poses, len(fields)),
        grid=(row_share // BLOCK,),
        in_specs=[smem()] * 2
        + [rows, pl.BlockSpec((count, *turned.shape[1:]), lambda i: (i, 0, 0))]
        + [vmem()] * (1 + len(fields)),
        out_specs=[rows, rows],
        out_shape=[out, out],
        scratch_shapes=[
            pltpu.VMEM((poses, side, side), jnp.float32),
            pltpu.VMEM((count, poses * WINDOW, side), jnp.bfloat16),
        ],
        name="finish",
    )(start, sizes, first, turned, pool2, *fields)


def on_device(
    density, images, image_bin, image_pose, image_class, defocus, pose_offset, step_sizes
):
    bins = lax.axis_size("bin")
    slabs = lax.axis_size("slab")
    chips = slabs // 2
    bin_index = lax.axis_index("bin")
    slab_index = lax.axis_index("slab")
    chip, core = slab_index // 2, slab_index % 2
    map_side, depth, _ = density.shape
    image_count, side, _ = images.shape
    pose_count = pose_offset.shape[1]
    classes = defocus.shape[0]
    row_share = map_side // bins
    owned = pose_count // slabs
    weight = 16.0 * pose_count / (image_count * slabs)

    def to_core(value):
        return lax.ppermute(value, "slab", [(s, s ^ 1) for s in range(slabs)])

    def to_chip(value, shift):
        return lax.ppermute(
            value, "slab", [(s, (s + 2 * shift) % slabs) for s in range(slabs)]
        )

    def to_bin(value, shift):
        return lax.ppermute(value, "bin", [(b, (b + shift) % bins) for b in range(bins)])

    where = jnp.stack([bin_index, chip, core]).astype(jnp.int32)
    picked = pick_images(
        images, where, image_bin[:, 0], image_pose, image_class, owned, chips, bins
    )
    picked, pose_offset, defocus = lax.optimization_barrier((picked, pose_offset, defocus))
    got_images = [picked[0]] + [to_bin(picked[d], d) for d in range(1, bins)]

    poses = bins * pose_count
    own_geo, geo, wide_geo = make_geometry(
        where, pose_offset, map_side, side, depth, row_share, chips, owned
    )
    pooling = pool_table(side, map_side).astype(jnp.bfloat16)
    pool_t = jnp.asarray(pooling.T)
    pool2 = jnp.asarray(np.concatenate([pooling, pooling], axis=0))
    table = hartley_table(side)
    ctf = ctf_table(defocus, side)

    def reduce_slab(keep, send, sent_as=jnp.float32):
        got = to_core(send)
        each = keep.shape[0] // chips
        moved = [
            to_chip(
                (keep[d * each : (d + 1) * each] + got[d * each : (d + 1) * each]).astype(sent_as), d
            )
            for d in range(1, chips)
        ]
        return [keep, got] + moved

    def added(parts, each):
        return functools.reduce(jnp.add, [part[:each].astype(jnp.float32) for part in parts])

    keep, send, fold = first_projection(density, pool_t, own_geo, pose_count)
    keep, send, ctf = lax.optimization_barrier((keep, send, ctf))
    proj_parts = reduce_slab(keep, send)
    keep, send, tally = image_sums(got_images, ctf, table, pose_count)
    tally = tally.reshape(2, chips, owned * classes)
    tally = added(reduce_slab(tally[0], tally[1]), 1).reshape(-1)
    total_parts = reduce_slab(keep, send)

    def share_field(field, early=(), late=()):
        near = [field] + [to_bin(field, bins - d) for d in range(1, bins)]
        near, early = lax.optimization_barrier((near, early))
        near = jnp.concatenate(near, axis=0)
        row = [near] + [to_chip(near, chips - d) for d in range(1, chips)]
        row, late = lax.optimization_barrier((row, late))
        return row + [to_core(part) for part in row], early, late

    field, residual = residual_field(proj_parts, total_parts, tally, ctf, table, weight, owned)
    field, geo, wide_geo = lax.optimization_barrier((field, geo, wide_geo))
    blocks = row_share // BLOCK * (depth // BLOCK)
    fields, turned, windows = share_field(
        field,
        turned_table(wide_geo, blocks, poses, map_side),
        window_table(geo, blocks, poses, map_side),
    )
    start = geo[2]
    first, keep, send = take_step(
        density, fold, fields, start, (windows, turned), step_sizes, bin_index, pool2, pool_t,
        row_share,
    )
    change = added(reduce_slab(keep, send, jnp.bfloat16), bins * owned)
    change = change.reshape(bins, owned, side, side)
    moved = [to_bin(change[d].astype(jnp.bfloat16), d) for d in range(1, bins)]
    field = residual_field(
        [change[0]] + moved, [residual], tally, ctf, table, weight, owned
    )
    gradient, refined = finish(first, share_field(field)[0], start, turned, step_sizes, pool2)
    return (gradient, refined)


def solution(mesh):
    return jax.shard_map(
        on_device,
        mesh=mesh,
        in_specs=(
            P("grp", "slab", None),
            P(("grp", "bin", "slab"), None, None),
            P(("grp", "bin", "slab"), None),
            P(("grp", "bin", "slab")),
            P(("grp", "bin", "slab")),
            P("grp"),
            P("grp", None),
            P(),
        ),
        out_specs=(P(("grp", "bin"), "slab", None), P(("grp", "bin"), "slab", None)),
        check_vma=False,
    )
```

```python
import functools
import math

import jax
import jax.numpy as jnp
import numpy as np
from jax import lax
from jax.experimental import pallas as pl
from jax.experimental.pallas import tpu as pltpu
from jax.sharding import PartitionSpec as P

AMP_CONTRAST = 0.1
PHASE_RATE = 60.0
BLOCK = 16
WINDOW = 16
LANES = 128
SMEM = pltpu.SMEM


def vmem():
    return pl.BlockSpec(memory_space=pltpu.VMEM)


def smem():
    return pl.BlockSpec(memory_space=SMEM)


def pool_table(image_side, map_side):
    row_index = np.arange(image_side)[:, None]
    col_index = np.arange(map_side)[None, :]
    return 0.5 * np.maximum(0.0, 1.0 - np.abs(col_index - 2.0 * row_index - 0.5) / 2.0)


def hartley_table(image_side):
    index_row = np.arange(image_side)
    phase_index = index_row[:, None] * index_row[None, :] % image_side
    angle_table = 2.0 * math.pi / image_side * phase_index
    table = (np.cos(angle_table) + np.sin(angle_table)) / math.sqrt(image_side)
    high = table.astype(jnp.bfloat16)
    low = (table - high.astype(np.float64)).astype(jnp.bfloat16)
    return jnp.asarray(np.concatenate([high, low], axis=1))


def ctf_table(defocus, image_side):
    index_row = jnp.arange(image_side, dtype=jnp.int32)
    frequency = (
        jnp.where(index_row < image_side // 2, index_row, index_row - image_side).astype(
            jnp.float32
        )
        / image_side
    )
    part = PHASE_RATE * defocus[:, None] * (frequency * frequency)[None, :]
    shifted = part + math.asin(AMP_CONTRAST)
    return -(
        jnp.sin(shifted)[:, :, None] * jnp.cos(part)[:, None, :]
        + jnp.cos(shifted)[:, :, None] * jnp.sin(part)[:, None, :]
    )


def block_lines(theta, y_low, z_low, side, map_side):
    middle = map_side / 2.0
    scale = 0.25 / math.sqrt(map_side)
    cosine, sine = jnp.cos(theta), jnp.sin(theta)
    y_part = (y_low.astype(jnp.float32) + (0.5 - middle)) * cosine
    z_part = (z_low.astype(jnp.float32) + (0.5 - middle)) * sine
    least = (
        y_part
        + jnp.minimum(0.0, (BLOCK - 1.0) * cosine)
        + z_part
        + jnp.minimum(0.0, (BLOCK - 1.0) * sine)
    )
    column = jnp.floor((least + (middle - 3.0)) * 0.5).astype(jnp.int32)
    start = jnp.clip(column, 0, side - WINDOW)
    offset = scale * (y_part + z_part - (2.0 * start.astype(jnp.float32) + (1.0 - middle)))
    return cosine * scale, sine * scale, start, offset


def geometry_kernel(
    sizes, offsets, own_cos, own_sin, own_start, own_offset, cosine, sine, start, offset,
    wide, lanes
):
    map_side, side, depth, row_share, bins, chips, owned = sizes
    here, slab = lax.axis_index("bin"), lax.axis_index("slab")
    chip, core = slab // 2, lax.rem(slab, 2)
    first_plane = (chip * 2 + core) * depth
    plane_blocks = depth // BLOCK

    def turn(away, place):
        across, ahead, beyond = away
        bin_at = lax.rem(here + beyond, bins)
        owner = lax.rem(chip + ahead, chips) * 2 + lax.rem(core + across, 2)
        return bin_at.astype(jnp.float32) + offsets[bin_at, owner * owned + place]

    def listed(beyonds):
        return [
            turn((across, ahead, beyond), place)
            for across in range(2)
            for ahead in range(chips)
            for beyond in range(beyonds)
            for place in range(owned)
        ]

    def spread(values, index, shape):
        theta = jnp.zeros(shape, jnp.float32)
        for k, value in enumerate(values):
            theta = jnp.where(index == k, value, theta)
        return math.pi * theta / bins

    def fill(outs, values, first_row):
        shape = outs[0].shape
        row = lax.broadcasted_iota(jnp.int32, shape, 0)
        block = lax.broadcasted_iota(jnp.int32, shape, 1)
        theta = spread(values, row, shape)
        found = block_lines(
            theta,
            first_row + block // plane_blocks * BLOCK,
            first_plane + block % plane_blocks * BLOCK,
            side,
            map_side,
        )
        for out, value in zip(outs, found):
            out[...] = value

    first_row = here * row_share
    values = listed(bins)
    fill((own_cos, own_sin, own_start, own_offset), listed(1), 0)
    fill((cosine, sine, start, offset), values, first_row)
    shape = lanes.shape
    block = lax.broadcasted_iota(jnp.int32, shape, 0)
    lane = lax.broadcasted_iota(jnp.int32, shape, 1)
    along_y, along_z, _, offset_wide = block_lines(
        spread(values, lane // WINDOW, shape),
        first_row + block // plane_blocks * BLOCK,
        first_plane + block % plane_blocks * BLOCK,
        side,
        map_side,
    )
    peak = 0.5 / math.sqrt(map_side)
    lanes[...] = offset_wide - peak * (lane % WINDOW).astype(jnp.float32)
    wide[0:1, :] = along_y[0:1]
    wide[1:2, :] = along_z[0:1]


def make_geometry(pose_offset, map_side, side, depth, row_share, chips, owned):
    bins, pose_count = pose_offset.shape
    poses = bins * pose_count

    def tables(count, blocks):
        shape = (count, -(-blocks // LANES) * LANES)
        return [jax.ShapeDtypeStruct(shape, t) for t in (jnp.float32,) * 2] + [
            jax.ShapeDtypeStruct(shape, jnp.int32),
            jax.ShapeDtypeStruct(shape, jnp.float32),
        ]

    plane_blocks = depth // BLOCK
    blocks = row_share // BLOCK * plane_blocks
    shapes = (
        tables(pose_count, map_side // BLOCK * plane_blocks)
        + tables(poses, blocks)
        + [
            jax.ShapeDtypeStruct((2, poses * WINDOW), jnp.float32),
            jax.ShapeDtypeStruct((blocks, poses * WINDOW), jnp.float32),
        ]
    )
    sizes = (map_side, side, depth, row_share, bins, chips, owned)
    out = pl.pallas_call(
        functools.partial(geometry_kernel, sizes),
        in_specs=[smem()],
        out_specs=[vmem()] * len(shapes),
        out_shape=shapes,
        name="geometry",
    )(pose_offset)
    return out[:4], out[4:8], out[8:]


def fill_windows(w_ref, geo, block, poses, map_side):
    lane = lax.broadcasted_iota(jnp.int32, (8, BLOCK * BLOCK), 1)
    row = lax.broadcasted_iota(jnp.int32, (8, BLOCK * BLOCK), 0).astype(jnp.float32)
    y_local = (lane // BLOCK).astype(jnp.float32)
    z_local = (lane % BLOCK).astype(jnp.float32)
    peak = 0.5 / math.sqrt(map_side)
    rows = [peak * (row + 8.0 * k) for k in range(WINDOW // 8)]
    cosine, sine, _, offset = geo
    for pose in range(poses):
        line = y_local * cosine[pose, 0] + z_local * sine[pose, 0] + offset[pose, block]
        parts = [jnp.maximum(0.0, peak - jnp.abs(line - r)) for r in rows]
        w_ref[pose * WINDOW : (pose + 1) * WINDOW, :] = jnp.concatenate(parts, axis=0).astype(
            jnp.bfloat16
        )


def fill_turned(t_ref, wide, lanes, block, map_side):
    peak = 0.5 / math.sqrt(map_side)
    local = lax.broadcasted_iota(jnp.int32, (BLOCK, LANES), 0).astype(jnp.float32)
    offset = lanes[pl.ds(block, 1), :]
    for at in range(0, wide.shape[1], LANES):
        span = slice(at, at + LANES)
        along_z = local * wide[1:2, span] + offset[:, span]
        along_y = wide[0:1, span]
        for y in range(BLOCK):
            line = along_z + float(y) * along_y
            t_ref[y * BLOCK : (y + 1) * BLOCK, span] = jnp.maximum(
                0.0, peak - jnp.abs(line)
            ).astype(jnp.bfloat16)


def windows_kernel(poses, map_side, cosine, sine, start, offset, windows):
    count = windows.shape[0]
    for k in range(count):
        index = pl.program_id(0) * count + k
        fill_windows(windows.at[k], (cosine, sine, start, offset), index, poses, map_side)


def turned_kernel(map_side, wide, lanes, turned):
    count = turned.shape[0]
    for k in range(count):
        index = pl.program_id(0) * count + k
        fill_turned(turned.at[k], wide, lanes, index, map_side)


def table_call(kernel, name, blocks, shape, operands, specs):
    count = math.gcd(blocks, 4)
    return pl.pallas_call(
        kernel,
        grid=(blocks // count,),
        in_specs=specs,
        out_specs=pl.BlockSpec((count, *shape), lambda i: (i, 0, 0)),
        out_shape=jax.ShapeDtypeStruct((blocks, *shape), jnp.bfloat16),
        name=name,
    )(*operands)


def window_table(geo, blocks, poses, map_side):
    return table_call(
        functools.partial(windows_kernel, poses, map_side), "window_table", blocks,
        (poses * WINDOW, BLOCK * BLOCK), geo, [smem()] * 4,
    )


def turned_table(wide_geo, blocks, poses, map_side):
    return table_call(
        functools.partial(turned_kernel, map_side), "turned_table", blocks,
        (BLOCK * BLOCK, poses * WINDOW), wide_geo, [vmem()] * 2,
    )


def add_projection(outs, prod, start, block, poses):
    share = poses // len(outs)
    for first in range(0, poses, 8):
        group = range(first, min(first + 8, poses))
        places = [
            (outs[pose // share], pose % share, pl.ds(start[pose, block], WINDOW))
            for pose in group
        ]
        values = [out[at, rows, :] for out, at, rows in places]
        for pose, value, (out, at, rows) in zip(group, values, places):
            out[at, rows, :] = value + prod[pose * WINDOW : (pose + 1) * WINDOW]


def first_projection_kernel(
    map_side, poses, cosine, sine, start, offset, dens, pool_t, keep, send, fold_ref, w_ref
):
    step = pl.program_id(0)
    geo = (cosine, sine, start, offset)

    @pl.when(step == 0)
    def _():
        keep[...] = jnp.zeros_like(keep)
        send[...] = jnp.zeros_like(send)

    height, depth, _ = dens.shape
    side = pool_t.shape[1]
    folded = jnp.dot(
        dens[...].reshape(height * depth, map_side), pool_t[...], preferred_element_type=jnp.float32
    )
    fold_ref[...] = folded.astype(jnp.bfloat16).reshape(height, depth, side)
    count = height * depth // (BLOCK * BLOCK)
    for k in range(count):
        row, plane = k // (depth // BLOCK) * BLOCK, k % (depth // BLOCK) * BLOCK
        weights = w_ref.at[k]
        fill_windows(weights, geo, step * count + k, poses, map_side)
        pixels = fold_ref[row : row + BLOCK, plane : plane + BLOCK, :].reshape(-1, side)
        prod = jnp.dot(weights[...], pixels, preferred_element_type=jnp.float32)
        add_projection((keep, send), prod, start, step * count + k, poses)


def first_projection(density, pool_t, geo, poses):
    map_side, depth, _ = density.shape
    side = pool_t.shape[1]
    height = 2 * BLOCK
    half = jax.ShapeDtypeStruct((poses // 2, side, side), jnp.float32)
    return pl.pallas_call(
        functools.partial(first_projection_kernel, map_side, poses),
        grid=(map_side // height,),
        in_specs=[smem(), smem(), smem(), smem(),
                  pl.BlockSpec((height, depth, map_side), lambda i: (i, 0, 0)),
                  vmem()],
        out_specs=[vmem(), vmem(), pl.BlockSpec((height, depth, side), lambda i: (i, 0, 0))],
        out_shape=[half, half, jax.ShapeDtypeStruct((map_side, depth, side), jnp.bfloat16)],
        scratch_shapes=[
            pltpu.VMEM(
                (height * depth // BLOCK**2, poses * WINDOW, BLOCK * BLOCK), jnp.bfloat16
            ),
        ],
        name="first_projection",
    )(*geo, density, pool_t)


def pick_kernel(owned, chips, bins_of, poses_of, classes_of, images, *refs):
    outs, order, filled = refs[:-2], refs[-2], refs[-1]
    groups = len(outs)
    each = outs[0].shape[0]
    side = images.shape[1]
    here, slab = lax.axis_index("bin"), lax.axis_index("slab")
    chip, core = slab // 2, lax.rem(slab, 2)
    lane = lax.broadcasted_iota(jnp.int32, (BLOCK, side), 1)

    def ahead(value, size):
        return jnp.where(value < 0, value + size, value)

    for slot in range(groups * each):
        order[slot] = -1
    for group in range(groups):
        filled[group] = 0
    for n in range(images.shape[0]):
        away = ahead(bins_of[n] - here, groups)
        rank = filled[away]
        filled[away] = rank + 1
        order[away * each + rank] = n
    for group in range(groups):
        for k in range(each):
            source = order[group * each + k]
            image = jnp.maximum(source, 0)
            outs[group][k, 0:side, :] = images[image]
            pose = poses_of[image]
            owner = pose // owned
            across = ahead(lax.rem(owner, 2) - core, 2)
            at = (across * chips + ahead(owner // 2 - chip, chips)) * owned + lax.rem(pose, owned)
            at = jnp.where(source >= 0, at, -1).astype(jnp.float32)
            named = classes_of[image].astype(jnp.float32)
            outs[group][k, side : side + BLOCK, :] = jnp.where(
                lane == 0, at, jnp.where(lane == 1, named, 0.0)
            ).astype(images.dtype)


def pick_images(images, image_bin, image_pose, image_class, owned, chips, groups):
    count, side, _ = images.shape
    each = count // 4
    out = jax.ShapeDtypeStruct((each, side + BLOCK, side), images.dtype)
    return pl.pallas_call(
        functools.partial(pick_kernel, owned, chips),
        in_specs=[smem()] * 3 + [vmem()],
        out_specs=[vmem()] * groups,
        out_shape=[out] * groups,
        scratch_shapes=[
            pltpu.SMEM((groups * each,), jnp.int32),
            pltpu.SMEM((groups,), jnp.int32),
        ],
        name="pick_images",
    )(image_bin, image_pose, image_class, images)


def times_hartley(value, table):
    count, side = value.shape
    high = value.astype(jnp.bfloat16)
    low = (value - high.astype(jnp.float32)).astype(jnp.bfloat16)
    both = jnp.dot(high, table, preferred_element_type=jnp.float32)
    rest = jnp.dot(low, table[:, :side], preferred_element_type=jnp.float32)
    return both[:, :side] + (both[:, side:] + rest)


def spectrum_kernel(groups, each, ctf, table, *refs):
    images, (keep, send, tally, marks, label, sums, found, sem) = refs[:groups], refs[groups:]
    half = keep.shape[0]
    side = keep.shape[1]
    poses = 2 * half
    classes = ctf.shape[0]
    for group in range(groups):
        for k in range(each):
            at = group * each + k
            row = images[group][k, side : side + BLOCK, :].astype(jnp.float32)
            marks[at : at + 1, :] = row[0:1].astype(jnp.int32)
    copy = pltpu.make_async_copy(marks, label, sem)
    copy.start()
    sums[...] = jnp.zeros_like(sums)
    for k in range(found.shape[0]):
        found[k] = 0.0
    hart = table[...]
    copy.wait()
    for group in range(groups):
        pixels = images[group][:, 0:side, :].reshape(each * side, side)
        both = jnp.dot(pixels, hart, preferred_element_type=jnp.float32)
        along = (both[:, :side] + both[:, side:]).reshape(each, side, side)
        turned = jnp.concatenate([along[k].T for k in range(each)], axis=0)
        full = times_hartley(turned, hart).reshape(each, side, side)
        for k in range(each):
            pose, kind = label[group * each + k, 0], label[group * each + k, 1]
            pose = jnp.where(pose < 0, poses, pose)
            sums[pose] += ctf[kind] * full[k]
            found[pose * classes + kind] += 1.0
    for k in range(tally.shape[0]):
        tally[k] = found[k]
    for part, out in enumerate((keep, send)):
        for pose in range(half):
            out[pose] = sums[part * half + pose].T


def image_sums(images, ctf, table, poses):
    each, _, side = images[0].shape
    slots = each * len(images)
    half = jax.ShapeDtypeStruct((poses // 2, side, side), jnp.float32)
    return pl.pallas_call(
        functools.partial(spectrum_kernel, len(images), each),
        in_specs=[vmem(), vmem()] + [vmem()] * len(images),
        out_specs=[vmem(), vmem(), smem()],
        out_shape=[half, half, jax.ShapeDtypeStruct((poses * ctf.shape[0],), jnp.float32)],
        scratch_shapes=[
            pltpu.VMEM((slots, side), jnp.int32),
            pltpu.SMEM((slots, side), jnp.int32),
            pltpu.VMEM((poses + 1, side, side), jnp.float32),
            pltpu.SMEM(((poses + 1) * ctf.shape[0],), jnp.float32),
            pltpu.SemaphoreType.DMA(()),
        ],
        name="image_sums",
    )(ctf, table, *images)


def filter_kernel(weight, count, tally, ctf, table, *refs):
    proj, rest = refs[:count], refs[count:]
    out = rest[-2] if len(rest) > 2 else rest[-1]
    owned, side, _ = out.shape
    classes = ctf.shape[0]
    hart = table[...]

    def added(parts):
        return functools.reduce(jnp.add, [part[...].astype(jnp.float32) for part in parts])

    along = times_hartley(added(proj).reshape(owned * side, side), hart)
    turned = jnp.concatenate([along[k * side : (k + 1) * side].T for k in range(owned)], axis=0)
    full = times_hartley(turned, hart)
    total = added(rest[:-2]) if len(rest) > 2 else None
    parts = []
    for k in range(owned):
        gain = jnp.zeros((side, side), jnp.float32)
        for c in range(classes):
            gain = gain + tally[k * classes + c] * (ctf[c] * ctf[c])
        value = gain * full[k * side : (k + 1) * side]
        if total is None:
            value = weight * value + rest[0][k]
        else:
            value = weight * (value - total[k])
            rest[-1][k] = value
        parts.append(value)
    along = times_hartley(jnp.concatenate(parts, axis=0), hart)
    turned = jnp.concatenate([along[k * side : (k + 1) * side].T for k in range(owned)], axis=0)
    field = times_hartley(turned, hart)
    out[...] = field.reshape(owned, side, side).astype(out.dtype)


def residual_field(parts, rest, tally, ctf, table, weight, owned):
    side = table.shape[0]
    block = pl.BlockSpec((owned, side, side), lambda i: (0, 0, 0))
    field = jax.ShapeDtypeStruct((owned, side, side), jnp.bfloat16)
    first = len(rest) > 1
    return pl.pallas_call(
        functools.partial(filter_kernel, weight, len(parts)),
        grid=(1,),
        in_specs=[smem(), vmem(), vmem()] + [block] * (len(parts) + len(rest)),
        out_specs=[block, block] if first else block,
        out_shape=[field, jax.ShapeDtypeStruct(field.shape, jnp.float32)] if first else field,
        name="residual_field",
    )(tally, ctf, table, *parts, *rest)


def load_fields(field, fields):
    at = 0
    for part in fields:
        count = part.shape[0]
        field[at : at + count] = part[...].astype(jnp.float32)
        at += count


def gather_windows(f_ref, field, start, block, poses):
    for pose in range(poses):
        f_ref[pose * WINDOW : (pose + 1) * WINDOW, :] = field[
            pose, pl.ds(start[pose, block], WINDOW), :
        ].astype(jnp.bfloat16)


def step_gradient(split_ref, f_ref, field, turned, pool2, start, first_block, poses):
    height, depth, width = split_ref.shape
    for k in range(depth // BLOCK):
        planes = slice(k * BLOCK, (k + 1) * BLOCK)
        gather_windows(f_ref.at[k], field, start, first_block + k, poses)
        back = jnp.dot(turned[k], f_ref[k], preferred_element_type=jnp.float32)
        high = back.astype(jnp.bfloat16)
        low = (back - high.astype(jnp.float32)).astype(jnp.bfloat16)
        split_ref[:, planes, :] = jnp.concatenate([high, low], axis=1).reshape(
            height, BLOCK, width
        )
    return jnp.dot(
        split_ref[...].reshape(height * depth, width),
        pool2[...],
        preferred_element_type=jnp.float32,
    )


def step_kernel(
    map_side, poses, parts, bin_ref, start, sizes, dens, fold, windows, turned, pool2, pool_t, *refs
):
    fields = refs[:parts]
    first, keep, send, field, f_ref, split_ref = refs[parts:]
    step = pl.program_id(0)

    @pl.when(step == 0)
    def _():
        keep[...] = jnp.zeros_like(keep)
        send[...] = jnp.zeros_like(send)
        load_fields(field, fields)

    height, depth, side = fold.shape
    count = depth // BLOCK
    grad = step_gradient(split_ref, f_ref, field, turned, pool2, start, step * count, poses)
    kept = dens[...].reshape(height * depth, map_side).astype(jnp.float32)
    moved = kept - sizes[0] * grad
    first[...] = moved.reshape(height, depth, map_side)
    folded = jnp.dot(moved.astype(jnp.bfloat16), pool_t[...], preferred_element_type=jnp.float32)
    before = fold[...].reshape(height * depth, side).astype(jnp.float32)
    change = folded.astype(jnp.bfloat16).astype(jnp.float32) - before
    high = change.astype(jnp.bfloat16)
    low = (change - high.astype(jnp.float32)).astype(jnp.bfloat16)
    split_ref[...] = jnp.concatenate([high, low], axis=1).reshape(height, depth, 2 * side)
    for k in range(count):
        pixels = split_ref[:, k * BLOCK : (k + 1) * BLOCK, :].reshape(BLOCK * BLOCK, 2 * side)
        prod = jnp.dot(windows[k], pixels, preferred_element_type=jnp.float32)
        prod = prod[:, :side] + prod[:, side:]
        add_projection((keep, send), prod, start, step * count + k, poses)


def take_step(density, fold, fields, start, tables, sizes, bin_index, pool2, pool_t, row_share):
    map_side, depth, _ = density.shape
    side = pool_t.shape[1]
    poses = start.shape[0]
    half = jax.ShapeDtypeStruct((poses // 2, side, side), jnp.float32)
    row_blocks, count = row_share // BLOCK, depth // BLOCK

    def own(width):
        return pl.BlockSpec((BLOCK, depth, width), lambda i, at: (at[0] * row_blocks + i, 0, 0))

    return pl.pallas_call(
        functools.partial(step_kernel, map_side, poses, len(fields)),
        grid_spec=pltpu.PrefetchScalarGridSpec(
            num_scalar_prefetch=1,
            grid=(row_blocks,),
            in_specs=[smem()] * 2
            + [own(map_side), own(side)]
            + [pl.BlockSpec((count, *table.shape[1:]), lambda i, at: (i, 0, 0)) for table in tables]
            + [vmem()] * (2 + len(fields)),
            out_specs=[
                pl.BlockSpec((BLOCK, depth, map_side), lambda i, at: (i, 0, 0)), vmem(), vmem()
            ],
            scratch_shapes=[
                pltpu.VMEM((poses, side, side), jnp.float32),
                pltpu.VMEM((count, poses * WINDOW, side), jnp.bfloat16),
                pltpu.VMEM((BLOCK, depth, 2 * side), jnp.bfloat16),
            ],
        ),
        out_shape=[jax.ShapeDtypeStruct((row_share, depth, map_side), jnp.float32), half, half],
        name="take_step",
    )(bin_index.reshape(1), start, sizes, density, fold, *tables, pool2, pool_t, *fields)


def finish_kernel(map_side, poses, parts, start, sizes, first, turned, pool2, *refs):
    fields = refs[:parts]
    gradient, refined, field, f_ref, split_ref = refs[parts:]
    step = pl.program_id(0)

    @pl.when(step == 0)
    def _():
        load_fields(field, fields)

    count = first.shape[1] // BLOCK
    grad = step_gradient(split_ref, f_ref, field, turned, pool2, start, step * count, poses)
    grad = grad.reshape(first.shape)
    gradient[...] = grad
    refined[...] = first[...] - sizes[1] * grad


def finish(first, fields, start, turned, sizes, pool2):
    row_share, depth, map_side = first.shape
    side = pool2.shape[0] // 2
    poses = start.shape[0]
    count = depth // BLOCK
    rows = pl.BlockSpec((BLOCK, depth, map_side), lambda i: (i, 0, 0))
    out = jax.ShapeDtypeStruct(first.shape, jnp.float32)
    return pl.pallas_call(
        functools.partial(finish_kernel, map_side, poses, len(fields)),
        grid=(row_share // BLOCK,),
        in_specs=[smem()] * 2
        + [rows, pl.BlockSpec((count, *turned.shape[1:]), lambda i: (i, 0, 0))]
        + [vmem()] * (1 + len(fields)),
        out_specs=[rows, rows],
        out_shape=[out, out],
        scratch_shapes=[
            pltpu.VMEM((poses, side, side), jnp.float32),
            pltpu.VMEM((count, poses * WINDOW, side), jnp.bfloat16),
            pltpu.VMEM((BLOCK, depth, 2 * side), jnp.bfloat16),
        ],
        name="finish",
    )(start, sizes, first, turned, pool2, *fields)


def on_device(
    density, images, image_bin, image_pose, image_class, defocus, pose_offset, step_sizes
):
    bins = lax.axis_size("bin")
    slabs = lax.axis_size("slab")
    chips = slabs // 2
    bin_index = lax.axis_index("bin")
    map_side, depth, _ = density.shape
    image_count, side, _ = images.shape
    pose_count = pose_offset.shape[1]
    classes = defocus.shape[0]
    row_share = map_side // bins
    owned = pose_count // slabs
    weight = 16.0 * pose_count / (image_count * slabs)

    def to_core(value):
        return lax.ppermute(value, "slab", [(s, s ^ 1) for s in range(slabs)])

    def to_chip(value, shift):
        return lax.ppermute(
            value, "slab", [(s, (s + 2 * shift) % slabs) for s in range(slabs)]
        )

    def to_bin(value, shift):
        return lax.ppermute(value, "bin", [(b, (b + shift) % bins) for b in range(bins)])

    picked = pick_images(images, image_bin[:, 0], image_pose, image_class, owned, chips, bins)
    poses = bins * pose_count
    own_geo, geo, wide_geo = make_geometry(
        pose_offset, map_side, side, depth, row_share, chips, owned
    )
    pooling = pool_table(side, map_side).astype(jnp.bfloat16)
    pool_t = jnp.asarray(pooling.T)
    pool2 = jnp.asarray(np.concatenate([pooling, pooling], axis=0))
    table = hartley_table(side)
    ctf = ctf_table(defocus, side)

    picked, own_geo, ctf = lax.optimization_barrier((picked, own_geo, ctf))
    got_images = [picked[0]] + [to_bin(picked[d], d) for d in range(1, bins)]

    def reduce_slab(keep, send, sent_as=jnp.float32):
        got = to_core(send)
        each = keep.shape[0] // chips
        moved = [
            to_chip(
                (keep[d * each : (d + 1) * each] + got[d * each : (d + 1) * each]).astype(sent_as), d
            )
            for d in range(1, chips)
        ]
        return [keep, got] + moved

    def added(parts, each):
        return functools.reduce(jnp.add, [part[:each].astype(jnp.float32) for part in parts])

    keep, send, fold = first_projection(density, pool_t, own_geo, pose_count)
    keep, send, ctf = lax.optimization_barrier((keep, send, ctf))
    proj_parts = reduce_slab(keep, send)
    keep, send, tally = image_sums(got_images, ctf, table, pose_count)
    tally = tally.reshape(2, chips, owned * classes)
    tally = added(reduce_slab(tally[0], tally[1]), 1).reshape(-1)
    total_parts = reduce_slab(keep, send)

    def share_field(field, early=(), late=()):
        near = [field] + [to_bin(field, bins - d) for d in range(1, bins)]
        near, early = lax.optimization_barrier((near, early))
        near = jnp.concatenate(near, axis=0)
        across = [to_chip(near, chips - d) for d in range(1, chips)]
        across, late = lax.optimization_barrier((across, late))
        row = [near] + across
        return row + [to_core(part) for part in row], early, late

    field, residual = residual_field(proj_parts, total_parts, tally, ctf, table, weight, owned)
    field, geo, wide_geo = lax.optimization_barrier((field, geo, wide_geo))
    blocks = row_share // BLOCK * (depth // BLOCK)
    fields, turned, windows = share_field(
        field,
        turned_table(wide_geo, blocks, poses, map_side),
        window_table(geo, blocks, poses, map_side),
    )
    start = geo[2]
    first, keep, send = take_step(
        density, fold, fields, start, (windows, turned), step_sizes, bin_index, pool2, pool_t,
        row_share,
    )
    change = added(reduce_slab(keep, send, jnp.bfloat16), bins * owned)
    change = change.reshape(bins, owned, side, side)
    moved = [to_bin(change[d].astype(jnp.bfloat16), d) for d in range(1, bins)]
    field = residual_field(
        [change[0]] + moved, [residual], tally, ctf, table, weight, owned
    )
    gradient, refined = finish(first, share_field(field)[0], start, turned, step_sizes, pool2)
    return (gradient, refined)


def solution(mesh):
    return jax.shard_map(
        on_device,
        mesh=mesh,
        in_specs=(
            P("grp", "slab", None),
            P(("grp", "bin", "slab"), None, None),
            P(("grp", "bin", "slab"), None),
            P(("grp", "bin", "slab")),
            P(("grp", "bin", "slab")),
            P("grp"),
            P("grp", None),
            P(),
        ),
        out_specs=(P(("grp", "bin"), "slab", None), P(("grp", "bin"), "slab", None)),
        check_vma=False,
    )
```

```python
import functools
import math

import jax
import jax.numpy as jnp
import numpy as np
from jax import lax
from jax.experimental import pallas as pl
from jax.experimental.pallas import tpu as pltpu
from jax.sharding import PartitionSpec as P

AMP_CONTRAST = 0.1
PHASE_RATE = 60.0
BLOCK = 16
WINDOW = 16
LANES = 128
SMEM = pltpu.SMEM


def vmem():
    return pl.BlockSpec(memory_space=pltpu.VMEM)


def smem():
    return pl.BlockSpec(memory_space=SMEM)


def pool_table(image_side, map_side):
    row_index = np.arange(image_side)[:, None]
    col_index = np.arange(map_side)[None, :]
    return 0.5 * np.maximum(0.0, 1.0 - np.abs(col_index - 2.0 * row_index - 0.5) / 2.0)


def hartley_table(image_side):
    index_row = np.arange(image_side)
    phase_index = index_row[:, None] * index_row[None, :] % image_side
    angle_table = 2.0 * math.pi / image_side * phase_index
    table = (np.cos(angle_table) + np.sin(angle_table)) / math.sqrt(image_side)
    high = table.astype(jnp.bfloat16)
    low = (table - high.astype(np.float64)).astype(jnp.bfloat16)
    return jnp.asarray(np.concatenate([high, low], axis=1))


def ctf_table(defocus, image_side):
    index_row = jnp.arange(image_side, dtype=jnp.int32)
    frequency = (
        jnp.where(index_row < image_side // 2, index_row, index_row - image_side).astype(
            jnp.float32
        )
        / image_side
    )
    part = PHASE_RATE * defocus[:, None] * (frequency * frequency)[None, :]
    shifted = part + math.asin(AMP_CONTRAST)
    return -(
        jnp.sin(shifted)[:, :, None] * jnp.cos(part)[:, None, :]
        + jnp.cos(shifted)[:, :, None] * jnp.sin(part)[:, None, :]
    )


def block_lines(theta, y_low, z_low, side, map_side):
    middle = map_side / 2.0
    scale = 0.25 / math.sqrt(map_side)
    cosine, sine = jnp.cos(theta), jnp.sin(theta)
    y_part = (y_low.astype(jnp.float32) + (0.5 - middle)) * cosine
    z_part = (z_low.astype(jnp.float32) + (0.5 - middle)) * sine
    least = (
        y_part
        + jnp.minimum(0.0, (BLOCK - 1.0) * cosine)
        + z_part
        + jnp.minimum(0.0, (BLOCK - 1.0) * sine)
    )
    column = jnp.floor((least + (middle - 3.0)) * 0.5).astype(jnp.int32)
    start = jnp.clip(column, 0, side - WINDOW)
    offset = scale * (y_part + z_part - (2.0 * start.astype(jnp.float32) + (1.0 - middle)))
    return cosine * scale, sine * scale, start, offset


def geometry_kernel(
    sizes, offsets, own_cos, own_sin, own_start, own_offset, cosine, sine, start, offset,
    wide, lanes
):
    map_side, side, depth, row_share, bins, chips, owned = sizes
    here, slab = lax.axis_index("bin"), lax.axis_index("slab")
    chip, core = slab // 2, lax.rem(slab, 2)
    first_plane = (chip * 2 + core) * depth
    plane_blocks = depth // BLOCK

    def turn(away, place):
        across, ahead, beyond = away
        bin_at = here ^ beyond
        owner = lax.rem(chip + ahead, chips) * 2 + lax.rem(core + across, 2)
        return bin_at.astype(jnp.float32) + offsets[bin_at, owner * owned + place]

    def listed(beyonds):
        return [
            turn((across, ahead, beyond), place)
            for across in range(2)
            for ahead in range(chips)
            for beyond in range(beyonds)
            for place in range(owned)
        ]

    def spread(values, index, shape):
        theta = jnp.zeros(shape, jnp.float32)
        for k, value in enumerate(values):
            theta = jnp.where(index == k, value, theta)
        return math.pi * theta / bins

    def fill(outs, values, first_row):
        shape = outs[0].shape
        row = lax.broadcasted_iota(jnp.int32, shape, 0)
        block = lax.broadcasted_iota(jnp.int32, shape, 1)
        theta = spread(values, row, shape)
        found = block_lines(
            theta,
            first_row + block // plane_blocks * BLOCK,
            first_plane + block % plane_blocks * BLOCK,
            side,
            map_side,
        )
        for out, value in zip(outs, found):
            out[...] = value

    first_row = here * row_share
    values = listed(bins)
    fill((own_cos, own_sin, own_start, own_offset), listed(1), 0)
    fill((cosine, sine, start, offset), values, first_row)
    shape = lanes.shape
    block = lax.broadcasted_iota(jnp.int32, shape, 0)
    lane = lax.broadcasted_iota(jnp.int32, shape, 1)
    along_y, along_z, _, offset_wide = block_lines(
        spread(values, lane // WINDOW, shape),
        first_row + block // plane_blocks * BLOCK,
        first_plane + block % plane_blocks * BLOCK,
        side,
        map_side,
    )
    peak = 0.5 / math.sqrt(map_side)
    lanes[...] = offset_wide - peak * (lane % WINDOW).astype(jnp.float32)
    wide[0:1, :] = along_y[0:1]
    wide[1:2, :] = along_z[0:1]


def make_geometry(pose_offset, map_side, side, depth, row_share, chips, owned):
    bins, pose_count = pose_offset.shape
    poses = bins * pose_count

    def tables(count, blocks):
        shape = (count, -(-blocks // LANES) * LANES)
        return [jax.ShapeDtypeStruct(shape, t) for t in (jnp.float32,) * 2] + [
            jax.ShapeDtypeStruct(shape, jnp.int32),
            jax.ShapeDtypeStruct(shape, jnp.float32),
        ]

    plane_blocks = depth // BLOCK
    blocks = row_share // BLOCK * plane_blocks
    shapes = (
        tables(pose_count, map_side // BLOCK * plane_blocks)
        + tables(poses, blocks)
        + [
            jax.ShapeDtypeStruct((2, poses * WINDOW), jnp.float32),
            jax.ShapeDtypeStruct((blocks, poses * WINDOW), jnp.float32),
        ]
    )
    sizes = (map_side, side, depth, row_share, bins, chips, owned)
    out = pl.pallas_call(
        functools.partial(geometry_kernel, sizes),
        in_specs=[smem()],
        out_specs=[vmem()] * len(shapes),
        out_shape=shapes,
        name="geometry",
    )(pose_offset)
    return out[:4], out[4:8], out[8:]


def fill_windows(w_ref, geo, block, poses, map_side):
    lane = lax.broadcasted_iota(jnp.int32, (8, BLOCK * BLOCK), 1)
    row = lax.broadcasted_iota(jnp.int32, (8, BLOCK * BLOCK), 0).astype(jnp.float32)
    y_local = (lane // BLOCK).astype(jnp.float32)
    z_local = (lane % BLOCK).astype(jnp.float32)
    peak = 0.5 / math.sqrt(map_side)
    rows = [peak * (row + 8.0 * k) for k in range(WINDOW // 8)]
    cosine, sine, _, offset = geo
    for pose in range(poses):
        line = y_local * cosine[pose, 0] + z_local * sine[pose, 0] + offset[pose, block]
        parts = [jnp.maximum(0.0, peak - jnp.abs(line - r)) for r in rows]
        w_ref[pose * WINDOW : (pose + 1) * WINDOW, :] = jnp.concatenate(parts, axis=0).astype(
            jnp.bfloat16
        )


def fill_turned(t_ref, wide, lanes, block, map_side):
    peak = 0.5 / math.sqrt(map_side)
    local = lax.broadcasted_iota(jnp.int32, (BLOCK, LANES), 0).astype(jnp.float32)
    offset = lanes[pl.ds(block, 1), :]
    for at in range(0, wide.shape[1], LANES):
        span = slice(at, at + LANES)
        along_z = local * wide[1:2, span] + offset[:, span]
        along_y = wide[0:1, span]
        for y in range(BLOCK):
            line = along_z + float(y) * along_y
            t_ref[y * BLOCK : (y + 1) * BLOCK, span] = jnp.maximum(
                0.0, peak - jnp.abs(line)
            ).astype(jnp.bfloat16)


def windows_kernel(poses, map_side, cosine, sine, start, offset, windows):
    count = windows.shape[0]
    for k in range(count):
        index = pl.program_id(0) * count + k
        fill_windows(windows.at[k], (cosine, sine, start, offset), index, poses, map_side)


def turned_kernel(map_side, wide, lanes, turned):
    count = turned.shape[0]
    for k in range(count):
        index = pl.program_id(0) * count + k
        fill_turned(turned.at[k], wide, lanes, index, map_side)


def table_call(kernel, name, blocks, shape, operands, specs):
    count = math.gcd(blocks, 4)
    return pl.pallas_call(
        kernel,
        grid=(blocks // count,),
        in_specs=specs,
        out_specs=pl.BlockSpec((count, *shape), lambda i: (i, 0, 0)),
        out_shape=jax.ShapeDtypeStruct((blocks, *shape), jnp.bfloat16),
        name=name,
    )(*operands)


def window_table(geo, blocks, poses, map_side):
    return table_call(
        functools.partial(windows_kernel, poses, map_side), "window_table", blocks,
        (poses * WINDOW, BLOCK * BLOCK), geo, [smem()] * 4,
    )


def turned_table(wide_geo, blocks, poses, map_side):
    return table_call(
        functools.partial(turned_kernel, map_side), "turned_table", blocks,
        (BLOCK * BLOCK, poses * WINDOW), wide_geo, [vmem()] * 2,
    )


def add_projection(outs, prod, start, block, poses):
    share = poses // len(outs)
    for first in range(0, poses, 8):
        group = range(first, min(first + 8, poses))
        places = [
            (outs[pose // share], pose % share, pl.ds(start[pose, block], WINDOW))
            for pose in group
        ]
        values = [out[at, rows, :] for out, at, rows in places]
        for pose, value, (out, at, rows) in zip(group, values, places):
            out[at, rows, :] = value + prod[pose * WINDOW : (pose + 1) * WINDOW]


def first_projection_kernel(
    map_side, poses, cosine, sine, start, offset, dens, pool_t, keep, send, fold_ref, w_ref
):
    step = pl.program_id(0)
    geo = (cosine, sine, start, offset)

    @pl.when(step == 0)
    def _():
        keep[...] = jnp.zeros_like(keep)
        send[...] = jnp.zeros_like(send)

    height, depth, _ = dens.shape
    side = pool_t.shape[1]
    folded = jnp.dot(
        dens[...].reshape(height * depth, map_side), pool_t[...], preferred_element_type=jnp.float32
    )
    fold_ref[...] = folded.astype(jnp.bfloat16).reshape(height, depth, side)
    count = height * depth // (BLOCK * BLOCK)
    for k in range(count):
        row, plane = k // (depth // BLOCK) * BLOCK, k % (depth // BLOCK) * BLOCK
        weights = w_ref.at[k]
        fill_windows(weights, geo, step * count + k, poses, map_side)
        pixels = fold_ref[row : row + BLOCK, plane : plane + BLOCK, :].reshape(-1, side)
        prod = jnp.dot(weights[...], pixels, preferred_element_type=jnp.float32)
        add_projection((keep, send), prod, start, step * count + k, poses)


def first_projection(density, pool_t, geo, poses):
    map_side, depth, _ = density.shape
    side = pool_t.shape[1]
    height = 2 * BLOCK
    half = jax.ShapeDtypeStruct((poses // 2, side, side), jnp.float32)
    return pl.pallas_call(
        functools.partial(first_projection_kernel, map_side, poses),
        grid=(map_side // height,),
        in_specs=[smem(), smem(), smem(), smem(),
                  pl.BlockSpec((height, depth, map_side), lambda i: (i, 0, 0)),
                  vmem()],
        out_specs=[vmem(), vmem(), pl.BlockSpec((height, depth, side), lambda i: (i, 0, 0))],
        out_shape=[half, half, jax.ShapeDtypeStruct((map_side, depth, side), jnp.bfloat16)],
        scratch_shapes=[
            pltpu.VMEM(
                (height * depth // BLOCK**2, poses * WINDOW, BLOCK * BLOCK), jnp.bfloat16
            ),
        ],
        name="first_projection",
    )(*geo, density, pool_t)


def pick_kernel(owned, chips, bins_of, poses_of, classes_of, images, *refs):
    outs, order, filled = refs[:-2], refs[-2], refs[-1]
    groups = len(outs)
    each = outs[0].shape[0]
    side = images.shape[1]
    here, slab = lax.axis_index("bin"), lax.axis_index("slab")
    chip, core = slab // 2, lax.rem(slab, 2)
    lane = lax.broadcasted_iota(jnp.int32, (BLOCK, side), 1)

    def ahead(value, size):
        return jnp.where(value < 0, value + size, value)

    for slot in range(groups * each):
        order[slot] = -1
    for group in range(groups):
        filled[group] = 0
    for n in range(images.shape[0]):
        away = bins_of[n] ^ here
        rank = filled[away]
        filled[away] = rank + 1
        order[away * each + rank] = n
    for group in range(groups):
        for k in range(each):
            source = order[group * each + k]
            image = jnp.maximum(source, 0)
            outs[group][k, 0:side, :] = images[image]
            pose = poses_of[image]
            owner = pose // owned
            across = ahead(lax.rem(owner, 2) - core, 2)
            at = (across * chips + ahead(owner // 2 - chip, chips)) * owned + lax.rem(pose, owned)
            at = jnp.where(source >= 0, at, -1).astype(jnp.float32)
            named = classes_of[image].astype(jnp.float32)
            outs[group][k, side : side + BLOCK, :] = jnp.where(
                lane == 0, at, jnp.where(lane == 1, named, 0.0)
            ).astype(images.dtype)


def pick_images(images, image_bin, image_pose, image_class, owned, chips, groups):
    count, side, _ = images.shape
    each = count // 4
    out = jax.ShapeDtypeStruct((each, side + BLOCK, side), images.dtype)
    return pl.pallas_call(
        functools.partial(pick_kernel, owned, chips),
        in_specs=[smem()] * 3 + [vmem()],
        out_specs=[vmem()] * groups,
        out_shape=[out] * groups,
        scratch_shapes=[
            pltpu.SMEM((groups * each,), jnp.int32),
            pltpu.SMEM((groups,), jnp.int32),
        ],
        name="pick_images",
    )(image_bin, image_pose, image_class, images)


def times_hartley(value, table):
    count, side = value.shape
    high = value.astype(jnp.bfloat16)
    low = (value - high.astype(jnp.float32)).astype(jnp.bfloat16)
    both = jnp.dot(high, table, preferred_element_type=jnp.float32)
    rest = jnp.dot(low, table[:, :side], preferred_element_type=jnp.float32)
    return both[:, :side] + (both[:, side:] + rest)


def spectrum_kernel(groups, each, ctf, table, *refs):
    images, (keep, send, marks, label, sums, sem) = refs[:groups], refs[groups:]
    half = keep.shape[0]
    side = keep.shape[2]
    poses = 2 * half
    for group in range(groups):
        for k in range(each):
            at = group * each + k
            row = images[group][k, side : side + BLOCK, :].astype(jnp.float32)
            marks[at : at + 1, :] = row[0:1].astype(jnp.int32)
    copy = pltpu.make_async_copy(marks, label, sem)
    copy.start()
    sums[...] = jnp.zeros_like(sums)
    hart = table[...]
    lane = lax.broadcasted_iota(jnp.int32, (8, side), 1)
    copy.wait()
    for group in range(groups):
        pixels = images[group][:, 0:side, :].reshape(each * side, side)
        both = jnp.dot(pixels, hart, preferred_element_type=jnp.float32)
        along = (both[:, :side] + both[:, side:]).reshape(each, side, side)
        turned = jnp.concatenate([along[k].T for k in range(each)], axis=0)
        full = times_hartley(turned, hart).reshape(each, side, side)
        for k in range(each):
            pose, kind = label[group * each + k, 0], label[group * each + k, 1]
            pose = jnp.where(pose < 0, poses, pose)
            sums[pose, 0:side, :] += ctf[kind] * full[k]
            sums[pose, side : side + 8, :] += jnp.where(lane == kind, 1.0, 0.0)
    for part, out in enumerate((keep, send)):
        for pose in range(half):
            out[pose, 0:side, :] = sums[part * half + pose, 0:side, :].T
            out[pose, side : side + 8, :] = sums[part * half + pose, side : side + 8, :]


def image_sums(images, ctf, table, poses):
    each, _, side = images[0].shape
    slots = each * len(images)
    half = jax.ShapeDtypeStruct((poses // 2, side + 8, side), jnp.float32)
    return pl.pallas_call(
        functools.partial(spectrum_kernel, len(images), each),
        in_specs=[vmem(), vmem()] + [vmem()] * len(images),
        out_specs=[vmem(), vmem()],
        out_shape=[half, half],
        scratch_shapes=[
            pltpu.VMEM((slots, side), jnp.int32),
            pltpu.SMEM((slots, side), jnp.int32),
            pltpu.VMEM((poses + 1, side + 8, side), jnp.float32),
            pltpu.SemaphoreType.DMA(()),
        ],
        name="image_sums",
    )(ctf, table, *images)


def added(parts):
    return functools.reduce(jnp.add, [part[...].astype(jnp.float32) for part in parts])


def through(values, hart, change):
    owned, side, _ = values.shape

    def turn(rows):
        return jnp.concatenate([rows[k * side : (k + 1) * side].T for k in range(owned)], axis=0)

    full = times_hartley(turn(times_hartley(values.reshape(owned * side, side), hart)), hart)
    parts = [change(k, full[k * side : (k + 1) * side]) for k in range(owned)]
    field = times_hartley(turn(times_hartley(jnp.concatenate(parts, axis=0), hart)), hart)
    return field.reshape(owned, side, side)


def first_filter_kernel(weight, count, ctf, table, *refs):
    proj, totals, (field, residual, gains) = refs[:count], refs[count:-3], refs[-3:]
    _, side, _ = field.shape
    total = added(totals)

    def change(k, value):
        gain = jnp.zeros((side, side), jnp.float32)
        for c in range(ctf.shape[0]):
            gain = gain + total[k, side : side + 1, c : c + 1] * (ctf[c] * ctf[c])
        value = weight * (gain * value - total[k, 0:side, :])
        gains[k] = weight * gain
        residual[k] = value
        return value

    field[...] = through(added(proj), table[...], change).astype(field.dtype)


def first_field(proj, totals, ctf, table, weight, owned):
    side = table.shape[0]
    block = pl.BlockSpec((owned, side, side), lambda i: (0, 0, 0))
    tall = pl.BlockSpec((owned, side + 8, side), lambda i: (0, 0, 0))
    kept = jax.ShapeDtypeStruct((owned, side, side), jnp.float32)
    return pl.pallas_call(
        functools.partial(first_filter_kernel, weight, len(proj)),
        grid=(1,),
        in_specs=[vmem(), vmem()] + [block] * len(proj) + [tall] * len(totals),
        out_specs=[block] * 3,
        out_shape=[jax.ShapeDtypeStruct(kept.shape, jnp.bfloat16), kept, kept],
        name="first_field",
    )(ctf, table, *proj, *totals)


def next_filter_kernel(table, residual, gains, *refs):
    parts, field = refs[:-1], refs[-1]

    def change(k, value):
        return gains[k] * value + residual[k]

    field[...] = through(added(parts), table[...], change).astype(field.dtype)


def next_field(parts, residual, gains, table):
    block = pl.BlockSpec(residual.shape, lambda i: (0, 0, 0))
    return pl.pallas_call(
        next_filter_kernel,
        grid=(1,),
        in_specs=[vmem()] + [block] * (2 + len(parts)),
        out_specs=block,
        out_shape=jax.ShapeDtypeStruct(residual.shape, jnp.bfloat16),
        name="next_field",
    )(table, residual, gains, *parts)


def load_fields(field, fields):
    at = 0
    for part in fields:
        count = part.shape[0]
        field[at : at + count] = part[...].astype(jnp.float32)
        at += count


def gather_windows(f_ref, field, start, block, poses):
    for pose in range(poses):
        f_ref[pose * WINDOW : (pose + 1) * WINDOW, :] = field[
            pose, pl.ds(start[pose, block], WINDOW), :
        ].astype(jnp.bfloat16)


def step_gradient(split_ref, f_ref, field, turned, pool2, start, first_block, poses):
    height, depth, width = split_ref.shape
    for k in range(depth // BLOCK):
        planes = slice(k * BLOCK, (k + 1) * BLOCK)
        gather_windows(f_ref.at[k], field, start, first_block + k, poses)
        back = jnp.dot(turned[k], f_ref[k], preferred_element_type=jnp.float32)
        high = back.astype(jnp.bfloat16)
        low = (back - high.astype(jnp.float32)).astype(jnp.bfloat16)
        split_ref[:, planes, :] = jnp.concatenate([high, low], axis=1).reshape(
            height, BLOCK, width
        )
    return jnp.dot(
        split_ref[...].reshape(height * depth, width),
        pool2[...],
        preferred_element_type=jnp.float32,
    )


def step_kernel(
    map_side, poses, parts, bin_ref, start, sizes, dens, fold, windows, turned, pool2, pool_t, *refs
):
    fields = refs[:parts]
    first, keep, sent, field, f_ref, split_ref, send = refs[parts:]
    step = pl.program_id(0)

    @pl.when(step == 0)
    def _():
        keep[...] = jnp.zeros_like(keep)
        send[...] = jnp.zeros_like(send)
        load_fields(field, fields)

    height, depth, side = fold.shape
    count = depth // BLOCK
    grad = step_gradient(split_ref, f_ref, field, turned, pool2, start, step * count, poses)
    kept = dens[...].reshape(height * depth, map_side).astype(jnp.float32)
    moved = kept - sizes[0] * grad
    first[...] = moved.reshape(height, depth, map_side)
    folded = jnp.dot(moved.astype(jnp.bfloat16), pool_t[...], preferred_element_type=jnp.float32)
    before = fold[...].reshape(height * depth, side).astype(jnp.float32)
    change = folded.astype(jnp.bfloat16).astype(jnp.float32) - before
    high = change.astype(jnp.bfloat16)
    low = (change - high.astype(jnp.float32)).astype(jnp.bfloat16)
    split_ref[...] = jnp.concatenate([high, low], axis=1).reshape(height, depth, 2 * side)
    for k in range(count):
        pixels = split_ref[:, k * BLOCK : (k + 1) * BLOCK, :].reshape(BLOCK * BLOCK, 2 * side)
        prod = jnp.dot(windows[k], pixels, preferred_element_type=jnp.float32)
        prod = prod[:, :side] + prod[:, side:]
        add_projection((keep, send), prod, start, step * count + k, poses)

    @pl.when(step == pl.num_programs(0) - 1)
    def _():
        sent[...] = send[...].astype(sent.dtype)


def take_step(density, fold, fields, start, tables, sizes, bin_index, pool2, pool_t, row_share):
    map_side, depth, _ = density.shape
    side = pool_t.shape[1]
    poses = start.shape[0]
    half = jax.ShapeDtypeStruct((poses // 2, side, side), jnp.float32)
    row_blocks, count = row_share // BLOCK, depth // BLOCK

    def own(width):
        return pl.BlockSpec((BLOCK, depth, width), lambda i, at: (at[0] * row_blocks + i, 0, 0))

    return pl.pallas_call(
        functools.partial(step_kernel, map_side, poses, len(fields)),
        grid_spec=pltpu.PrefetchScalarGridSpec(
            num_scalar_prefetch=1,
            grid=(row_blocks,),
            in_specs=[smem()] * 2
            + [own(map_side), own(side)]
            + [pl.BlockSpec((count, *table.shape[1:]), lambda i, at: (i, 0, 0)) for table in tables]
            + [vmem()] * (2 + len(fields)),
            out_specs=[
                pl.BlockSpec((BLOCK, depth, map_side), lambda i, at: (i, 0, 0)), vmem(), vmem()
            ],
            scratch_shapes=[
                pltpu.VMEM((poses, side, side), jnp.float32),
                pltpu.VMEM((count, poses * WINDOW, side), jnp.bfloat16),
                pltpu.VMEM((BLOCK, depth, 2 * side), jnp.bfloat16),
                pltpu.VMEM(half.shape, jnp.float32),
            ],
        ),
        out_shape=[
            jax.ShapeDtypeStruct((row_share, depth, map_side), jnp.float32),
            half,
            jax.ShapeDtypeStruct(half.shape, jnp.bfloat16),
        ],
        name="take_step",
    )(bin_index.reshape(1), start, sizes, density, fold, *tables, pool2, pool_t, *fields)


def finish_kernel(map_side, poses, parts, start, sizes, first, turned, pool2, *refs):
    fields = refs[:parts]
    gradient, refined, field, f_ref, split_ref = refs[parts:]
    step = pl.program_id(0)

    @pl.when(step == 0)
    def _():
        load_fields(field, fields)

    count = first.shape[1] // BLOCK
    grad = step_gradient(split_ref, f_ref, field, turned, pool2, start, step * count, poses)
    grad = grad.reshape(first.shape)
    gradient[...] = grad
    refined[...] = first[...] - sizes[1] * grad


def finish(first, fields, start, turned, sizes, pool2):
    row_share, depth, map_side = first.shape
    side = pool2.shape[0] // 2
    poses = start.shape[0]
    count = depth // BLOCK
    rows = pl.BlockSpec((BLOCK, depth, map_side), lambda i: (i, 0, 0))
    out = jax.ShapeDtypeStruct(first.shape, jnp.float32)
    return pl.pallas_call(
        functools.partial(finish_kernel, map_side, poses, len(fields)),
        grid=(row_share // BLOCK,),
        in_specs=[smem()] * 2
        + [rows, pl.BlockSpec((count, *turned.shape[1:]), lambda i: (i, 0, 0))]
        + [vmem()] * (1 + len(fields)),
        out_specs=[rows, rows],
        out_shape=[out, out],
        scratch_shapes=[
            pltpu.VMEM((poses, side, side), jnp.float32),
            pltpu.VMEM((count, poses * WINDOW, side), jnp.bfloat16),
            pltpu.VMEM((BLOCK, depth, 2 * side), jnp.bfloat16),
        ],
        name="finish",
    )(start, sizes, first, turned, pool2, *fields)


def on_device(
    density, images, image_bin, image_pose, image_class, defocus, pose_offset, step_sizes
):
    bins = lax.axis_size("bin")
    slabs = lax.axis_size("slab")
    chips = slabs // 2
    bin_index = lax.axis_index("bin")
    map_side, depth, _ = density.shape
    image_count, side, _ = images.shape
    pose_count = pose_offset.shape[1]
    row_share = map_side // bins
    owned = pose_count // slabs
    weight = 16.0 * pose_count / (image_count * slabs)

    def to_core(value):
        return lax.ppermute(value, "slab", [(s, s ^ 1) for s in range(slabs)])

    def to_chip(value, shift):
        return lax.ppermute(
            value, "slab", [(s, (s + 2 * shift) % slabs) for s in range(slabs)]
        )

    def to_bin(value, shift):
        return lax.ppermute(value, "bin", [(b, b ^ shift) for b in range(bins)])

    picked = pick_images(images, image_bin[:, 0], image_pose, image_class, owned, chips, bins)
    poses = bins * pose_count
    own_geo, geo, wide_geo = make_geometry(
        pose_offset, map_side, side, depth, row_share, chips, owned
    )
    pooling = pool_table(side, map_side).astype(jnp.bfloat16)
    pool_t = jnp.asarray(pooling.T)
    pool2 = jnp.asarray(np.concatenate([pooling, pooling], axis=0))
    table = hartley_table(side)
    ctf = ctf_table(defocus, side)

    picked, own_geo, ctf = lax.optimization_barrier((picked, own_geo, ctf))
    got_images = [picked[0]] + [to_bin(picked[d], d) for d in range(1, bins)]

    def reduce_slab(keep, send, sent_as=jnp.float32):
        got = to_core(send)
        each = keep.shape[0] // chips

        def joined(d):
            rows = slice(d * each, (d + 1) * each)
            return (keep[rows] + got[rows].astype(jnp.float32)).astype(sent_as)

        return [keep, got] + [to_chip(joined(d), d) for d in range(1, chips)]

    keep, send, fold = first_projection(density, pool_t, own_geo, pose_count)
    keep, send, ctf = lax.optimization_barrier((keep, send, ctf))
    proj_parts = reduce_slab(keep, send)
    keep, send = image_sums(got_images, ctf, table, pose_count)
    total_parts = reduce_slab(keep, send)

    def share_field(field, early=(), late=()):
        near = [field] + [to_bin(field, d) for d in range(1, bins)]
        near, early = lax.optimization_barrier((near, early))
        near = jnp.concatenate(near, axis=0)
        across = [to_chip(near, chips - d) for d in range(1, chips)]
        across, late = lax.optimization_barrier((across, late))
        row = [near] + across
        return row + [to_core(part) for part in row], early, late

    field, residual, gains = first_field(proj_parts, total_parts, ctf, table, weight, owned)
    field, geo, wide_geo = lax.optimization_barrier((field, geo, wide_geo))
    blocks = row_share // BLOCK * (depth // BLOCK)
    fields, turned, windows = share_field(
        field,
        turned_table(wide_geo, blocks, poses, map_side),
        window_table(geo, blocks, poses, map_side),
    )
    start = geo[2]
    first, keep, send = take_step(
        density, fold, fields, start, (windows, turned), step_sizes, bin_index, pool2, pool_t,
        row_share,
    )
    parts = reduce_slab(keep, send, jnp.bfloat16)

    def change(d):
        rows = slice(d * owned, (d + 1) * owned)
        return functools.reduce(jnp.add, [part[rows].astype(jnp.float32) for part in parts])

    moved = [to_bin(change(d).astype(jnp.bfloat16), d) for d in range(1, bins)]
    field = next_field(parts + moved, residual, gains, table)
    gradient, refined = finish(first, share_field(field)[0], start, turned, step_sizes, pool2)
    return (gradient, refined)


def solution(mesh):
    return jax.shard_map(
        on_device,
        mesh=mesh,
        in_specs=(
            P("grp", "slab", None),
            P(("grp", "bin", "slab"), None, None),
            P(("grp", "bin", "slab"), None),
            P(("grp", "bin", "slab")),
            P(("grp", "bin", "slab")),
            P("grp"),
            P("grp", None),
            P(),
        ),
        out_specs=(P(("grp", "bin"), "slab", None), P(("grp", "bin"), "slab", None)),
        check_vma=False,
    )
```

```python
import functools
import math

import jax
import jax.numpy as jnp
import numpy as np
from jax import lax
from jax.experimental import pallas as pl
from jax.experimental.pallas import tpu as pltpu
from jax.sharding import PartitionSpec as P


AMP_CONTRAST = 0.1
PHASE_RATE = 60.0
BLOCK = 16
WINDOW = 16
LANES = 128
SMEM = pltpu.SMEM


def vmem():
    return pl.BlockSpec(memory_space=pltpu.VMEM)


def smem():
    return pl.BlockSpec(memory_space=SMEM)


def pool_table(image_side, map_side):
    row_index = np.arange(image_side)[:, None]
    col_index = np.arange(map_side)[None, :]
    return 0.5 * np.maximum(0.0, 1.0 - np.abs(col_index - 2.0 * row_index - 0.5) / 2.0)


def hartley_table(image_side):
    index_row = np.arange(image_side)
    phase_index = index_row[:, None] * index_row[None, :] % image_side
    angle_table = 2.0 * math.pi / image_side * phase_index
    table = (np.cos(angle_table) + np.sin(angle_table)) / math.sqrt(image_side)
    high = table.astype(jnp.bfloat16)
    low = (table - high.astype(np.float64)).astype(jnp.bfloat16)
    return jnp.asarray(np.concatenate([high, low], axis=1))


def fill_ctf(ctf, defocus):
    classes, side, _ = ctf.shape
    row = lax.broadcasted_iota(jnp.int32, (classes, side), 0)
    lane = lax.broadcasted_iota(jnp.int32, (classes, side), 1)
    value = jnp.zeros((classes, side), jnp.float32)
    for c in range(classes):
        value = jnp.where(row == c, defocus[c], value)
    frequency = jnp.where(lane < side // 2, lane, lane - side).astype(jnp.float32) / side
    part = PHASE_RATE * value * (frequency * frequency)
    shifted = part + math.asin(AMP_CONTRAST)
    across = (jnp.cos(part), jnp.sin(part))
    down = jnp.concatenate(
        [
            jnp.sin(shifted),
            jnp.cos(shifted),
            jnp.zeros((side - 2 * classes, side), jnp.float32),
        ],
        axis=0,
    ).T
    for c in range(classes):
        ctf[c] = -(
            down[:, c : c + 1] * across[0][c : c + 1]
            + down[:, classes + c : classes + c + 1] * across[1][c : c + 1]
        )


def block_lines(theta, y_low, z_low, side, map_side):
    middle = map_side / 2.0
    scale = 0.25 / math.sqrt(map_side)
    cosine, sine = jnp.cos(theta), jnp.sin(theta)
    y_part = (y_low.astype(jnp.float32) + (0.5 - middle)) * cosine
    z_part = (z_low.astype(jnp.float32) + (0.5 - middle)) * sine
    least = (
        y_part
        + jnp.minimum(0.0, (BLOCK - 1.0) * cosine)
        + z_part
        + jnp.minimum(0.0, (BLOCK - 1.0) * sine)
    )
    column = jnp.floor((least + (middle - 3.0)) * 0.5).astype(jnp.int32)
    start = jnp.clip(column, 0, side - WINDOW)
    offset = scale * (y_part + z_part - (2.0 * start.astype(jnp.float32) + (1.0 - middle)))
    return cosine * scale, sine * scale, start, offset


def geometry_kernel(
    sizes, offsets, own_cos, own_sin, own_start, own_offset, cosine, sine, start, offset,
    wide, lanes
):
    map_side, side, depth, row_share, bins, chips, owned = sizes
    here, slab = lax.axis_index("bin"), lax.axis_index("slab")
    chip, core = slab // 2, lax.rem(slab, 2)
    first_plane = (chip * 2 + core) * depth
    plane_blocks = depth // BLOCK

    def turn(away, place):
        across, ahead, beyond = away
        bin_at = lax.rem(here + beyond, bins)
        owner = lax.rem(chip + ahead, chips) * 2 + lax.rem(core + across, 2)
        return bin_at.astype(jnp.float32) + offsets[bin_at, owner * owned + place]

    def listed(beyonds):
        return [
            turn((across, ahead, beyond), place)
            for across in range(2)
            for ahead in range(chips)
            for beyond in range(beyonds)
            for place in range(owned)
        ]

    def spread(values, index, shape):
        theta = jnp.zeros(shape, jnp.float32)
        for k, value in enumerate(values):
            theta = jnp.where(index == k, value, theta)
        return math.pi * theta / bins

    def fill(outs, values, first_row):
        shape = outs[0].shape
        row = lax.broadcasted_iota(jnp.int32, shape, 0)
        block = lax.broadcasted_iota(jnp.int32, shape, 1)
        theta = spread(values, row, shape)
        found = block_lines(
            theta,
            first_row + block // plane_blocks * BLOCK,
            first_plane + block % plane_blocks * BLOCK,
            side,
            map_side,
        )
        for out, value in zip(outs, found):
            out[...] = value

    first_row = here * row_share
    values = listed(bins)
    fill((own_cos, own_sin, own_start, own_offset), listed(1), 0)
    fill((cosine, sine, start, offset), values, first_row)
    shape = lanes.shape
    block = lax.broadcasted_iota(jnp.int32, shape, 0)
    lane = lax.broadcasted_iota(jnp.int32, shape, 1)
    along_y, along_z, _, offset_wide = block_lines(
        spread(values, lane // WINDOW, shape),
        first_row + block // plane_blocks * BLOCK,
        first_plane + block % plane_blocks * BLOCK,
        side,
        map_side,
    )
    peak = 0.5 / math.sqrt(map_side)
    lanes[...] = offset_wide - peak * (lane % WINDOW).astype(jnp.float32)
    wide[0:1, :] = along_y[0:1]
    wide[1:2, :] = along_z[0:1]


def make_geometry(pose_offset, map_side, side, depth, row_share, chips, owned):
    bins, pose_count = pose_offset.shape
    poses = bins * pose_count

    def tables(count, blocks):
        shape = (count, -(-blocks // LANES) * LANES)
        return [jax.ShapeDtypeStruct(shape, t) for t in (jnp.float32,) * 2] + [
            jax.ShapeDtypeStruct(shape, jnp.int32),
            jax.ShapeDtypeStruct(shape, jnp.float32),
        ]

    plane_blocks = depth // BLOCK
    blocks = row_share // BLOCK * plane_blocks
    shapes = (
        tables(pose_count, map_side // BLOCK * plane_blocks)
        + tables(poses, blocks)
        + [
            jax.ShapeDtypeStruct((2, poses * WINDOW), jnp.float32),
            jax.ShapeDtypeStruct((blocks, poses * WINDOW), jnp.float32),
        ]
    )
    sizes = (map_side, side, depth, row_share, bins, chips, owned)
    out = pl.pallas_call(
        functools.partial(geometry_kernel, sizes),
        in_specs=[smem()],
        out_specs=[vmem()] * len(shapes),
        out_shape=shapes,
        name="geometry",
    )(pose_offset)
    return out[:4], out[4:8], out[8:]


def fill_windows(w_ref, geo, block, poses, map_side):
    lane = lax.broadcasted_iota(jnp.int32, (8, BLOCK * BLOCK), 1)
    row = lax.broadcasted_iota(jnp.int32, (8, BLOCK * BLOCK), 0).astype(jnp.float32)
    y_local = (lane // BLOCK).astype(jnp.float32)
    z_local = (lane % BLOCK).astype(jnp.float32)
    peak = 0.5 / math.sqrt(map_side)
    rows = [peak * (row + 8.0 * k) for k in range(WINDOW // 8)]
    cosine, sine, _, offset = geo
    for pose in range(poses):
        line = y_local * cosine[pose, 0] + z_local * sine[pose, 0] + offset[pose, block]
        parts = [jnp.maximum(0.0, peak - jnp.abs(line - r)) for r in rows]
        w_ref[pose * WINDOW : (pose + 1) * WINDOW, :] = jnp.concatenate(parts, axis=0).astype(
            jnp.bfloat16
        )


def fill_turned(t_ref, wide, lanes, block, map_side):
    peak = 0.5 / math.sqrt(map_side)
    local = lax.broadcasted_iota(jnp.int32, (BLOCK, LANES), 0).astype(jnp.float32)
    offset = lanes[pl.ds(block, 1), :]
    for at in range(0, wide.shape[1], LANES):
        span = slice(at, at + LANES)
        along_z = local * wide[1:2, span] + offset[:, span]
        along_y = wide[0:1, span]
        for y in range(BLOCK):
            line = along_z + float(y) * along_y
            t_ref[y * BLOCK : (y + 1) * BLOCK, span] = jnp.maximum(
                0.0, peak - jnp.abs(line)
            ).astype(jnp.bfloat16)


def windows_kernel(poses, map_side, cosine, sine, start, offset, windows):
    count = windows.shape[0]
    for k in range(count):
        index = pl.program_id(0) * count + k
        fill_windows(windows.at[k], (cosine, sine, start, offset), index, poses, map_side)


def turned_kernel(map_side, wide, lanes, turned):
    count = turned.shape[0]
    for k in range(count):
        index = pl.program_id(0) * count + k
        fill_turned(turned.at[k], wide, lanes, index, map_side)


def table_call(kernel, blocks, shape, operands, specs):
    count = math.gcd(blocks, 4)
    return pl.pallas_call(
        kernel,
        grid=(blocks // count,),
        in_specs=specs,
        out_specs=pl.BlockSpec((count, *shape), lambda i: (i, 0, 0)),
        out_shape=jax.ShapeDtypeStruct((blocks, *shape), jnp.bfloat16),
    )(*operands)


def window_table(geo, blocks, poses, map_side):
    return table_call(
        functools.partial(windows_kernel, poses, map_side), blocks,
        (poses * WINDOW, BLOCK * BLOCK), geo, [smem()] * 4,
    )


def turned_table(wide_geo, blocks, poses, map_side):
    return table_call(
        functools.partial(turned_kernel, map_side), blocks,
        (BLOCK * BLOCK, poses * WINDOW), wide_geo, [vmem()] * 2,
    )


def add_projection(outs, prod, start, block, poses):
    share = poses // len(outs)
    for first in range(0, poses, 8):
        group = range(first, min(first + 8, poses))
        places = [
            (outs[pose // share], pose % share, pl.ds(start[pose, block], WINDOW))
            for pose in group
        ]
        values = [out[at, rows, :] for out, at, rows in places]
        for pose, value, (out, at, rows) in zip(group, values, places):
            out[at, rows, :] = value + prod[pose * WINDOW : (pose + 1) * WINDOW]


def first_projection_kernel(
    map_side, poses, cosine, sine, start, offset, dens, pool_t, keep, send, fold_ref, w_ref
):
    step = pl.program_id(0)
    geo = (cosine, sine, start, offset)

    @pl.when(step == 0)
    def _():
        keep[...] = jnp.zeros_like(keep)
        send[...] = jnp.zeros_like(send)

    height, depth, _ = dens.shape
    side = pool_t.shape[1]
    folded = jnp.dot(
        dens[...].reshape(height * depth, map_side), pool_t[...], preferred_element_type=jnp.float32
    )
    fold_ref[...] = folded.astype(jnp.bfloat16).reshape(height, depth, side)
    count = height * depth // (BLOCK * BLOCK)
    for k in range(count):
        row, plane = k // (depth // BLOCK) * BLOCK, k % (depth // BLOCK) * BLOCK
        weights = w_ref.at[k]
        fill_windows(weights, geo, step * count + k, poses, map_side)
        pixels = fold_ref[row : row + BLOCK, plane : plane + BLOCK, :].reshape(-1, side)
        prod = jnp.dot(weights[...], pixels, preferred_element_type=jnp.float32)
        add_projection((keep, send), prod, start, step * count + k, poses)


def first_projection(density, pool_t, geo, poses):
    map_side, depth, _ = density.shape
    side = pool_t.shape[1]
    height = 2 * BLOCK
    half = jax.ShapeDtypeStruct((poses // 2, side, side), jnp.float32)
    return pl.pallas_call(
        functools.partial(first_projection_kernel, map_side, poses),
        grid=(map_side // height,),
        in_specs=[smem(), smem(), smem(), smem(),
                  pl.BlockSpec((height, depth, map_side), lambda i: (i, 0, 0)),
                  vmem()],
        out_specs=[vmem(), vmem(), pl.BlockSpec((height, depth, side), lambda i: (i, 0, 0))],
        out_shape=[half, half, jax.ShapeDtypeStruct((map_side, depth, side), jnp.bfloat16)],
        scratch_shapes=[
            pltpu.VMEM(
                (height * depth // BLOCK**2, poses * WINDOW, BLOCK * BLOCK), jnp.bfloat16
            ),
        ],
        name="first_projection",
    )(*geo, density, pool_t)


def pick_kernel(owned, chips, bins_of, poses_of, classes_of, images, *refs):
    outs, order, filled = refs[:-2], refs[-2], refs[-1]
    groups = len(outs)
    each = outs[0].shape[0]
    side = images.shape[1]
    here, slab = lax.axis_index("bin"), lax.axis_index("slab")
    chip, core = slab // 2, lax.rem(slab, 2)
    lane = lax.broadcasted_iota(jnp.int32, (BLOCK, side), 1)

    def ahead(value, size):
        return jnp.where(value < 0, value + size, value)

    for slot in range(groups * each):
        order[slot] = -1
    for group in range(groups):
        filled[group] = 0
    for n in range(images.shape[0]):
        away = ahead(bins_of[n] - here, groups)
        rank = filled[away]
        filled[away] = rank + 1
        order[away * each + rank] = n
    for group in range(groups):
        for k in range(each):
            source = order[group * each + k]
            image = jnp.maximum(source, 0)
            outs[group][k, 0:side, :] = images[image]
            pose = poses_of[image]
            owner = pose // owned
            across = ahead(lax.rem(owner, 2) - core, 2)
            at = (across * chips + ahead(owner // 2 - chip, chips)) * owned + lax.rem(pose, owned)
            at = jnp.where(source >= 0, at, -1).astype(jnp.float32)
            named = classes_of[image].astype(jnp.float32)
            outs[group][k, side : side + BLOCK, :] = jnp.where(
                lane == 0, at, jnp.where(lane == 1, named, 0.0)
            ).astype(images.dtype)


def pick_images(images, image_bin, image_pose, image_class, owned, chips, groups):
    count, side, _ = images.shape
    each = count // 4
    out = jax.ShapeDtypeStruct((each, side + BLOCK, side), images.dtype)
    return pl.pallas_call(
        functools.partial(pick_kernel, owned, chips),
        in_specs=[smem()] * 3 + [vmem()],
        out_specs=[vmem()] * groups,
        out_shape=[out] * groups,
        scratch_shapes=[
            pltpu.SMEM((groups * each,), jnp.int32),
            pltpu.SMEM((groups,), jnp.int32),
        ],
        name="pick_images",
    )(image_bin, image_pose, image_class, images)


def times_hartley(value, table):
    _, side = value.shape
    high = value.astype(jnp.bfloat16)
    low = (value - high.astype(jnp.float32)).astype(jnp.bfloat16)
    both = jnp.dot(high, table, preferred_element_type=jnp.float32)
    rest = jnp.dot(low, table[:, :side], preferred_element_type=jnp.float32)
    return both[:, :side] + (both[:, side:] + rest)


def spectrum_kernel(groups, each, defocus, table, *refs):
    images, (keep, send, ctf, marks, label, sums, sem) = refs[:groups], refs[groups:]
    half = keep.shape[0]
    side = keep.shape[2]
    poses = 2 * half
    for group in range(groups):
        for k in range(each):
            at = group * each + k
            row = images[group][k, side : side + BLOCK, :].astype(jnp.float32)
            marks[at : at + 1, :] = row[0:1].astype(jnp.int32)
    copy = pltpu.make_async_copy(marks, label, sem)
    copy.start()
    sums[...] = jnp.zeros_like(sums)
    fill_ctf(ctf, defocus)
    hart = table[...]
    lane = lax.broadcasted_iota(jnp.int32, (8, side), 1)
    copy.wait()
    for group in range(groups):
        pixels = images[group][:, 0:side, :].reshape(each * side, side)
        both = jnp.dot(pixels, hart, preferred_element_type=jnp.float32)
        along = (both[:, :side] + both[:, side:]).reshape(each, side, side)
        turned = jnp.concatenate([along[k].T for k in range(each)], axis=0)
        full = times_hartley(turned, hart).reshape(each, side, side)
        for k in range(each):
            pose, kind = label[group * each + k, 0], label[group * each + k, 1]
            pose = jnp.where(pose < 0, poses, pose)
            sums[pose, 0:side, :] += ctf[kind] * full[k]
            sums[pose, side : side + 8, :] += jnp.where(lane == kind, 1.0, 0.0)
    for part, out in enumerate((keep, send)):
        for pose in range(half):
            out[pose, 0:side, :] = sums[part * half + pose, 0:side, :].T
            out[pose, side : side + 8, :] = sums[part * half + pose, side : side + 8, :]


def image_sums(images, defocus, table, poses):
    each, _, side = images[0].shape
    slots = each * len(images)
    half = jax.ShapeDtypeStruct((poses // 2, side + 8, side), jnp.float32)
    return pl.pallas_call(
        functools.partial(spectrum_kernel, len(images), each),
        in_specs=[smem(), vmem()] + [vmem()] * len(images),
        out_specs=[vmem()] * 3,
        out_shape=[half, half, jax.ShapeDtypeStruct((*defocus.shape, side, side), jnp.float32)],
        scratch_shapes=[
            pltpu.VMEM((slots, side), jnp.int32),
            pltpu.SMEM((slots, side), jnp.int32),
            pltpu.VMEM((poses + 1, side + 8, side), jnp.float32),
            pltpu.SemaphoreType.DMA(()),
        ],
        name="image_sums",
    )(defocus, table, *images)


def added(parts):
    return functools.reduce(jnp.add, [part[...].astype(jnp.float32) for part in parts])


def through(values, hart, change):
    owned, side, _ = values.shape

    def turn(rows):
        return jnp.concatenate([rows[k * side : (k + 1) * side].T for k in range(owned)], axis=0)

    full = times_hartley(turn(times_hartley(values.reshape(owned * side, side), hart)), hart)
    parts = [change(k, full[k * side : (k + 1) * side]) for k in range(owned)]
    field = times_hartley(turn(times_hartley(jnp.concatenate(parts, axis=0), hart)), hart)
    return field.reshape(owned, side, side)


def first_filter_kernel(weight, count, ctf, table, *refs):
    proj, totals, (field, residual, gains) = refs[:count], refs[count:-3], refs[-3:]
    _, side, _ = field.shape
    total = added(totals)

    def change(k, value):
        gain = jnp.zeros((side, side), jnp.float32)
        for c in range(ctf.shape[0]):
            gain = gain + total[k, side : side + 1, c : c + 1] * (ctf[c] * ctf[c])
        value = weight * (gain * value - total[k, 0:side, :])
        gains[k] = weight * gain
        residual[k] = value
        return value

    field[...] = through(added(proj), table[...], change).astype(field.dtype)


def first_field(proj, totals, ctf, table, weight, owned):
    side = table.shape[0]
    block = pl.BlockSpec((owned, side, side), lambda i: (0, 0, 0))
    tall = pl.BlockSpec((owned, side + 8, side), lambda i: (0, 0, 0))
    kept = jax.ShapeDtypeStruct((owned, side, side), jnp.float32)
    return pl.pallas_call(
        functools.partial(first_filter_kernel, weight, len(proj)),
        grid=(1,),
        in_specs=[vmem(), vmem()] + [block] * len(proj) + [tall] * len(totals),
        out_specs=[block] * 3,
        out_shape=[jax.ShapeDtypeStruct(kept.shape, jnp.bfloat16), kept, kept],
        name="first_field",
    )(ctf, table, *proj, *totals)


def next_filter_kernel(table, residual, gains, *refs):
    parts, field = refs[:-1], refs[-1]

    def change(k, value):
        return gains[k] * value + residual[k]

    field[...] = through(added(parts), table[...], change).astype(field.dtype)


def next_field(parts, residual, gains, table):
    block = pl.BlockSpec(residual.shape, lambda i: (0, 0, 0))
    return pl.pallas_call(
        next_filter_kernel,
        grid=(1,),
        in_specs=[vmem()] + [block] * (2 + len(parts)),
        out_specs=block,
        out_shape=jax.ShapeDtypeStruct(residual.shape, jnp.bfloat16),
        name="next_field",
    )(table, residual, gains, *parts)


def load_fields(field, fields):
    at = 0
    for part in fields:
        count = part.shape[0]
        field[at : at + count] = part[...].astype(jnp.float32)
        at += count


def gather_windows(f_ref, field, start, block, poses):
    for pose in range(poses):
        f_ref[pose * WINDOW : (pose + 1) * WINDOW, :] = field[
            pose, pl.ds(start[pose, block], WINDOW), :
        ].astype(jnp.bfloat16)


def step_gradient(split_ref, f_ref, field, turned, pool2, start, first_block, poses):
    height, depth, width = split_ref.shape
    for k in range(depth // BLOCK):
        planes = slice(k * BLOCK, (k + 1) * BLOCK)
        gather_windows(f_ref.at[k], field, start, first_block + k, poses)
        back = jnp.dot(turned[k], f_ref[k], preferred_element_type=jnp.float32)
        high = back.astype(jnp.bfloat16)
        low = (back - high.astype(jnp.float32)).astype(jnp.bfloat16)
        split_ref[:, planes, :] = jnp.concatenate([high, low], axis=1).reshape(
            height, BLOCK, width
        )
    return jnp.dot(
        split_ref[...].reshape(height * depth, width),
        pool2[...],
        preferred_element_type=jnp.float32,
    )


def step_kernel(
    map_side, poses, parts, bin_ref, start, sizes, dens, fold, windows, turned, pool2, pool_t, *refs
):
    fields = refs[:parts]
    first, keep, sent, field, f_ref, split_ref, send = refs[parts:]
    step = pl.program_id(0)

    @pl.when(step == 0)
    def _():
        keep[...] = jnp.zeros_like(keep)
        send[...] = jnp.zeros_like(send)
        load_fields(field, fields)

    height, depth, side = fold.shape
    count = depth // BLOCK
    grad = step_gradient(split_ref, f_ref, field, turned, pool2, start, step * count, poses)
    kept = dens[...].reshape(height * depth, map_side).astype(jnp.float32)
    moved = kept - sizes[0] * grad
    first[...] = moved.reshape(height, depth, map_side)
    folded = jnp.dot(moved.astype(jnp.bfloat16), pool_t[...], preferred_element_type=jnp.float32)
    before = fold[...].reshape(height * depth, side).astype(jnp.float32)
    change = folded.astype(jnp.bfloat16).astype(jnp.float32) - before
    high = change.astype(jnp.bfloat16)
    low = (change - high.astype(jnp.float32)).astype(jnp.bfloat16)
    split_ref[...] = jnp.concatenate([high, low], axis=1).reshape(height, depth, 2 * side)
    for k in range(count):
        pixels = split_ref[:, k * BLOCK : (k + 1) * BLOCK, :].reshape(BLOCK * BLOCK, 2 * side)
        prod = jnp.dot(windows[k], pixels, preferred_element_type=jnp.float32)
        prod = prod[:, :side] + prod[:, side:]
        add_projection((keep, send), prod, start, step * count + k, poses)

    @pl.when(step == pl.num_programs(0) - 1)
    def _():
        sent[...] = send[...].astype(sent.dtype)


def take_step(density, fold, fields, start, tables, sizes, bin_index, pool2, pool_t, row_share):
    map_side, depth, _ = density.shape
    side = pool_t.shape[1]
    poses = start.shape[0]
    half = jax.ShapeDtypeStruct((poses // 2, side, side), jnp.float32)
    row_blocks, count = row_share // BLOCK, depth // BLOCK

    def own(width):
        return pl.BlockSpec((BLOCK, depth, width), lambda i, at: (at[0] * row_blocks + i, 0, 0))

    return pl.pallas_call(
        functools.partial(step_kernel, map_side, poses, len(fields)),
        grid_spec=pltpu.PrefetchScalarGridSpec(
            num_scalar_prefetch=1,
            grid=(row_blocks,),
            in_specs=[smem()] * 2
            + [own(map_side), own(side)]
            + [pl.BlockSpec((count, *table.shape[1:]), lambda i, at: (i, 0, 0)) for table in tables]
            + [vmem()] * (2 + len(fields)),
            out_specs=[
                pl.BlockSpec((BLOCK, depth, map_side), lambda i, at: (i, 0, 0)), vmem(), vmem()
            ],
            scratch_shapes=[
                pltpu.VMEM((poses, side, side), jnp.float32),
                pltpu.VMEM((count, poses * WINDOW, side), jnp.bfloat16),
                pltpu.VMEM((BLOCK, depth, 2 * side), jnp.bfloat16),
                pltpu.VMEM(half.shape, jnp.float32),
            ],
        ),
        out_shape=[
            jax.ShapeDtypeStruct((row_share, depth, map_side), jnp.float32),
            half,
            jax.ShapeDtypeStruct(half.shape, jnp.bfloat16),
        ],
        name="take_step",
    )(bin_index.reshape(1), start, sizes, density, fold, *tables, pool2, pool_t, *fields)


def finish_kernel(poses, parts, start, sizes, first, turned, pool2, *refs):
    fields = refs[:parts]
    gradient, refined, field, f_ref, split_ref = refs[parts:]
    step = pl.program_id(0)

    @pl.when(step == 0)
    def _():
        load_fields(field, fields)

    count = first.shape[1] // BLOCK
    grad = step_gradient(split_ref, f_ref, field, turned, pool2, start, step * count, poses)
    grad = grad.reshape(first.shape)
    gradient[...] = grad
    refined[...] = first[...] - sizes[1] * grad


def finish(first, fields, start, turned, sizes, pool2):
    row_share, depth, map_side = first.shape
    side = pool2.shape[0] // 2
    poses = start.shape[0]
    count = depth // BLOCK
    rows = pl.BlockSpec((BLOCK, depth, map_side), lambda i: (i, 0, 0))
    out = jax.ShapeDtypeStruct(first.shape, jnp.float32)
    return pl.pallas_call(
        functools.partial(finish_kernel, poses, len(fields)),
        grid=(row_share // BLOCK,),
        in_specs=[smem()] * 2
        + [rows, pl.BlockSpec((count, *turned.shape[1:]), lambda i: (i, 0, 0))]
        + [vmem()] * (1 + len(fields)),
        out_specs=[rows, rows],
        out_shape=[out, out],
        scratch_shapes=[
            pltpu.VMEM((poses, side, side), jnp.float32),
            pltpu.VMEM((count, poses * WINDOW, side), jnp.bfloat16),
            pltpu.VMEM((BLOCK, depth, 2 * side), jnp.bfloat16),
        ],
        name="finish",
    )(start, sizes, first, turned, pool2, *fields)


def on_device(
    density, images, image_bin, image_pose, image_class, defocus, pose_offset, step_sizes
):
    bins = lax.axis_size("bin")
    slabs = lax.axis_size("slab")
    chips = slabs // 2
    bin_index = lax.axis_index("bin")
    map_side, depth, _ = density.shape
    image_count, side, _ = images.shape
    pose_count = pose_offset.shape[1]
    row_share = map_side // bins
    owned = pose_count // slabs
    weight = 16.0 * pose_count / (image_count * slabs)

    def to_core(value):
        return lax.ppermute(value, "slab", [(s, s ^ 1) for s in range(slabs)])

    def to_chip(value, shift):
        return lax.ppermute(
            value, "slab", [(s, (s + 2 * shift) % slabs) for s in range(slabs)]
        )

    def to_bin(value, shift):
        return lax.ppermute(value, "bin", [(b, (b + shift) % bins) for b in range(bins)])

    picked = pick_images(images, image_bin[:, 0], image_pose, image_class, owned, chips, bins)
    poses = bins * pose_count
    own_geo, geo, wide_geo = make_geometry(
        pose_offset, map_side, side, depth, row_share, chips, owned
    )
    pooling = pool_table(side, map_side).astype(jnp.bfloat16)
    pool_t = jnp.asarray(pooling.T)
    pool2 = jnp.asarray(np.concatenate([pooling, pooling], axis=0))
    table = hartley_table(side)

    picked, own_geo = lax.optimization_barrier((picked, own_geo))
    got_images = [picked[0]]
    for d in range(1, bins):
        got_images.append(to_bin(picked[d], d))

    def reduce_slab(keep, send, sent_as=jnp.float32):
        got = to_core(send)
        each = keep.shape[0] // chips

        def joined(d):
            rows = slice(d * each, (d + 1) * each)
            return (keep[rows] + got[rows].astype(jnp.float32)).astype(sent_as)

        return [keep, got] + [to_chip(joined(d), d) for d in range(1, chips)]

    keep, send, fold = first_projection(density, pool_t, own_geo, pose_count)
    keep, send, defocus = lax.optimization_barrier((keep, send, defocus))
    proj_parts = reduce_slab(keep, send)
    keep, send, ctf = image_sums(got_images, defocus, table, pose_count)
    total_parts = reduce_slab(keep, send)

    def share_field(field, early=(), late=()):
        near = [field] + [to_bin(field, bins - d) for d in range(1, bins)]
        near, early = lax.optimization_barrier((near, early))
        near = jnp.concatenate(near, axis=0)
        across = [to_chip(near, chips - d) for d in range(1, chips)]
        across, late = lax.optimization_barrier((across, late))
        row = [near] + across
        return row + [to_core(part) for part in row], early, late

    field, residual, gains = first_field(proj_parts, total_parts, ctf, table, weight, owned)
    field, geo, wide_geo = lax.optimization_barrier((field, geo, wide_geo))
    blocks = row_share // BLOCK * (depth // BLOCK)
    fields, turned, windows = share_field(
        field,
        turned_table(wide_geo, blocks, poses, map_side),
        window_table(geo, blocks, poses, map_side),
    )
    start = geo[2]
    first, keep, send = take_step(
        density, fold, fields, start, (windows, turned), step_sizes, bin_index, pool2, pool_t,
        row_share,
    )
    parts = reduce_slab(keep, send, jnp.bfloat16)

    def change(d):
        rows = slice(d * owned, (d + 1) * owned)
        return functools.reduce(jnp.add, [part[rows].astype(jnp.float32) for part in parts])

    moved = [to_bin(change(d).astype(jnp.bfloat16), d) for d in range(1, bins)]
    field = next_field(parts + moved, residual, gains, table)
    gradient, refined = finish(first, share_field(field)[0], start, turned, step_sizes, pool2)
    return (gradient, refined)


def solution(mesh):
    return jax.shard_map(
        on_device,
        mesh=mesh,
        in_specs=(
            P("grp", "slab", None),
            P(("grp", "bin", "slab"), None, None),
            P(("grp", "bin", "slab"), None),
            P(("grp", "bin", "slab")),
            P(("grp", "bin", "slab")),
            P("grp"),
            P("grp", None),
            P(),
        ),
        out_specs=(P(("grp", "bin"), "slab", None), P(("grp", "bin"), "slab", None)),
        check_vma=False,
    )
```

```python
import functools
import math

import jax
import jax.numpy as jnp
import numpy as np
from jax import lax
from jax.experimental import pallas as pl
from jax.experimental.pallas import tpu as pltpu
from jax.sharding import PartitionSpec as P


AMP_CONTRAST = 0.1
PHASE_RATE = 60.0
BLOCK = 16
WINDOW = 16
LANES = 128
SMEM = pltpu.SMEM


def vmem():
    return pl.BlockSpec(memory_space=pltpu.VMEM)


def smem():
    return pl.BlockSpec(memory_space=SMEM)


def pool_table(image_side, map_side):
    row_index = np.arange(image_side)[:, None]
    col_index = np.arange(map_side)[None, :]
    return 0.5 * np.maximum(0.0, 1.0 - np.abs(col_index - 2.0 * row_index - 0.5) / 2.0)


def hartley_table(image_side):
    index_row = np.arange(image_side)
    phase_index = index_row[:, None] * index_row[None, :] % image_side
    angle_table = 2.0 * math.pi / image_side * phase_index
    table = (np.cos(angle_table) + np.sin(angle_table)) / math.sqrt(image_side)
    high = table.astype(jnp.bfloat16)
    low = (table - high.astype(np.float64)).astype(jnp.bfloat16)
    return jnp.asarray(np.concatenate([high, low], axis=1))


def fill_ctf(ctf, defocus):
    classes, side, _ = ctf.shape
    row = lax.broadcasted_iota(jnp.int32, (classes, side), 0)
    lane = lax.broadcasted_iota(jnp.int32, (classes, side), 1)
    value = jnp.zeros((classes, side), jnp.float32)
    for c in range(classes):
        value = jnp.where(row == c, defocus[c], value)
    frequency = jnp.where(lane < side // 2, lane, lane - side).astype(jnp.float32) / side
    part = PHASE_RATE * value * (frequency * frequency)
    shifted = part + math.asin(AMP_CONTRAST)
    across = (jnp.cos(part), jnp.sin(part))
    down = jnp.concatenate(
        [
            jnp.sin(shifted),
            jnp.cos(shifted),
            jnp.zeros((side - 2 * classes, side), jnp.float32),
        ],
        axis=0,
    ).T
    for c in range(classes):
        ctf[c] = -(
            down[:, c : c + 1] * across[0][c : c + 1]
            + down[:, classes + c : classes + c + 1] * across[1][c : c + 1]
        )


def block_lines(theta, y_low, z_low, side, map_side):
    middle = map_side / 2.0
    scale = 0.25 / math.sqrt(map_side)
    cosine, sine = jnp.cos(theta), jnp.sin(theta)
    y_part = (y_low.astype(jnp.float32) + (0.5 - middle)) * cosine
    z_part = (z_low.astype(jnp.float32) + (0.5 - middle)) * sine
    least = (
        y_part
        + jnp.minimum(0.0, (BLOCK - 1.0) * cosine)
        + z_part
        + jnp.minimum(0.0, (BLOCK - 1.0) * sine)
    )
    column = jnp.floor((least + (middle - 3.0)) * 0.5).astype(jnp.int32)
    start = jnp.clip(column, 0, side - WINDOW)
    offset = scale * (y_part + z_part - (2.0 * start.astype(jnp.float32) + (1.0 - middle)))
    return cosine * scale, sine * scale, start, offset


def geometry_kernel(
    sizes, offsets, own_cos, own_sin, own_start, own_offset, cosine, sine, start, offset,
    wide, lanes
):
    map_side, side, depth, row_share, bins, chips, owned = sizes
    here, slab = lax.axis_index("bin"), lax.axis_index("slab")
    chip, core = slab // 2, lax.rem(slab, 2)
    first_plane = (chip * 2 + core) * depth
    plane_blocks = depth // BLOCK

    def turn(away, place):
        across, ahead, beyond = away
        bin_at = lax.rem(here + beyond, bins)
        owner = lax.rem(chip + ahead, chips) * 2 + lax.rem(core + across, 2)
        return bin_at.astype(jnp.float32) + offsets[bin_at, owner * owned + place]

    def listed(beyonds):
        return [
            turn((across, ahead, beyond), place)
            for across in range(2)
            for ahead in range(chips)
            for beyond in range(beyonds)
            for place in range(owned)
        ]

    def spread(values, index, shape):
        theta = jnp.zeros(shape, jnp.float32)
        for k, value in enumerate(values):
            theta = jnp.where(index == k, value, theta)
        return math.pi * theta / bins

    def fill(outs, values, first_row):
        shape = outs[0].shape
        row = lax.broadcasted_iota(jnp.int32, shape, 0)
        block = lax.broadcasted_iota(jnp.int32, shape, 1)
        theta = spread(values, row, shape)
        found = block_lines(
            theta,
            first_row + block // plane_blocks * BLOCK,
            first_plane + block % plane_blocks * BLOCK,
            side,
            map_side,
        )
        for out, value in zip(outs, found):
            out[...] = value

    first_row = here * row_share
    values = listed(bins)
    fill((own_cos, own_sin, own_start, own_offset), listed(1), 0)
    fill((cosine, sine, start, offset), values, first_row)
    shape = lanes.shape
    block = lax.broadcasted_iota(jnp.int32, shape, 0)
    lane = lax.broadcasted_iota(jnp.int32, shape, 1)
    along_y, along_z, _, offset_wide = block_lines(
        spread(values, lane // WINDOW, shape),
        first_row + block // plane_blocks * BLOCK,
        first_plane + block % plane_blocks * BLOCK,
        side,
        map_side,
    )
    peak = 0.5 / math.sqrt(map_side)
    lanes[...] = offset_wide - peak * (lane % WINDOW).astype(jnp.float32)
    wide[0:1, :] = along_y[0:1]
    wide[1:2, :] = along_z[0:1]


def make_geometry(pose_offset, map_side, side, depth, row_share, chips, owned):
    bins, pose_count = pose_offset.shape
    poses = bins * pose_count

    def tables(count, blocks):
        shape = (count, -(-blocks // LANES) * LANES)
        return [jax.ShapeDtypeStruct(shape, t) for t in (jnp.float32,) * 2] + [
            jax.ShapeDtypeStruct(shape, jnp.int32),
            jax.ShapeDtypeStruct(shape, jnp.float32),
        ]

    plane_blocks = depth // BLOCK
    blocks = row_share // BLOCK * plane_blocks
    shapes = (
        tables(pose_count, map_side // BLOCK * plane_blocks)
        + tables(poses, blocks)
        + [
            jax.ShapeDtypeStruct((2, poses * WINDOW), jnp.float32),
            jax.ShapeDtypeStruct((blocks, poses * WINDOW), jnp.float32),
        ]
    )
    sizes = (map_side, side, depth, row_share, bins, chips, owned)
    out = pl.pallas_call(
        functools.partial(geometry_kernel, sizes),
        in_specs=[smem()],
        out_specs=[vmem()] * len(shapes),
        out_shape=shapes,
        name="geometry",
    )(pose_offset)
    return out[:4], out[4:8], out[8:]


def fill_windows(w_ref, geo, block, poses, map_side):
    lane = lax.broadcasted_iota(jnp.int32, (8, BLOCK * BLOCK), 1)
    row = lax.broadcasted_iota(jnp.int32, (8, BLOCK * BLOCK), 0).astype(jnp.float32)
    y_local = (lane // BLOCK).astype(jnp.float32)
    z_local = (lane % BLOCK).astype(jnp.float32)
    peak = 0.5 / math.sqrt(map_side)
    rows = [peak * (row + 8.0 * k) for k in range(WINDOW // 8)]
    cosine, sine, _, offset = geo
    for pose in range(poses):
        line = y_local * cosine[pose, 0] + z_local * sine[pose, 0] + offset[pose, block]
        parts = [jnp.maximum(0.0, peak - jnp.abs(line - r)) for r in rows]
        w_ref[pose * WINDOW : (pose + 1) * WINDOW, :] = jnp.concatenate(parts, axis=0).astype(
            jnp.bfloat16
        )


def fill_turned(t_ref, wide, lanes, block, map_side):
    peak = 0.5 / math.sqrt(map_side)
    local = lax.broadcasted_iota(jnp.int32, (BLOCK, LANES), 0).astype(jnp.float32)
    offset = lanes[pl.ds(block, 1), :]
    for at in range(0, wide.shape[1], LANES):
        span = slice(at, at + LANES)
        along_z = local * wide[1:2, span] + offset[:, span]
        along_y = wide[0:1, span]
        for y in range(BLOCK):
            line = along_z + float(y) * along_y
            t_ref[y * BLOCK : (y + 1) * BLOCK, span] = jnp.maximum(
                0.0, peak - jnp.abs(line)
            ).astype(jnp.bfloat16)


def windows_kernel(poses, map_side, cosine, sine, start, offset, windows):
    count = windows.shape[0]
    for k in range(count):
        index = pl.program_id(0) * count + k
        fill_windows(windows.at[k], (cosine, sine, start, offset), index, poses, map_side)


def turned_kernel(map_side, wide, lanes, turned):
    count = turned.shape[0]
    for k in range(count):
        index = pl.program_id(0) * count + k
        fill_turned(turned.at[k], wide, lanes, index, map_side)


def table_call(kernel, blocks, shape, operands, specs):
    count = math.gcd(blocks, 4)
    return pl.pallas_call(
        kernel,
        grid=(blocks // count,),
        in_specs=specs,
        out_specs=pl.BlockSpec((count, *shape), lambda i: (i, 0, 0)),
        out_shape=jax.ShapeDtypeStruct((blocks, *shape), jnp.bfloat16),
    )(*operands)


def window_table(geo, blocks, poses, map_side):
    return table_call(
        functools.partial(windows_kernel, poses, map_side), blocks,
        (poses * WINDOW, BLOCK * BLOCK), geo, [smem()] * 4,
    )


def turned_table(wide_geo, blocks, poses, map_side):
    return table_call(
        functools.partial(turned_kernel, map_side), blocks,
        (BLOCK * BLOCK, poses * WINDOW), wide_geo, [vmem()] * 2,
    )


def add_projection(outs, prod, start, block, poses):
    share = poses // len(outs)
    for first in range(0, poses, 8):
        group = range(first, min(first + 8, poses))
        places = [
            (outs[pose // share], pose % share, pl.ds(start[pose, block], WINDOW))
            for pose in group
        ]
        values = [out[at, rows, :] for out, at, rows in places]
        for pose, value, (out, at, rows) in zip(group, values, places):
            out[at, rows, :] = value + prod[pose * WINDOW : (pose + 1) * WINDOW]


def first_projection_kernel(
    map_side, poses, cosine, sine, start, offset, dens, pool_t, keep, send, fold_ref, w_ref
):
    step = pl.program_id(0)
    geo = (cosine, sine, start, offset)

    @pl.when(step == 0)
    def _():
        keep[...] = jnp.zeros_like(keep)
        send[...] = jnp.zeros_like(send)

    height, depth, _ = dens.shape
    side = pool_t.shape[1]
    folded = jnp.dot(
        dens[...].reshape(height * depth, map_side), pool_t[...], preferred_element_type=jnp.float32
    )
    fold_ref[...] = folded.astype(jnp.bfloat16).reshape(height, depth, side)
    count = height * depth // (BLOCK * BLOCK)
    for k in range(count):
        row, plane = k // (depth // BLOCK) * BLOCK, k % (depth // BLOCK) * BLOCK
        weights = w_ref.at[k]
        fill_windows(weights, geo, step * count + k, poses, map_side)
        pixels = fold_ref[row : row + BLOCK, plane : plane + BLOCK, :].reshape(-1, side)
        prod = jnp.dot(weights[...], pixels, preferred_element_type=jnp.float32)
        add_projection((keep, send), prod, start, step * count + k, poses)


def first_projection(density, pool_t, geo, poses):
    map_side, depth, _ = density.shape
    side = pool_t.shape[1]
    height = 2 * BLOCK
    half = jax.ShapeDtypeStruct((poses // 2, side, side), jnp.float32)
    return pl.pallas_call(
        functools.partial(first_projection_kernel, map_side, poses),
        grid=(map_side // height,),
        in_specs=[smem(), smem(), smem(), smem(),
                  pl.BlockSpec((height, depth, map_side), lambda i: (i, 0, 0)),
                  vmem()],
        out_specs=[vmem(), vmem(), pl.BlockSpec((height, depth, side), lambda i: (i, 0, 0))],
        out_shape=[half, half, jax.ShapeDtypeStruct((map_side, depth, side), jnp.bfloat16)],
        scratch_shapes=[
            pltpu.VMEM(
                (height * depth // BLOCK**2, poses * WINDOW, BLOCK * BLOCK), jnp.bfloat16
            ),
        ],
        name="first_projection",
    )(*geo, density, pool_t)


def pick_kernel(owned, chips, bins_of, poses_of, classes_of, images, *refs):
    outs, order, filled = refs[:-2], refs[-2], refs[-1]
    groups = len(outs)
    each = outs[0].shape[0]
    side = images.shape[1]
    here, slab = lax.axis_index("bin"), lax.axis_index("slab")
    chip, core = slab // 2, lax.rem(slab, 2)
    lane = lax.broadcasted_iota(jnp.int32, (BLOCK, side), 1)

    def ahead(value, size):
        return jnp.where(value < 0, value + size, value)

    for slot in range(groups * each):
        order[slot] = -1
    for group in range(groups):
        filled[group] = 0
    for n in range(images.shape[0]):
        away = ahead(bins_of[n] - here, groups)
        rank = filled[away]
        filled[away] = rank + 1
        order[away * each + rank] = n
    for group in range(groups):
        for k in range(each):
            source = order[group * each + k]
            image = jnp.maximum(source, 0)
            outs[group][k, 0:side, :] = images[image]
            pose = poses_of[image]
            owner = pose // owned
            across = ahead(lax.rem(owner, 2) - core, 2)
            at = (across * chips + ahead(owner // 2 - chip, chips)) * owned + lax.rem(pose, owned)
            at = jnp.where(source >= 0, at, -1).astype(jnp.float32)
            named = classes_of[image].astype(jnp.float32)
            outs[group][k, side : side + BLOCK, :] = jnp.where(
                lane == 0, at, jnp.where(lane == 1, named, 0.0)
            ).astype(images.dtype)


def pick_images(images, image_bin, image_pose, image_class, owned, chips, groups):
    count, side, _ = images.shape
    each = count // 4
    out = jax.ShapeDtypeStruct((each, side + BLOCK, side), images.dtype)
    return pl.pallas_call(
        functools.partial(pick_kernel, owned, chips),
        in_specs=[smem()] * 3 + [vmem()],
        out_specs=[vmem()] * groups,
        out_shape=[out] * groups,
        scratch_shapes=[
            pltpu.SMEM((groups * each,), jnp.int32),
            pltpu.SMEM((groups,), jnp.int32),
        ],
        name="pick_images",
    )(image_bin, image_pose, image_class, images)


def times_hartley(value, table):
    _, side = value.shape
    high = value.astype(jnp.bfloat16)
    low = (value - high.astype(jnp.float32)).astype(jnp.bfloat16)
    both = jnp.dot(high, table, preferred_element_type=jnp.float32)
    rest = jnp.dot(low, table[:, :side], preferred_element_type=jnp.float32)
    return both[:, :side] + (both[:, side:] + rest)


def spectrum_kernel(groups, each, defocus, table, *refs):
    images, (keep, send, ctf, marks, label, sums, sem) = refs[:groups], refs[groups:]
    half = keep.shape[0]
    side = keep.shape[2]
    poses = 2 * half
    for group in range(groups):
        for k in range(each):
            at = group * each + k
            row = images[group][k, side : side + BLOCK, :].astype(jnp.float32)
            marks[at : at + 1, :] = row[0:1].astype(jnp.int32)
    copy = pltpu.make_async_copy(marks, label, sem)
    copy.start()
    sums[...] = jnp.zeros_like(sums)
    fill_ctf(ctf, defocus)
    hart = table[...]
    lane = lax.broadcasted_iota(jnp.int32, (8, side), 1)
    copy.wait()
    for group in range(groups):
        pixels = images[group][:, 0:side, :].reshape(each * side, side)
        both = jnp.dot(pixels, hart, preferred_element_type=jnp.float32)
        along = (both[:, :side] + both[:, side:]).reshape(each, side, side)
        turned = jnp.concatenate([along[k].T for k in range(each)], axis=0)
        full = times_hartley(turned, hart).reshape(each, side, side)
        for k in range(each):
            pose, kind = label[group * each + k, 0], label[group * each + k, 1]
            pose = jnp.where(pose < 0, poses, pose)
            sums[pose, 0:side, :] += ctf[kind] * full[k]
            sums[pose, side : side + 8, :] += jnp.where(lane == kind, 1.0, 0.0)
    for part, out in enumerate((keep, send)):
        for pose in range(half):
            out[pose, 0:side, :] = sums[part * half + pose, 0:side, :].T
            out[pose, side : side + 8, :] = sums[part * half + pose, side : side + 8, :]


def image_sums(images, defocus, table, poses):
    each, _, side = images[0].shape
    slots = each * len(images)
    half = jax.ShapeDtypeStruct((poses // 2, side + 8, side), jnp.float32)
    return pl.pallas_call(
        functools.partial(spectrum_kernel, len(images), each),
        in_specs=[smem(), vmem()] + [vmem()] * len(images),
        out_specs=[vmem()] * 3,
        out_shape=[half, half, jax.ShapeDtypeStruct((*defocus.shape, side, side), jnp.float32)],
        scratch_shapes=[
            pltpu.VMEM((slots, side), jnp.int32),
            pltpu.SMEM((slots, side), jnp.int32),
            pltpu.VMEM((poses + 1, side + 8, side), jnp.float32),
            pltpu.SemaphoreType.DMA(()),
        ],
        name="image_sums",
    )(defocus, table, *images)


def added(parts):
    return functools.reduce(jnp.add, [part[...].astype(jnp.float32) for part in parts])


def through(values, hart, change):
    owned, side, _ = values.shape

    def turn(rows):
        return jnp.concatenate([rows[k * side : (k + 1) * side].T for k in range(owned)], axis=0)

    full = times_hartley(turn(times_hartley(values.reshape(owned * side, side), hart)), hart)
    parts = [change(k, full[k * side : (k + 1) * side]) for k in range(owned)]
    field = times_hartley(turn(times_hartley(jnp.concatenate(parts, axis=0), hart)), hart)
    return field.reshape(owned, side, side)


def first_filter_kernel(weight, count, ctf, table, *refs):
    proj, totals, (field, residual, gains) = refs[:count], refs[count:-3], refs[-3:]
    _, side, _ = field.shape
    total = added(totals)

    def change(k, value):
        gain = jnp.zeros((side, side), jnp.float32)
        for c in range(ctf.shape[0]):
            gain = gain + total[k, side : side + 1, c : c + 1] * (ctf[c] * ctf[c])
        value = weight * (gain * value - total[k, 0:side, :])
        gains[k] = weight * gain
        residual[k] = value
        return value

    field[...] = through(added(proj), table[...], change).astype(field.dtype)


def first_field(proj, totals, ctf, table, weight, owned):
    side = table.shape[0]
    block = pl.BlockSpec((owned, side, side), lambda i: (0, 0, 0))
    tall = pl.BlockSpec((owned, side + 8, side), lambda i: (0, 0, 0))
    kept = jax.ShapeDtypeStruct((owned, side, side), jnp.float32)
    return pl.pallas_call(
        functools.partial(first_filter_kernel, weight, len(proj)),
        grid=(1,),
        in_specs=[vmem(), vmem()] + [block] * len(proj) + [tall] * len(totals),
        out_specs=[block] * 3,
        out_shape=[jax.ShapeDtypeStruct(kept.shape, jnp.bfloat16), kept, kept],
        name="first_field",
    )(ctf, table, *proj, *totals)


def next_filter_kernel(table, residual, gains, *refs):
    parts, field = refs[:-1], refs[-1]

    def change(k, value):
        return gains[k] * value + residual[k]

    field[...] = through(added(parts), table[...], change).astype(field.dtype)


def next_field(parts, residual, gains, table):
    block = pl.BlockSpec(residual.shape, lambda i: (0, 0, 0))
    return pl.pallas_call(
        next_filter_kernel,
        grid=(1,),
        in_specs=[vmem()] + [block] * (2 + len(parts)),
        out_specs=block,
        out_shape=jax.ShapeDtypeStruct(residual.shape, jnp.bfloat16),
        name="next_field",
    )(table, residual, gains, *parts)


def load_fields(field, fields):
    at = 0
    for part in fields:
        count = part.shape[0]
        field[at : at + count] = part[...].astype(jnp.float32)
        at += count


def gather_windows(f_ref, field, start, block, poses):
    for pose in range(poses):
        f_ref[pose * WINDOW : (pose + 1) * WINDOW, :] = field[
            pose, pl.ds(start[pose, block], WINDOW), :
        ].astype(jnp.bfloat16)


def step_gradient(split_ref, f_ref, field, turned, pool2, start, first_block, poses):
    height, depth, width = split_ref.shape
    for k in range(depth // BLOCK):
        planes = slice(k * BLOCK, (k + 1) * BLOCK)
        gather_windows(f_ref.at[k], field, start, first_block + k, poses)
        back = jnp.dot(turned[k], f_ref[k], preferred_element_type=jnp.float32)
        high = back.astype(jnp.bfloat16)
        low = (back - high.astype(jnp.float32)).astype(jnp.bfloat16)
        split_ref[:, planes, :] = jnp.concatenate([high, low], axis=1).reshape(
            height, BLOCK, width
        )
    return jnp.dot(
        split_ref[...].reshape(height * depth, width),
        pool2[...],
        preferred_element_type=jnp.float32,
    )


def step_kernel(
    map_side, poses, parts, bin_ref, start, sizes, dens, fold, windows, turned, pool2, pool_t, *refs
):
    fields = refs[:parts]
    first, keep, sent, field, f_ref, split_ref, send = refs[parts:]
    step = pl.program_id(0)

    @pl.when(step == 0)
    def _():
        keep[...] = jnp.zeros_like(keep)
        send[...] = jnp.zeros_like(send)
        load_fields(field, fields)

    height, depth, side = fold.shape
    count = depth // BLOCK
    grad = step_gradient(split_ref, f_ref, field, turned, pool2, start, step * count, poses)
    kept = dens[...].reshape(height * depth, map_side).astype(jnp.float32)
    moved = kept - sizes[0] * grad
    first[...] = moved.reshape(height, depth, map_side)
    folded = jnp.dot(moved.astype(jnp.bfloat16), pool_t[...], preferred_element_type=jnp.float32)
    before = fold[...].reshape(height * depth, side).astype(jnp.float32)
    change = folded.astype(jnp.bfloat16).astype(jnp.float32) - before
    high = change.astype(jnp.bfloat16)
    low = (change - high.astype(jnp.float32)).astype(jnp.bfloat16)
    split_ref[...] = jnp.concatenate([high, low], axis=1).reshape(height, depth, 2 * side)
    for k in range(count):
        pixels = split_ref[:, k * BLOCK : (k + 1) * BLOCK, :].reshape(BLOCK * BLOCK, 2 * side)
        prod = jnp.dot(windows[k], pixels, preferred_element_type=jnp.float32)
        prod = prod[:, :side] + prod[:, side:]
        add_projection((keep, send), prod, start, step * count + k, poses)

    @pl.when(step == pl.num_programs(0) - 1)
    def _():
        sent[...] = send[...].astype(sent.dtype)


def take_step(density, fold, fields, start, tables, sizes, bin_index, pool2, pool_t, row_share):
    map_side, depth, _ = density.shape
    side = pool_t.shape[1]
    poses = start.shape[0]
    half = jax.ShapeDtypeStruct((poses // 2, side, side), jnp.float32)
    row_blocks, count = row_share // BLOCK, depth // BLOCK

    def own(width):
        return pl.BlockSpec((BLOCK, depth, width), lambda i, at: (at[0] * row_blocks + i, 0, 0))

    return pl.pallas_call(
        functools.partial(step_kernel, map_side, poses, len(fields)),
        grid_spec=pltpu.PrefetchScalarGridSpec(
            num_scalar_prefetch=1,
            grid=(row_blocks,),
            in_specs=[smem()] * 2
            + [own(map_side), own(side)]
            + [pl.BlockSpec((count, *table.shape[1:]), lambda i, at: (i, 0, 0)) for table in tables]
            + [vmem()] * (2 + len(fields)),
            out_specs=[
                pl.BlockSpec((BLOCK, depth, map_side), lambda i, at: (i, 0, 0)), vmem(), vmem()
            ],
            scratch_shapes=[
                pltpu.VMEM((poses, side, side), jnp.float32),
                pltpu.VMEM((count, poses * WINDOW, side), jnp.bfloat16),
                pltpu.VMEM((BLOCK, depth, 2 * side), jnp.bfloat16),
                pltpu.VMEM(half.shape, jnp.float32),
            ],
        ),
        out_shape=[
            jax.ShapeDtypeStruct((row_share, depth, map_side), jnp.float32),
            half,
            jax.ShapeDtypeStruct(half.shape, jnp.bfloat16),
        ],
        name="take_step",
    )(bin_index.reshape(1), start, sizes, density, fold, *tables, pool2, pool_t, *fields)


def finish_kernel(poses, parts, start, sizes, first, turned, pool2, *refs):
    fields = refs[:parts]
    gradient, refined, field, f_ref, split_ref = refs[parts:]
    step = pl.program_id(0)

    @pl.when(step == 0)
    def _():
        load_fields(field, fields)

    count = first.shape[1] // BLOCK
    grad = step_gradient(split_ref, f_ref, field, turned, pool2, start, step * count, poses)
    grad = grad.reshape(first.shape)
    gradient[...] = grad
    refined[...] = first[...] - sizes[1] * grad


def finish(first, fields, start, turned, sizes, pool2):
    row_share, depth, map_side = first.shape
    side = pool2.shape[0] // 2
    poses = start.shape[0]
    count = depth // BLOCK
    rows = pl.BlockSpec((BLOCK, depth, map_side), lambda i: (i, 0, 0))
    out = jax.ShapeDtypeStruct(first.shape, jnp.float32)
    return pl.pallas_call(
        functools.partial(finish_kernel, poses, len(fields)),
        grid=(row_share // BLOCK,),
        in_specs=[smem()] * 2
        + [rows, pl.BlockSpec((count, *turned.shape[1:]), lambda i: (i, 0, 0))]
        + [vmem()] * (1 + len(fields)),
        out_specs=[rows, rows],
        out_shape=[out, out],
        scratch_shapes=[
            pltpu.VMEM((poses, side, side), jnp.float32),
            pltpu.VMEM((count, poses * WINDOW, side), jnp.bfloat16),
            pltpu.VMEM((BLOCK, depth, 2 * side), jnp.bfloat16),
        ],
        name="finish",
    )(start, sizes, first, turned, pool2, *fields)


def on_device(
    density, images, image_bin, image_pose, image_class, defocus, pose_offset, step_sizes
):
    bins = lax.axis_size("bin")
    slabs = lax.axis_size("slab")
    chips = slabs // 2
    bin_index = lax.axis_index("bin")
    map_side, depth, _ = density.shape
    image_count, side, _ = images.shape
    pose_count = pose_offset.shape[1]
    row_share = map_side // bins
    owned = pose_count // slabs
    weight = 16.0 * pose_count / (image_count * slabs)

    def to_core(value):
        return lax.ppermute(value, "slab", [(s, s ^ 1) for s in range(slabs)])

    def to_chip(value, shift):
        return lax.ppermute(
            value, "slab", [(s, (s + 2 * shift) % slabs) for s in range(slabs)]
        )

    def to_bin(value, shift):
        return lax.ppermute(value, "bin", [(b, (b + shift) % bins) for b in range(bins)])

    picked = pick_images(images, image_bin[:, 0], image_pose, image_class, owned, chips, bins)
    poses = bins * pose_count
    own_geo, geo, wide_geo = make_geometry(
        pose_offset, map_side, side, depth, row_share, chips, owned
    )
    pooling = pool_table(side, map_side).astype(jnp.bfloat16)
    pool_t = jnp.asarray(pooling.T)
    pool2 = jnp.asarray(np.concatenate([pooling, pooling], axis=0))
    table = hartley_table(side)

    picked, own_geo = lax.optimization_barrier((picked, own_geo))
    got_images = [picked[0]]
    for d in range(1, bins):
        got_images.append(to_bin(picked[d], d))

    def reduce_slab(keep, send, sent_as=jnp.float32):
        got = to_core(send)
        each = keep.shape[0] // chips

        def joined(d):
            rows = slice(d * each, (d + 1) * each)
            return (keep[rows] + got[rows].astype(jnp.float32)).astype(sent_as)

        return [keep, got] + [to_chip(joined(d), d) for d in range(1, chips)]

    keep, send, fold = first_projection(density, pool_t, own_geo, pose_count)
    keep, send, defocus = lax.optimization_barrier((keep, send, defocus))
    proj_parts = reduce_slab(keep, send)
    keep, send, ctf = image_sums(got_images, defocus, table, pose_count)
    total_parts = reduce_slab(keep, send)

    def share_field(field, meanwhile=()):
        near = [field] + [to_bin(field, bins - d) for d in range(1, bins)]
        near = jnp.concatenate(near, axis=0)
        across = [to_chip(near, chips - d) for d in range(1, chips)]
        across, meanwhile = lax.optimization_barrier((across, meanwhile))
        row = [near] + across
        return row + [to_core(part) for part in row], meanwhile

    blocks = row_share // BLOCK * (depth // BLOCK)
    turned = turned_table(wide_geo, blocks, poses, map_side)

    field, residual, gains = first_field(proj_parts, total_parts, ctf, table, weight, owned)
    field, geo = lax.optimization_barrier((field, geo))
    fields, windows = share_field(field, window_table(geo, blocks, poses, map_side))
    start = geo[2]
    first, keep, send = take_step(
        density, fold, fields, start, (windows, turned), step_sizes, bin_index, pool2, pool_t,
        row_share,
    )
    got = to_core(send)
    whole = bins * owned

    def joined(chip_on, low, high):
        rows = slice(chip_on * whole + low * owned, chip_on * whole + high * owned)
        return keep[rows] + got[rows].astype(jnp.float32)

    def cross(low, high):
        return [to_chip(joined(d, low, high).astype(jnp.bfloat16), d) for d in range(1, chips)]

    def block_of(d, low, across):
        rows = slice((d - low) * owned, (d - low + 1) * owned)
        value = functools.reduce(
            jnp.add, [part[rows].astype(jnp.float32) for part in across], joined(0, d, d + 1)
        )
        return value.astype(jnp.bfloat16)

    half = bins // 2
    far = cross(half, bins)
    near = cross(0, half)
    leaving = [block_of(d, half, far) for d in range(half, bins)]
    moved = [to_bin(value, half + k) for k, value in enumerate(leaving)]
    near, _ = lax.optimization_barrier((near, leaving))
    moved += [to_bin(block_of(d, 0, near), d) for d in range(1, half)]
    parts = [keep, got] + near
    field = next_field(parts + moved, residual, gains, table)
    gradient, refined = finish(first, share_field(field)[0], start, turned, step_sizes, pool2)
    return (gradient, refined)


def solution(mesh):
    return jax.shard_map(
        on_device,
        mesh=mesh,
        in_specs=(
            P("grp", "slab", None),
            P(("grp", "bin", "slab"), None, None),
            P(("grp", "bin", "slab"), None),
            P(("grp", "bin", "slab")),
            P(("grp", "bin", "slab")),
            P("grp"),
            P("grp", None),
            P(),
        ),
        out_specs=(P(("grp", "bin"), "slab", None), P(("grp", "bin"), "slab", None)),
        check_vma=False,
    )
```

```python
import functools
import math

import jax
import jax.numpy as jnp
import numpy as np
from jax import lax
from jax.experimental import pallas as pl
from jax.experimental.pallas import tpu as pltpu
from jax.sharding import PartitionSpec as P


AMP_CONTRAST = 0.1
PHASE_RATE = 60.0
BLOCK = 16
WINDOW = 16
LANES = 128
SMEM = pltpu.SMEM


def vmem():
    return pl.BlockSpec(memory_space=pltpu.VMEM)


def smem():
    return pl.BlockSpec(memory_space=SMEM)


def pool_table(image_side, map_side):
    row_index = np.arange(image_side)[:, None]
    col_index = np.arange(map_side)[None, :]
    return 0.5 * np.maximum(0.0, 1.0 - np.abs(col_index - 2.0 * row_index - 0.5) / 2.0)


def hartley_table(image_side):
    index_row = np.arange(image_side)
    phase_index = index_row[:, None] * index_row[None, :] % image_side
    angle_table = 2.0 * math.pi / image_side * phase_index
    table = (np.cos(angle_table) + np.sin(angle_table)) / math.sqrt(image_side)
    high = table.astype(jnp.bfloat16)
    low = (table - high.astype(np.float64)).astype(jnp.bfloat16)
    return jnp.asarray(np.concatenate([high, low], axis=1))


def fill_ctf(ctf, defocus):
    classes, side, _ = ctf.shape
    row = lax.broadcasted_iota(jnp.int32, (classes, side), 0)
    lane = lax.broadcasted_iota(jnp.int32, (classes, side), 1)
    value = jnp.zeros((classes, side), jnp.float32)
    for c in range(classes):
        value = jnp.where(row == c, defocus[c], value)
    frequency = jnp.where(lane < side // 2, lane, lane - side).astype(jnp.float32) / side
    part = PHASE_RATE * value * (frequency * frequency)
    shifted = part + math.asin(AMP_CONTRAST)
    across = (jnp.cos(part), jnp.sin(part))
    down = jnp.concatenate(
        [
            jnp.sin(shifted),
            jnp.cos(shifted),
            jnp.zeros((side - 2 * classes, side), jnp.float32),
        ],
        axis=0,
    ).T
    for c in range(classes):
        ctf[c] = -(
            down[:, c : c + 1] * across[0][c : c + 1]
            + down[:, classes + c : classes + c + 1] * across[1][c : c + 1]
        )


def block_lines(theta, y_low, z_low, side, map_side):
    middle = map_side / 2.0
    scale = 0.25 / math.sqrt(map_side)
    cosine, sine = jnp.cos(theta), jnp.sin(theta)
    y_part = (y_low.astype(jnp.float32) + (0.5 - middle)) * cosine
    z_part = (z_low.astype(jnp.float32) + (0.5 - middle)) * sine
    least = (
        y_part
        + jnp.minimum(0.0, (BLOCK - 1.0) * cosine)
        + z_part
        + jnp.minimum(0.0, (BLOCK - 1.0) * sine)
    )
    column = jnp.floor((least + (middle - 3.0)) * 0.5).astype(jnp.int32)
    start = jnp.clip(column, 0, side - WINDOW)
    offset = scale * (y_part + z_part - (2.0 * start.astype(jnp.float32) + (1.0 - middle)))
    return cosine * scale, sine * scale, start, offset


def geometry_kernel(
    sizes, offsets, own_cos, own_sin, own_start, own_offset, cosine, sine, start, offset,
    wide, lanes
):
    map_side, side, depth, row_share, bins, chips, owned = sizes
    here, slab = lax.axis_index("bin"), lax.axis_index("slab")
    chip, core = slab // 2, lax.rem(slab, 2)
    first_plane = (chip * 2 + core) * depth
    plane_blocks = depth // BLOCK

    def turn(away, place):
        across, ahead, beyond = away
        bin_at = lax.rem(here + beyond, bins)
        owner = lax.rem(chip + ahead, chips) * 2 + lax.rem(core + across, 2)
        return bin_at.astype(jnp.float32) + offsets[bin_at, owner * owned + place]

    def listed(beyonds):
        return [
            turn((across, ahead, beyond), place)
            for across in range(2)
            for ahead in range(chips)
            for beyond in range(beyonds)
            for place in range(owned)
        ]

    def spread(values, index, shape):
        theta = jnp.zeros(shape, jnp.float32)
        for k, value in enumerate(values):
            theta = jnp.where(index == k, value, theta)
        return math.pi * theta / bins

    def fill(outs, values, first_row):
        shape = outs[0].shape
        row = lax.broadcasted_iota(jnp.int32, shape, 0)
        block = lax.broadcasted_iota(jnp.int32, shape, 1)
        theta = spread(values, row, shape)
        found = block_lines(
            theta,
            first_row + block // plane_blocks * BLOCK,
            first_plane + block % plane_blocks * BLOCK,
            side,
            map_side,
        )
        for out, value in zip(outs, found):
            out[...] = value

    first_row = here * row_share
    values = listed(bins)
    fill((own_cos, own_sin, own_start, own_offset), listed(1), 0)
    fill((cosine, sine, start, offset), values, first_row)
    shape = lanes.shape
    block = lax.broadcasted_iota(jnp.int32, shape, 0)
    lane = lax.broadcasted_iota(jnp.int32, shape, 1)
    along_y, along_z, _, offset_wide = block_lines(
        spread(values, lane // WINDOW, shape),
        first_row + block // plane_blocks * BLOCK,
        first_plane + block % plane_blocks * BLOCK,
        side,
        map_side,
    )
    peak = 0.5 / math.sqrt(map_side)
    lanes[...] = offset_wide - peak * (lane % WINDOW).astype(jnp.float32)
    wide[0:1, :] = along_y[0:1]
    wide[1:2, :] = along_z[0:1]


def make_geometry(pose_offset, map_side, side, depth, row_share, chips, owned):
    bins, pose_count = pose_offset.shape
    poses = bins * pose_count

    def tables(count, blocks):
        shape = (count, -(-blocks // LANES) * LANES)
        return [jax.ShapeDtypeStruct(shape, t) for t in (jnp.float32,) * 2] + [
            jax.ShapeDtypeStruct(shape, jnp.int32),
            jax.ShapeDtypeStruct(shape, jnp.float32),
        ]

    plane_blocks = depth // BLOCK
    blocks = row_share // BLOCK * plane_blocks
    shapes = (
        tables(pose_count, map_side // BLOCK * plane_blocks)
        + tables(poses, blocks)
        + [
            jax.ShapeDtypeStruct((2, poses * WINDOW), jnp.float32),
            jax.ShapeDtypeStruct((blocks, poses * WINDOW), jnp.float32),
        ]
    )
    sizes = (map_side, side, depth, row_share, bins, chips, owned)
    out = pl.pallas_call(
        functools.partial(geometry_kernel, sizes),
        in_specs=[smem()],
        out_specs=[vmem()] * len(shapes),
        out_shape=shapes,
        name="geometry",
    )(pose_offset)
    return out[:4], out[4:8], out[8:]


def fill_windows(w_ref, geo, block, poses, map_side):
    lane = lax.broadcasted_iota(jnp.int32, (8, BLOCK * BLOCK), 1)
    row = lax.broadcasted_iota(jnp.int32, (8, BLOCK * BLOCK), 0).astype(jnp.float32)
    y_local = (lane // BLOCK).astype(jnp.float32)
    z_local = (lane % BLOCK).astype(jnp.float32)
    peak = 0.5 / math.sqrt(map_side)
    rows = [peak * (row + 8.0 * k) for k in range(WINDOW // 8)]
    cosine, sine, _, offset = geo
    for pose in range(poses):
        line = y_local * cosine[pose, 0] + z_local * sine[pose, 0] + offset[pose, block]
        parts = [jnp.maximum(0.0, peak - jnp.abs(line - r)) for r in rows]
        w_ref[pose * WINDOW : (pose + 1) * WINDOW, :] = jnp.concatenate(parts, axis=0).astype(
            jnp.bfloat16
        )


def fill_turned(t_ref, wide, lanes, block, map_side):
    peak = 0.5 / math.sqrt(map_side)
    local = lax.broadcasted_iota(jnp.int32, (BLOCK, LANES), 0).astype(jnp.float32)
    offset = lanes[pl.ds(block, 1), :]
    for at in range(0, wide.shape[1], LANES):
        span = slice(at, at + LANES)
        along_z = local * wide[1:2, span] + offset[:, span]
        along_y = wide[0:1, span]
        for y in range(BLOCK):
            line = along_z + float(y) * along_y
            t_ref[y * BLOCK : (y + 1) * BLOCK, span] = jnp.maximum(
                0.0, peak - jnp.abs(line)
            ).astype(jnp.bfloat16)


def windows_kernel(poses, map_side, cosine, sine, start, offset, windows):
    count = windows.shape[0]
    for k in range(count):
        index = pl.program_id(0) * count + k
        fill_windows(windows.at[k], (cosine, sine, start, offset), index, poses, map_side)


def turned_kernel(map_side, wide, lanes, turned):
    count = turned.shape[0]
    for k in range(count):
        index = pl.program_id(0) * count + k
        fill_turned(turned.at[k], wide, lanes, index, map_side)


def table_call(kernel, blocks, shape, operands, specs):
    count = math.gcd(blocks, 4)
    return pl.pallas_call(
        kernel,
        grid=(blocks // count,),
        in_specs=specs,
        out_specs=pl.BlockSpec((count, *shape), lambda i: (i, 0, 0)),
        out_shape=jax.ShapeDtypeStruct((blocks, *shape), jnp.bfloat16),
    )(*operands)


def window_table(geo, blocks, poses, map_side):
    return table_call(
        functools.partial(windows_kernel, poses, map_side), blocks,
        (poses * WINDOW, BLOCK * BLOCK), geo, [smem()] * 4,
    )


def turned_table(wide_geo, blocks, poses, map_side):
    return table_call(
        functools.partial(turned_kernel, map_side), blocks,
        (BLOCK * BLOCK, poses * WINDOW), wide_geo, [vmem()] * 2,
    )


def add_projection(outs, prod, start, block, poses):
    share = poses // len(outs)
    for first in range(0, poses, 8):
        group = range(first, min(first + 8, poses))
        places = [
            (outs[pose // share], pose % share, pl.ds(start[pose, block], WINDOW))
            for pose in group
        ]
        values = [out[at, rows, :] for out, at, rows in places]
        for pose, value, (out, at, rows) in zip(group, values, places):
            out[at, rows, :] = value + prod[pose * WINDOW : (pose + 1) * WINDOW]


def first_projection_kernel(
    map_side, poses, cosine, sine, start, offset, dens, pool_t, keep, send, fold_ref, w_ref
):
    step = pl.program_id(0)
    geo = (cosine, sine, start, offset)

    @pl.when(step == 0)
    def _():
        keep[...] = jnp.zeros_like(keep)
        send[...] = jnp.zeros_like(send)

    height, depth, _ = dens.shape
    side = pool_t.shape[1]
    folded = jnp.dot(
        dens[...].reshape(height * depth, map_side), pool_t[...], preferred_element_type=jnp.float32
    )
    fold_ref[...] = folded.astype(jnp.bfloat16).reshape(height, depth, side)
    count = height * depth // (BLOCK * BLOCK)
    for k in range(count):
        row, plane = k // (depth // BLOCK) * BLOCK, k % (depth // BLOCK) * BLOCK
        weights = w_ref.at[k]
        fill_windows(weights, geo, step * count + k, poses, map_side)
        pixels = fold_ref[row : row + BLOCK, plane : plane + BLOCK, :].reshape(-1, side)
        prod = jnp.dot(weights[...], pixels, preferred_element_type=jnp.float32)
        add_projection((keep, send), prod, start, step * count + k, poses)


def first_projection(density, pool_t, geo, poses):
    map_side, depth, _ = density.shape
    side = pool_t.shape[1]
    height = 4 * BLOCK
    half = jax.ShapeDtypeStruct((poses // 2, side, side), jnp.float32)
    return pl.pallas_call(
        functools.partial(first_projection_kernel, map_side, poses),
        grid=(map_side // height,),
        in_specs=[smem(), smem(), smem(), smem(),
                  pl.BlockSpec((height, depth, map_side), lambda i: (i, 0, 0)),
                  vmem()],
        out_specs=[vmem(), vmem(), pl.BlockSpec((height, depth, side), lambda i: (i, 0, 0))],
        out_shape=[half, half, jax.ShapeDtypeStruct((map_side, depth, side), jnp.bfloat16)],
        scratch_shapes=[
            pltpu.VMEM(
                (height * depth // BLOCK**2, poses * WINDOW, BLOCK * BLOCK), jnp.bfloat16
            ),
        ],
        name="first_projection",
    )(*geo, density, pool_t)


def pick_kernel(owned, chips, bins_of, poses_of, classes_of, images, *refs):
    outs, order, filled = refs[:-2], refs[-2], refs[-1]
    groups = len(outs)
    each = outs[0].shape[0]
    side = images.shape[1]
    here, slab = lax.axis_index("bin"), lax.axis_index("slab")
    chip, core = slab // 2, lax.rem(slab, 2)
    lane = lax.broadcasted_iota(jnp.int32, (BLOCK, side), 1)

    def ahead(value, size):
        return jnp.where(value < 0, value + size, value)

    for slot in range(groups * each):
        order[slot] = -1
    for group in range(groups):
        filled[group] = 0
    for n in range(images.shape[0]):
        away = ahead(bins_of[n] - here, groups)
        rank = filled[away]
        filled[away] = rank + 1
        order[away * each + rank] = n
    for group in range(groups):
        for k in range(each):
            source = order[group * each + k]
            image = jnp.maximum(source, 0)
            outs[group][k, 0:side, :] = images[image]
            pose = poses_of[image]
            owner = pose // owned
            across = ahead(lax.rem(owner, 2) - core, 2)
            at = (across * chips + ahead(owner // 2 - chip, chips)) * owned + lax.rem(pose, owned)
            at = jnp.where(source >= 0, at, -1).astype(jnp.float32)
            named = classes_of[image].astype(jnp.float32)
            outs[group][k, side : side + BLOCK, :] = jnp.where(
                lane == 0, at, jnp.where(lane == 1, named, 0.0)
            ).astype(images.dtype)


def pick_images(images, image_bin, image_pose, image_class, owned, chips, groups):
    count, side, _ = images.shape
    each = count // 4
    out = jax.ShapeDtypeStruct((each, side + BLOCK, side), images.dtype)
    return pl.pallas_call(
        functools.partial(pick_kernel, owned, chips),
        in_specs=[smem()] * 3 + [vmem()],
        out_specs=[vmem()] * groups,
        out_shape=[out] * groups,
        scratch_shapes=[
            pltpu.SMEM((groups * each,), jnp.int32),
            pltpu.SMEM((groups,), jnp.int32),
        ],
        name="pick_images",
    )(image_bin, image_pose, image_class, images)


def times_hartley(value, table):
    _, side = value.shape
    high = value.astype(jnp.bfloat16)
    low = (value - high.astype(jnp.float32)).astype(jnp.bfloat16)
    both = jnp.dot(high, table, preferred_element_type=jnp.float32)
    rest = jnp.dot(low, table[:, :side], preferred_element_type=jnp.float32)
    return both[:, :side] + (both[:, side:] + rest)


def spectrum_kernel(groups, each, defocus, table, *refs):
    images, (keep, send, ctf, marks, label, sums, sem) = refs[:groups], refs[groups:]
    half = keep.shape[0]
    side = keep.shape[2]
    poses = 2 * half
    for group in range(groups):
        for k in range(each):
            at = group * each + k
            row = images[group][k, side : side + BLOCK, :].astype(jnp.float32)
            marks[at : at + 1, :] = row[0:1].astype(jnp.int32)
    copy = pltpu.make_async_copy(marks, label, sem)
    copy.start()
    sums[...] = jnp.zeros_like(sums)
    fill_ctf(ctf, defocus)
    hart = table[...]
    lane = lax.broadcasted_iota(jnp.int32, (8, side), 1)
    copy.wait()
    for group in range(groups):
        pixels = images[group][:, 0:side, :].reshape(each * side, side)
        both = jnp.dot(pixels, hart, preferred_element_type=jnp.float32)
        along = (both[:, :side] + both[:, side:]).reshape(each, side, side)
        turned = jnp.concatenate([along[k].T for k in range(each)], axis=0)
        full = times_hartley(turned, hart).reshape(each, side, side)
        for k in range(each):
            pose, kind = label[group * each + k, 0], label[group * each + k, 1]
            pose = jnp.where(pose < 0, poses, pose)
            sums[pose, 0:side, :] += ctf[kind] * full[k]
            sums[pose, side : side + 8, :] += jnp.where(lane == kind, 1.0, 0.0)
    for part, out in enumerate((keep, send)):
        for pose in range(half):
            out[pose, 0:side, :] = sums[part * half + pose, 0:side, :].T
            out[pose, side : side + 8, :] = sums[part * half + pose, side : side + 8, :]


def image_sums(images, defocus, table, poses):
    each, _, side = images[0].shape
    slots = each * len(images)
    half = jax.ShapeDtypeStruct((poses // 2, side + 8, side), jnp.float32)
    return pl.pallas_call(
        functools.partial(spectrum_kernel, len(images), each),
        in_specs=[smem(), vmem()] + [vmem()] * len(images),
        out_specs=[vmem()] * 3,
        out_shape=[half, half, jax.ShapeDtypeStruct((*defocus.shape, side, side), jnp.float32)],
        scratch_shapes=[
            pltpu.VMEM((slots, side), jnp.int32),
            pltpu.SMEM((slots, side), jnp.int32),
            pltpu.VMEM((poses + 1, side + 8, side), jnp.float32),
            pltpu.SemaphoreType.DMA(()),
        ],
        name="image_sums",
    )(defocus, table, *images)


def added(parts):
    return functools.reduce(jnp.add, [part[...].astype(jnp.float32) for part in parts])


def through(values, hart, change):
    owned, side, _ = values.shape

    def turn(rows):
        return jnp.concatenate([rows[k * side : (k + 1) * side].T for k in range(owned)], axis=0)

    full = times_hartley(turn(times_hartley(values.reshape(owned * side, side), hart)), hart)
    parts = [change(k, full[k * side : (k + 1) * side]) for k in range(owned)]
    field = times_hartley(turn(times_hartley(jnp.concatenate(parts, axis=0), hart)), hart)
    return field.reshape(owned, side, side)


def first_filter_kernel(weight, count, ctf, table, *refs):
    proj, totals, (field, residual, gains) = refs[:count], refs[count:-3], refs[-3:]
    _, side, _ = field.shape
    total = added(totals)

    def change(k, value):
        gain = jnp.zeros((side, side), jnp.float32)
        for c in range(ctf.shape[0]):
            gain = gain + total[k, side : side + 1, c : c + 1] * (ctf[c] * ctf[c])
        value = weight * (gain * value - total[k, 0:side, :])
        gains[k] = weight * gain
        residual[k] = value
        return value

    field[...] = through(added(proj), table[...], change).astype(field.dtype)


def first_field(proj, totals, ctf, table, weight, owned):
    side = table.shape[0]
    block = pl.BlockSpec((owned, side, side), lambda i: (0, 0, 0))
    tall = pl.BlockSpec((owned, side + 8, side), lambda i: (0, 0, 0))
    kept = jax.ShapeDtypeStruct((owned, side, side), jnp.float32)
    return pl.pallas_call(
        functools.partial(first_filter_kernel, weight, len(proj)),
        grid=(1,),
        in_specs=[vmem(), vmem()] + [block] * len(proj) + [tall] * len(totals),
        out_specs=[block] * 3,
        out_shape=[jax.ShapeDtypeStruct(kept.shape, jnp.bfloat16), kept, kept],
        name="first_field",
    )(ctf, table, *proj, *totals)


def next_filter_kernel(table, residual, gains, *refs):
    parts, field = refs[:-1], refs[-1]

    def change(k, value):
        return gains[k] * value + residual[k]

    field[...] = through(added(parts), table[...], change).astype(field.dtype)


def next_field(parts, residual, gains, table):
    block = pl.BlockSpec(residual.shape, lambda i: (0, 0, 0))
    return pl.pallas_call(
        next_filter_kernel,
        grid=(1,),
        in_specs=[vmem()] + [block] * (2 + len(parts)),
        out_specs=block,
        out_shape=jax.ShapeDtypeStruct(residual.shape, jnp.bfloat16),
        name="next_field",
    )(table, residual, gains, *parts)


def load_fields(field, fields):
    at = 0
    for part in fields:
        count = part.shape[0]
        field[at : at + count] = part[...].astype(jnp.float32)
        at += count


def gather_windows(f_ref, field, start, block, poses):
    for pose in range(poses):
        f_ref[pose * WINDOW : (pose + 1) * WINDOW, :] = field[
            pose, pl.ds(start[pose, block], WINDOW), :
        ].astype(jnp.bfloat16)


def step_gradient(split_ref, f_ref, field, turned, pool2, start, first_block, poses):
    height, depth, width = split_ref.shape
    for k in range(depth // BLOCK):
        planes = slice(k * BLOCK, (k + 1) * BLOCK)
        gather_windows(f_ref.at[k], field, start, first_block + k, poses)
        back = jnp.dot(turned[k], f_ref[k], preferred_element_type=jnp.float32)
        high = back.astype(jnp.bfloat16)
        low = (back - high.astype(jnp.float32)).astype(jnp.bfloat16)
        split_ref[:, planes, :] = jnp.concatenate([high, low], axis=1).reshape(
            height, BLOCK, width
        )
    return jnp.dot(
        split_ref[...].reshape(height * depth, width),
        pool2[...],
        preferred_element_type=jnp.float32,
    )


def step_kernel(
    map_side, poses, parts, bin_ref, start, sizes, dens, fold, windows, turned, pool2, pool_t, *refs
):
    fields = refs[:parts]
    first, keep, sent, field, f_ref, split_ref, send = refs[parts:]
    step = pl.program_id(0)

    @pl.when(step == 0)
    def _():
        keep[...] = jnp.zeros_like(keep)
        send[...] = jnp.zeros_like(send)
        load_fields(field, fields)

    height, depth, side = fold.shape
    count = depth // BLOCK
    grad = step_gradient(split_ref, f_ref, field, turned, pool2, start, step * count, poses)
    kept = dens[...].reshape(height * depth, map_side).astype(jnp.float32)
    moved = kept - sizes[0] * grad
    first[...] = moved.reshape(height, depth, map_side)
    folded = jnp.dot(moved.astype(jnp.bfloat16), pool_t[...], preferred_element_type=jnp.float32)
    before = fold[...].reshape(height * depth, side).astype(jnp.float32)
    change = folded.astype(jnp.bfloat16).astype(jnp.float32) - before
    high = change.astype(jnp.bfloat16)
    low = (change - high.astype(jnp.float32)).astype(jnp.bfloat16)
    split_ref[...] = jnp.concatenate([high, low], axis=1).reshape(height, depth, 2 * side)
    for k in range(count):
        pixels = split_ref[:, k * BLOCK : (k + 1) * BLOCK, :].reshape(BLOCK * BLOCK, 2 * side)
        prod = jnp.dot(windows[k], pixels, preferred_element_type=jnp.float32)
        prod = prod[:, :side] + prod[:, side:]
        add_projection((keep, send), prod, start, step * count + k, poses)

    @pl.when(step == pl.num_programs(0) - 1)
    def _():
        sent[...] = send[...].astype(sent.dtype)


def take_step(density, fold, fields, start, tables, sizes, bin_index, pool2, pool_t, row_share):
    map_side, depth, _ = density.shape
    side = pool_t.shape[1]
    poses = start.shape[0]
    half = jax.ShapeDtypeStruct((poses // 2, side, side), jnp.float32)
    row_blocks, count = row_share // BLOCK, depth // BLOCK

    def own(width):
        return pl.BlockSpec((BLOCK, depth, width), lambda i, at: (at[0] * row_blocks + i, 0, 0))

    return pl.pallas_call(
        functools.partial(step_kernel, map_side, poses, len(fields)),
        grid_spec=pltpu.PrefetchScalarGridSpec(
            num_scalar_prefetch=1,
            grid=(row_blocks,),
            in_specs=[smem()] * 2
            + [own(map_side), own(side)]
            + [pl.BlockSpec((count, *table.shape[1:]), lambda i, at: (i, 0, 0)) for table in tables]
            + [vmem()] * (2 + len(fields)),
            out_specs=[
                pl.BlockSpec((BLOCK, depth, map_side), lambda i, at: (i, 0, 0)), vmem(), vmem()
            ],
            scratch_shapes=[
                pltpu.VMEM((poses, side, side), jnp.float32),
                pltpu.VMEM((count, poses * WINDOW, side), jnp.bfloat16),
                pltpu.VMEM((BLOCK, depth, 2 * side), jnp.bfloat16),
                pltpu.VMEM(half.shape, jnp.float32),
            ],
        ),
        out_shape=[
            jax.ShapeDtypeStruct((row_share, depth, map_side), jnp.float32),
            half,
            jax.ShapeDtypeStruct(half.shape, jnp.bfloat16),
        ],
        name="take_step",
    )(bin_index.reshape(1), start, sizes, density, fold, *tables, pool2, pool_t, *fields)


def finish_kernel(poses, parts, start, sizes, first, turned, pool2, *refs):
    fields = refs[:parts]
    gradient, refined, field, f_ref, split_ref = refs[parts:]
    step = pl.program_id(0)

    @pl.when(step == 0)
    def _():
        load_fields(field, fields)

    count = first.shape[1] // BLOCK
    grad = step_gradient(split_ref, f_ref, field, turned, pool2, start, step * count, poses)
    grad = grad.reshape(first.shape)
    gradient[...] = grad
    refined[...] = first[...] - sizes[1] * grad


def finish(first, fields, start, turned, sizes, pool2):
    row_share, depth, map_side = first.shape
    side = pool2.shape[0] // 2
    poses = start.shape[0]
    count = depth // BLOCK
    rows = pl.BlockSpec((BLOCK, depth, map_side), lambda i: (i, 0, 0))
    out = jax.ShapeDtypeStruct(first.shape, jnp.float32)
    return pl.pallas_call(
        functools.partial(finish_kernel, poses, len(fields)),
        grid=(row_share // BLOCK,),
        in_specs=[smem()] * 2
        + [rows, pl.BlockSpec((count, *turned.shape[1:]), lambda i: (i, 0, 0))]
        + [vmem()] * (1 + len(fields)),
        out_specs=[rows, rows],
        out_shape=[out, out],
        scratch_shapes=[
            pltpu.VMEM((poses, side, side), jnp.float32),
            pltpu.VMEM((count, poses * WINDOW, side), jnp.bfloat16),
            pltpu.VMEM((BLOCK, depth, 2 * side), jnp.bfloat16),
        ],
        name="finish",
    )(start, sizes, first, turned, pool2, *fields)


def on_device(
    density, images, image_bin, image_pose, image_class, defocus, pose_offset, step_sizes
):
    bins = lax.axis_size("bin")
    slabs = lax.axis_size("slab")
    chips = slabs // 2
    bin_index = lax.axis_index("bin")
    map_side, depth, _ = density.shape
    image_count, side, _ = images.shape
    pose_count = pose_offset.shape[1]
    row_share = map_side // bins
    owned = pose_count // slabs
    weight = 16.0 * pose_count / (image_count * slabs)

    def to_core(value):
        return lax.ppermute(value, "slab", [(s, s ^ 1) for s in range(slabs)])

    def to_chip(value, shift):
        return lax.ppermute(
            value, "slab", [(s, (s + 2 * shift) % slabs) for s in range(slabs)]
        )

    def to_bin(value, shift):
        return lax.ppermute(value, "bin", [(b, (b + shift) % bins) for b in range(bins)])

    picked = pick_images(images, image_bin[:, 0], image_pose, image_class, owned, chips, bins)
    poses = bins * pose_count
    own_geo, geo, wide_geo = make_geometry(
        pose_offset, map_side, side, depth, row_share, chips, owned
    )
    pooling = pool_table(side, map_side).astype(jnp.bfloat16)
    pool_t = jnp.asarray(pooling.T)
    pool2 = jnp.asarray(np.concatenate([pooling, pooling], axis=0))
    table = hartley_table(side)

    picked, own_geo = lax.optimization_barrier((picked, own_geo))
    got_images = [picked[0]]
    for d in range(1, bins):
        got_images.append(to_bin(picked[d], d))

    def reduce_slab(keep, send, sent_as=jnp.float32):
        got = to_core(send)
        each = keep.shape[0] // chips

        def joined(d):
            rows = slice(d * each, (d + 1) * each)
            return (keep[rows] + got[rows].astype(jnp.float32)).astype(sent_as)

        return [keep, got] + [to_chip(joined(d), d) for d in range(1, chips)]

    keep, send, fold = first_projection(density, pool_t, own_geo, pose_count)
    keep, send, defocus = lax.optimization_barrier((keep, send, defocus))
    proj_parts = reduce_slab(keep, send)
    keep, send, ctf = image_sums(got_images, defocus, table, pose_count)
    total_parts = reduce_slab(keep, send)

    def share_field(field, early=(), late=()):
        near = [field] + [to_bin(field, bins - d) for d in range(1, bins)]
        near, early = lax.optimization_barrier((near, early))
        near = jnp.concatenate(near, axis=0)
        across = [to_chip(near, chips - d) for d in range(1, chips)]
        across, late = lax.optimization_barrier((across, late))
        row = [near] + across
        return row + [to_core(part) for part in row], early, late

    field, residual, gains = first_field(proj_parts, total_parts, ctf, table, weight, owned)
    field, geo, wide_geo = lax.optimization_barrier((field, geo, wide_geo))
    blocks = row_share // BLOCK * (depth // BLOCK)
    fields, turned, windows = share_field(
        field,
        turned_table(wide_geo, blocks, poses, map_side),
        window_table(geo, blocks, poses, map_side),
    )
    start = geo[2]
    first, keep, send = take_step(
        density, fold, fields, start, (windows, turned), step_sizes, bin_index, pool2, pool_t,
        row_share,
    )
    got = to_core(send)
    whole = bins * owned

    def joined(chip_on, low, high):
        rows = slice(chip_on * whole + low * owned, chip_on * whole + high * owned)
        return keep[rows] + got[rows].astype(jnp.float32)

    def cross(low, high):
        return [to_chip(joined(d, low, high).astype(jnp.bfloat16), d) for d in range(1, chips)]

    def block_of(d, low, across):
        rows = slice((d - low) * owned, (d - low + 1) * owned)
        value = functools.reduce(
            jnp.add, [part[rows].astype(jnp.float32) for part in across], joined(0, d, d + 1)
        )
        return value.astype(jnp.bfloat16)

    half = bins // 2
    far = cross(half, bins)
    near = cross(0, half)
    leaving = [block_of(d, half, far) for d in range(half, bins)]
    moved = [to_bin(value, half + k) for k, value in enumerate(leaving)]
    near, _ = lax.optimization_barrier((near, leaving))
    moved += [to_bin(block_of(d, 0, near), d) for d in range(1, half)]
    parts = [keep, got] + near
    field = next_field(parts + moved, residual, gains, table)
    gradient, refined = finish(first, share_field(field)[0], start, turned, step_sizes, pool2)
    return (gradient, refined)


def solution(mesh):
    return jax.shard_map(
        on_device,
        mesh=mesh,
        in_specs=(
            P("grp", "slab", None),
            P(("grp", "bin", "slab"), None, None),
            P(("grp", "bin", "slab"), None),
            P(("grp", "bin", "slab")),
            P(("grp", "bin", "slab")),
            P("grp"),
            P("grp", None),
            P(),
        ),
        out_specs=(P(("grp", "bin"), "slab", None), P(("grp", "bin"), "slab", None)),
        check_vma=False,
    )
```
